256 devices in a mesh: lon: 4 (over y_hi, core), lat: 64 (over y_lo, x, z).
Axes of the slice: x: 4, y: 4 (y_hi: 2, y_lo: 2; y = y_hi * 2 + y_lo), z: 8, core: 2. Of those that a mesh axis runs over, the one named last changes fastest.
Arguments:
- increment: float32 [2, 512, 32, 2048], P(None, 'lat', None, 'lon'), may hold values from -6 to 6
- spread: float32 [2, 512, 32], P(None, 'lat'), may hold values from 0.5 to 2
- lon_scale: float32 [2, 512], P(None, 'lat'), may hold values from 4 to 2048
- lat_scale: float32 [2, 32], replicated, may hold values from 2 to 256
- vertical: float32 [2, 32, 32], replicated, may hold values from -1 to 1
Outputs:
- covariance: float32 [2, 512, 32, 2048], P(None, 'lat', None, 'lon')
The draws below stay inside these ranges and needn't reach their ends.
All inputs are finite; a program needn't handle non-finite values.
Results may differ from the reference program's by a relative error of at most 0.0003.
Values sent between devices are 32-bit elements; how exact they have to be, the bound alone decides.
A program may use at most 128 MiB of HBM per device.

```python
import math
import jax
import jax.numpy as jnp
from jax import lax

V = 2
LEV = 32
NLON = 2048
NLAT = 512


def steps_of(stream_key, shape, shards, smallest, top_value):
    def one(dim, blocks):
        heights = jax.random.uniform(jax.random.fold_in(jax.random.fold_in(stream_key, 6), dim), (blocks,), jnp.float32, smallest / len(shards), top_value / len(shards))
        return jnp.repeat(jnp.exp(heights), shape[dim] // blocks).reshape((-1,) + (1,) * (len(shape) - dim - 1))

    factor_of = one(*shards[0])
    for cut in shards[1:]:
        factor_of = factor_of * one(*cut)
    return factor_of


def gaussian(key, shape, scale, limit, split=(), kind=jnp.bfloat16):
    values = scale * jax.random.normal(key, shape, jnp.float32)
    if split:
        values = values * steps_of(key, shape, split, -0.22, 0.18)
    return jnp.clip(values, -limit, limit).astype(kind)


def setup_inputs(seed: int = 0) -> dict:
    splits = jax.random.split(jax.random.key(seed), 6)
    increment = gaussian(splits[0], (V, NLAT, LEV, NLON), 1.0, 6.0, ((1, 64), (3, 4)), jnp.float32)
    spread = jnp.clip(jnp.exp(math.log(2.0) - 1.3862944 * jax.random.uniform(splits[1], (V, NLAT, LEV), jnp.float32) ** steps_of(splits[1], (V, NLAT, LEV), ((1, 64),), -0.2, 0.2)), 0.5, 2.0)
    lon_scale = jnp.clip(jnp.exp(math.log(2048.0) - 6.2383246 * jax.random.uniform(splits[2], (V, NLAT), jnp.float32) ** steps_of(splits[2], (V, NLAT), ((1, 64),), -0.2, 0.2)), 4.0, 2048.0)
    lat_scale = jnp.clip(jnp.exp(jax.random.uniform(splits[3], (V, LEV), jnp.float32, math.log(2.0), math.log(256.0))), 2.0, 256.0)
    vertical = gaussian(splits[4], (V, LEV, LEV), LEV ** -0.5, 1.0, (), jnp.float32)
    return dict(increment=increment, spread=spread, lon_scale=lon_scale, lat_scale=lat_scale, vertical=vertical)


highest = lax.Precision.HIGHEST

def norm_factor(poles):
    return jnp.sqrt(2.0 * jnp.sqrt(jnp.pi) * jnp.sqrt(8.0 * poles) / (1.0 - poles))

def cascade(series, poles, initial, reverse):
    gains = 1.0 - poles

    def advance(carried, element):
        section_one = poles * carried[0] + gains * element
        section_two = poles * carried[1] + gains * section_one
        section_three = poles * carried[2] + gains * section_two
        section_four = poles * carried[3] + gains * section_three
        return (jnp.stack([section_one, section_two, section_three, section_four]), section_four)
    finished, outputs = lax.scan(advance, initial, series, reverse=reverse)
    return (outputs, finished)

def periodic(series, poles, reverse):
    latitudes = series.shape[1]
    initial = jnp.zeros((4,) + series.shape[1:], jnp.float32)
    unforced, offsets = cascade(series, poles, initial, reverse)
    unit_state = jnp.broadcast_to(jnp.eye(4, dtype=jnp.float32)[:, None, :], (4, latitudes, 4))
    silent = jnp.zeros((series.shape[0], latitudes, 4), jnp.float32)
    ignored, matrix = cascade(silent, poles, unit_state, reverse)
    solved = []
    for k in range(4):
        running = offsets[k]
        for j in range(k):
            running = running + matrix[k, :, j][:, None] * solved[j]
        solved.append(running / (1.0 - matrix[k, :, k])[:, None])
    outputs, finished = cascade(series, poles, jnp.stack(solved), reverse)
    return outputs

def reference(increment, spread, lon_scale, lat_scale, vertical):
    returned = []
    for variable in range(increment.shape[0]):
        lon_pole = jnp.exp(-1.0 / lon_scale[variable])[:, None]
        lat_pole = jnp.exp(-1.0 / lat_scale[variable])[:, None]
        scaled = spread[variable][:, :, None] * increment[variable]
        series = jnp.moveaxis(scaled, 2, 0)
        series = periodic(series, lon_pole, False)
        series = periodic(series, lon_pole, True)
        zonal_part = jnp.moveaxis(series, 0, 2) * norm_factor(lon_pole)[:, :, None]
        initial = jnp.zeros((4,) + zonal_part.shape[1:], jnp.float32)
        forward, finished = cascade(zonal_part, lat_pole, initial, False)
        backward, finished = cascade(forward, lat_pole, initial, True)
        meridional = backward * norm_factor(lat_pole)[None]
        blended = jnp.einsum('lm,amn->aln', vertical[variable], meridional, precision=highest)
        returned.append(spread[variable][:, :, None] * blended)
    return jnp.stack(returned)
```

```python
import functools
import math

import jax
import jax.numpy as jnp
from jax import lax
from jax.experimental import pallas as pl
from jax.experimental.pallas import tpu as pltpu
from jax.sharding import PartitionSpec as P

MESH = pl.DeviceIdType.MESH
BLK = 128
F32 = jnp.float32
BF16 = jnp.bfloat16


def split(a):
    high = a.astype(BF16)
    return high, (a - high.astype(F32)).astype(BF16)


def dot3(a, b, dims):
    ah, al = a
    bh, bl = b

    def one(p, q):
        return lax.dot_general(p, q, (dims, ((), ())), preferred_element_type=F32)

    return one(ah, bh) + (one(ah, bl) + one(al, bh))


def pole_terms(scale):
    x = 1.0 / scale
    t = jnp.ones_like(x)
    for k in range(10, 1, -1):
        t = 1.0 - x * (1.0 / k) * t
    pole = 1.0 - x * t
    gain = 1.0 - pole
    s = gain / (2.0 - gain)
    s2 = s * s
    series = 1.0 / 3 + s2 * (1.0 / 5 + s2 * (1.0 / 7 + s2 * (1.0 / 9 + s2 * (1.0 / 11))))
    log_pole = -2.0 * s * (1.0 + s2 * series)
    norm = jnp.sqrt((2.0 * math.sqrt(math.pi)) * jnp.sqrt(8.0 * pole) / gain)
    return gain, pole, log_pole, norm


def circle_terms(scale, laps):
    gain, pole, log_pole, norm = pole_terms(scale)
    q = pole * pole
    r = 1.0 / (1.0 + pole)
    r2 = r * r
    r4 = r2 * r2
    p3 = r4
    p2 = (3.0 + q) * r4 * r
    p1 = (3.0 + 6.0 * q + q * q) * r4 * r2
    p0 = (1.0 + 9.0 * q + 9.0 * q * q + q * q * q) * r4 * r2 * r
    u = gain * BLK
    c0 = gain * p0
    c1 = gain * u * (p1 - 0.5 * p2 * gain + p3 * gain * gain * (1.0 / 3))
    c2 = gain * u * u * (0.5 * p2 - 0.5 * p3 * gain)
    c3 = gain * u * u * u * p3 * (1.0 / 6)
    lam = BLK * log_pole
    beta = jnp.exp(laps * lam)
    b0 = 1.0 / (1.0 - beta)
    b1 = beta * b0 * b0
    b2 = b1 * b0 * (1.0 + beta)
    b3 = b1 * b0 * b0 * (1.0 + beta * (4.0 + beta))
    n = float(laps)
    e3 = c3 * b0
    e2 = c2 * b0 + 3.0 * n * c3 * b1
    e1 = c1 * b0 + 2.0 * n * c2 * b1 + 3.0 * n * n * c3 * b2
    e0 = c0 * b0 + n * c1 * b1 + n * n * c2 * b2 + n * n * n * c3 * b3
    return [lam, e0 * norm, e1 * norm, e2 * norm, e3 * norm]


def kernel(
    n_lon, n_lat,
    lon_scale, lat_scale, inc_ref, spread_ref, vert_ref, out_ref,
    coef, column, inside, local_mom, mom_send, mom_recv, zon, rx, tx, back, fwd_mat, bwd_mat, mat_hi, mat_lo,
    ms_sem, mr_sem, s1_sem, r1_sem, s2_sem, r2_sem,
):
    nv, rows, lev, width = inc_ref.shape
    blocks = width // BLK
    laps = blocks * n_lon
    poles = nv * rows
    nlat = rows * n_lat
    group = min(4, rows)
    me_lon = lax.axis_index("lon")
    me = lax.axis_index("lat")
    my_v = lax.rem(me, nv)
    my_lev = me // nv

    barrier = pltpu.get_barrier_semaphore()

    @pl.loop(1, n_lat)
    def _(k):
        pl.semaphore_signal(barrier, inc=1, device_id={"lat": lax.rem(me + k, n_lat)}, device_id_type=MESH)

    for s in range(1, n_lon):
        pl.semaphore_signal(
            barrier, inc=1, device_id={"lon": lax.rem(me_lon + s, n_lon)}, device_id_type=MESH
        )

    row_of = lax.broadcasted_iota(jnp.int32, (poles, BLK), 0)
    scale = jnp.zeros((poles, BLK), F32)
    for v in range(nv):
        for t in range(rows):
            scale = jnp.where(row_of == v * rows + t, lon_scale[v, t], scale)
    for k, part in enumerate(circle_terms(scale, laps)):
        coef[k] = part
    eye = lax.broadcasted_iota(jnp.int32, (lev, lev), 0) == lax.broadcasted_iota(jnp.int32, (lev, lev), 1)
    for v in range(nv):
        for t in range(rows):
            line = jnp.broadcast_to(spread_ref[v, t : t + 1, :], (lev, lev))
            one = jnp.sum(jnp.where(eye, line, 0.0), axis=1, keepdims=True)
            column[v, t] = jnp.broadcast_to(one, (lev, BLK))

    def tile(shape, dim):
        return lax.broadcasted_iota(jnp.int32, shape, dim)

    lane8 = tile((8, BLK), 1).astype(F32) * (1.0 / BLK)
    order = tile((8, BLK), 0)
    ahead = order < 4
    rank = lax.rem(order, 4)
    to_end = 1.0 - lane8
    to_start = lane8 + 1.0 / BLK
    behind = lane8
    before = (BLK - 1.0) / BLK - lane8

    def power(tau):
        t2 = tau * tau
        return jnp.where(rank == 0, 1.0, jnp.where(rank == 1, tau, jnp.where(rank == 2, t2, t2 * tau)))

    def coefs(r):
        return [coef[k, pl.ds(r, 1), :] for k in range(5)]

    def wide_column(v, t):
        one = column[v, t]
        return jnp.concatenate([one] * blocks, axis=1)

    def first(v, g):
        pieces = []
        for u in range(group):
            t = g * group + u
            lam, e0, e1, e2, e3 = coefs(v * rows + t)
            x = inc_ref[v, t] * wide_column(v, t)
            stacked = jnp.concatenate([x[:, c * BLK : (c + 1) * BLK] for c in range(blocks)], axis=0)
            gap = jnp.abs(tile((BLK, BLK), 0) - tile((BLK, BLK), 1)).astype(F32) * (1.0 / BLK)
            far = float(laps) - gap
            near = jnp.exp(lam * gap) * (e0 + gap * (e1 + gap * (e2 + gap * e3)))
            around = jnp.exp(lam * far) * (e0 + far * (e1 + far * (e2 + far * e3)))
            inside[v, t] = dot3(split(stacked), split(near + around), ((1,), (0,)))
            tau = jnp.where(ahead, to_end, to_start)
            small = jnp.exp(lam * tau) * power(tau)
            nothing = jnp.zeros((8, BLK), F32)
            lines = []
            for c in range(blocks):
                lines.append(jnp.concatenate([small if d == c else nothing for d in range(blocks)], axis=1))
            whole = []
            for c in range(blocks):
                shifted = jnp.where(ahead, to_end + float(blocks - 1 - c), to_start + float(c))
                whole.append(jnp.exp(lam * shifted) * power(shifted))
            lines.append(jnp.concatenate(whole, axis=1))
            basis = jnp.concatenate(lines, axis=0)
            moments = dot3(split(basis), split(x), ((1,), (1,)))
            local_mom[v, t] = moments[: 8 * blocks]
            pieces.append(moments[8 * blocks :])
        mom_send[v, g] = jnp.concatenate(pieces, axis=1)

    def moment_copy(v, s):
        return pltpu.make_async_remote_copy(
            src_ref=mom_send.at[v],
            dst_ref=mom_recv.at[v, s - 1],
            send_sem=ms_sem.at[v, s - 1],
            recv_sem=mr_sem.at[v, s - 1],
            device_id={"lon": lax.rem(me_lon + s, n_lon)},
            device_id_type=MESH,
        )

    for v in range(nv):

        @pl.loop(0, rows // group)
        def _(g):
            first(v, g)

        if v == 0:
            pl.semaphore_wait(barrier, n_lat - 1 + n_lon - 1)
        for s in range(1, n_lon):
            moment_copy(v, s).start()

    def second(v, g):
        for u in range(group):
            t = g * group + u
            lam, e0, e1, e2, e3 = coefs(v * rows + t)

            def mixed(a0, a1, a2, a3):
                return jnp.where(rank == 0, a0, jnp.where(rank == 1, a1, jnp.where(rank == 2, a2, a3)))

            q0 = mixed(e0, e1, e2, e3)
            q1 = mixed(e1, 2.0 * e2, 3.0 * e3, 0.0)
            q2 = mixed(e2, 3.0 * e3, 0.0, 0.0)
            q3 = mixed(e3, 0.0, 0.0, 0.0)

            def reach(y):
                return jnp.exp(lam * y) * (q0 + y * (q1 + y * (q2 + y * q3)))

            by_gap = {}
            for gap in list(range(1, blocks)) + list(range(laps - blocks + 1, laps)):
                by_gap[gap] = reach(jnp.where(ahead, behind + float(gap - 1), before + float(laps - gap - 1)))
            nothing = jnp.zeros((8, BLK), F32)
            lines = []
            for c in range(blocks):
                lines.append(
                    jnp.concatenate(
                        [nothing if d == c else by_gap[(d - c) % laps] for d in range(blocks)], axis=1
                    )
                )
            sources = [local_mom[v, t]]
            for s in range(1, n_lon):
                line = []
                for d in range(blocks):
                    line.append(
                        reach(
                            jnp.where(
                                ahead,
                                behind + float(d + blocks * (s - 1)),
                                before + float(blocks - 1 - d + blocks * (n_lon - 1 - s)),
                            )
                        )
                    )
                lines.append(jnp.concatenate(line, axis=1))
                sources.append(mom_recv[v, s - 1, g][:, u * lev : (u + 1) * lev])
            table = jnp.concatenate(lines, axis=0)
            moments = jnp.concatenate(sources, axis=0)
            added = dot3(split(moments.T), split(table), ((1,), (0,)))
            own = inside[v, t]
            own = jnp.concatenate([own[c * lev : (c + 1) * lev] for c in range(blocks)], axis=1)
            total = own + added
            for c in range(blocks):
                zon[v, c, pl.ds(t, lev, stride=rows), :] = total[:, c * BLK : (c + 1) * BLK]

    def out_copy(d, v, level):
        return pltpu.make_async_remote_copy(
            src_ref=zon.at[v, :, pl.ds(level * rows, rows), :],
            dst_ref=rx.at[:, pl.ds(me * rows, rows), :],
            send_sem=s1_sem,
            recv_sem=r1_sem,
            device_id={"lat": d},
            device_id_type=MESH,
        )

    for v in range(nv):
        for s in range(1, n_lon):
            moment_copy(v, s).wait()

        @pl.loop(0, rows // group)
        def _(g):
            second(v, g)

        @pl.loop(0, lev)
        def _(k):
            level = lax.rem(my_lev + k, lev)
            d = level * nv + v

            @pl.when(d != me)
            def _():
                out_copy(d, v, level).start()

    mine = jnp.full((8, BLK), lat_scale[my_v, my_lev], F32)
    gain, pole, log_pole, norm = [part[:1] for part in pole_terms(mine)]
    g2 = gain * gain
    lead = g2 * g2 * (1.0 / 6)
    size = min(BLK, nlat)

    @pl.loop(0, nlat // size)
    def _(i):
        for j in range(nlat // size):
            away = (i - j) * size + tile((size, size), 0) - tile((size, size), 1)
            n = jnp.abs(away).astype(F32)
            value = lead[:, :size] * (n + 1.0) * (n + 2.0) * (n + 3.0) * jnp.exp(log_pole[:, :size] * n)
            fwd_mat[pl.ds(i * size, size), j * size : (j + 1) * size] = jnp.where(away >= 0, value, 0.0)
            bwd_mat[pl.ds(i * size, size), j * size : (j + 1) * size] = jnp.where(
                away <= 0, norm[:, :size] * value, 0.0
            )

    @pl.loop(0, nlat // size)
    def _(i):
        at = pl.ds(i * size, size)
        both = dot3(split(bwd_mat[at, :]), split(fwd_mat[...]), ((1,), (0,)))
        mat_hi[at, :], mat_lo[at, :] = split(both)

    rx[:, pl.ds(me * rows, rows), :] = zon[my_v, :, pl.ds(my_lev * rows, rows), :]
    some = pl.ds(0, (n_lat - 1) * rows)
    pltpu.make_async_copy(rx.at[:, some, :], rx.at[:, some, :], r1_sem).wait()

    def back_copy(d):
        return pltpu.make_async_remote_copy(
            src_ref=tx.at[:, pl.ds(d * rows, rows), :],
            dst_ref=back.at[:, pl.ds((my_v * lev + my_lev) * rows, rows), :],
            send_sem=s2_sem,
            recv_sem=r2_sem,
            device_id={"lat": d},
            device_id_type=MESH,
        )

    per = size // rows

    @pl.loop(0, nlat // size)
    def _(i):
        at = pl.ds(i * size, size)
        everything = jnp.concatenate([rx[c] for c in range(blocks)], axis=1)
        result = dot3((mat_hi[at, :], mat_lo[at, :]), split(everything), ((1,), (0,)))
        for c in range(blocks):
            tx[c, at, :] = result[:, c * BLK : (c + 1) * BLK]

        @pl.loop(0, per)
        def _(k):
            d = i * per + k

            @pl.when(d != me)
            def _():
                back_copy(d).start()

    back[:, pl.ds((my_v * lev + my_lev) * rows, rows), :] = tx[:, pl.ds(me * rows, rows), :]
    pltpu.make_async_copy(back.at[:, some, :], back.at[:, some, :], r2_sem).wait()

    for v in range(nv):
        weights = split(vert_ref[v])

        @pl.loop(0, rows)
        def _(t):
            levels = jnp.concatenate(
                [back[c, pl.ds(v * lev * rows + t, lev, stride=rows), :] for c in range(blocks)], axis=1
            )
            out_ref[v, t] = dot3(weights, split(levels), ((1,), (0,))) * wide_column(v, t)

    pltpu.make_async_copy(tx.at[:, some, :], tx.at[:, some, :], s1_sem).wait()
    pltpu.make_async_copy(tx.at[:, some, :], tx.at[:, some, :], s2_sem).wait()


def per_device(n_lon, n_lat, increment, spread, lon_scale, lat_scale, vertical):
    nv, rows, lev, width = increment.shape
    blocks = width // BLK
    poles = nv * rows
    nlat = rows * n_lat
    group = min(4, rows)
    vmem = pl.BlockSpec(memory_space=pltpu.VMEM)
    smem = pl.BlockSpec(memory_space=pltpu.SMEM)
    return pl.pallas_call(
        functools.partial(kernel, n_lon, n_lat),
        out_shape=jax.ShapeDtypeStruct(increment.shape, F32),
        in_specs=[smem, smem, vmem, vmem, vmem],
        out_specs=vmem,
        scratch_shapes=[
            pltpu.VMEM((5, poles, BLK), F32),
            pltpu.VMEM((nv, rows, lev, BLK), F32),
            pltpu.VMEM((nv, rows, blocks * lev, BLK), F32),
            pltpu.VMEM((nv, rows, 8 * blocks, lev), F32),
            pltpu.VMEM((nv, rows // group, 8, group * lev), F32),
            pltpu.VMEM((nv, n_lon - 1, rows // group, 8, group * lev), F32),
            pltpu.VMEM((nv, blocks, lev * rows, BLK), F32),
            pltpu.VMEM((blocks, nlat, BLK), F32),
            pltpu.VMEM((blocks, nlat, BLK), F32),
            pltpu.VMEM((blocks, nv * lev * rows, BLK), F32),
            pltpu.VMEM((nlat, nlat), F32),
            pltpu.VMEM((nlat, nlat), F32),
            pltpu.VMEM((nlat, nlat), BF16),
            pltpu.VMEM((nlat, nlat), BF16),
            pltpu.SemaphoreType.DMA((nv, n_lon - 1)),
            pltpu.SemaphoreType.DMA((nv, n_lon - 1)),
            pltpu.SemaphoreType.DMA,
            pltpu.SemaphoreType.DMA,
            pltpu.SemaphoreType.DMA,
            pltpu.SemaphoreType.DMA,
        ],
        compiler_params=pltpu.CompilerParams(
            collective_id=0, has_side_effects=True, vmem_limit_bytes=48 * 1024 * 1024
        ),
    )(lon_scale, lat_scale, increment, spread, vertical)


def solution(mesh):
    in_specs = (P(None, "lat", None, "lon"), P(None, "lat", None), P(None, "lat"), P(), P())
    out_specs = P(None, "lat", None, "lon")
    body = functools.partial(per_device, mesh.shape["lon"], mesh.shape["lat"])
    return jax.shard_map(body, mesh=mesh, in_specs=in_specs, out_specs=out_specs, check_vma=False)
```

```python
import functools
import math

import jax
import jax.numpy as jnp
from jax import lax
from jax.experimental import pallas as pl
from jax.experimental.pallas import tpu as pltpu
from jax.sharding import PartitionSpec as P

MESH = pl.DeviceIdType.MESH
BLK = 128
F32 = jnp.float32
BF16 = jnp.bfloat16


def split(a):
    high = a.astype(BF16)
    return high, (a - high.astype(F32)).astype(BF16)


def dot3(a, b, dims):
    ah, al = a
    bh, bl = b

    def one(p, q):
        return lax.dot_general(p, q, (dims, ((), ())), preferred_element_type=F32)

    return one(ah, bh) + (one(ah, bl) + one(al, bh))


def pole_terms(scale):
    x = 1.0 / scale
    t = jnp.ones_like(x)
    for k in range(10, 1, -1):
        t = 1.0 - x * (1.0 / k) * t
    pole = 1.0 - x * t
    gain = 1.0 - pole
    s = gain / (2.0 - gain)
    s2 = s * s
    series = 1.0 / 3 + s2 * (1.0 / 5 + s2 * (1.0 / 7 + s2 * (1.0 / 9 + s2 * (1.0 / 11))))
    log_pole = -2.0 * s * (1.0 + s2 * series)
    norm = jnp.sqrt((2.0 * math.sqrt(math.pi)) * jnp.sqrt(8.0 * pole) / gain)
    return gain, pole, log_pole, norm


def circle_terms(scale, laps):
    gain, pole, log_pole, norm = pole_terms(scale)
    q = pole * pole
    r = 1.0 / (1.0 + pole)
    r2 = r * r
    r4 = r2 * r2
    p3 = r4
    p2 = (3.0 + q) * r4 * r
    p1 = (3.0 + 6.0 * q + q * q) * r4 * r2
    p0 = (1.0 + 9.0 * q + 9.0 * q * q + q * q * q) * r4 * r2 * r
    u = gain * BLK
    c0 = gain * p0
    c1 = gain * u * (p1 - 0.5 * p2 * gain + p3 * gain * gain * (1.0 / 3))
    c2 = gain * u * u * (0.5 * p2 - 0.5 * p3 * gain)
    c3 = gain * u * u * u * p3 * (1.0 / 6)
    lam = BLK * log_pole
    beta = jnp.exp(laps * lam)
    b0 = 1.0 / (1.0 - beta)
    b1 = beta * b0 * b0
    b2 = b1 * b0 * (1.0 + beta)
    b3 = b1 * b0 * b0 * (1.0 + beta * (4.0 + beta))
    n = float(laps)
    e3 = c3 * b0
    e2 = c2 * b0 + 3.0 * n * c3 * b1
    e1 = c1 * b0 + 2.0 * n * c2 * b1 + 3.0 * n * n * c3 * b2
    e0 = c0 * b0 + n * c1 * b1 + n * n * c2 * b2 + n * n * n * c3 * b3
    return [lam, e0 * norm, e1 * norm, e2 * norm, e3 * norm]


def kernel(
    n_lon, n_lat,
    lon_hbm, lat_hbm, inc_hbm, spread_hbm, vert_hbm, out_hbm,
    lon_scale, lat_scale, inc_ref, spread_ref, vert_ref, out_ref,
    coef, column, inside, local_mom, mom_send, mom_recv, zon, rx, tx, back, fwd_mat, bwd_mat, mat_hi, mat_lo,
    in_sem, out_sem, ms_sem, mr_sem, s1_sem, r1_sem, s2_sem, r2_sem,
):
    nv, rows, lev, width = inc_ref.shape
    blocks = width // BLK
    laps = blocks * n_lon
    poles = nv * rows
    nlat = rows * n_lat
    group = min(4, rows)
    me_lon = lax.axis_index("lon")
    me = lax.axis_index("lat")
    my_v = lax.rem(me, nv)
    my_lev = me // nv

    loads = [
        pltpu.make_async_copy(lon_hbm, lon_scale, in_sem.at[0]),
        pltpu.make_async_copy(spread_hbm, spread_ref, in_sem.at[1]),
        pltpu.make_async_copy(lat_hbm, lat_scale, in_sem.at[2]),
        pltpu.make_async_copy(vert_hbm, vert_ref, in_sem.at[3]),
    ]
    fields = [pltpu.make_async_copy(inc_hbm.at[v], inc_ref.at[v], in_sem.at[4 + v]) for v in range(nv)]
    for load in loads[:2] + fields + loads[2:]:
        load.start()

    barrier = pltpu.get_barrier_semaphore()

    for s in range(1, n_lon):
        pl.semaphore_signal(
            barrier, inc=1, device_id={"lon": lax.rem(me_lon + s, n_lon)}, device_id_type=MESH
        )

    @pl.loop(1, n_lat)
    def _(k):
        pl.semaphore_signal(barrier, inc=1, device_id={"lat": lax.rem(me + k, n_lat)}, device_id_type=MESH)

    loads[0].wait()
    loads[1].wait()
    row_of = lax.broadcasted_iota(jnp.int32, (poles, BLK), 0)
    scale = jnp.zeros((poles, BLK), F32)
    for v in range(nv):
        for t in range(rows):
            scale = jnp.where(row_of == v * rows + t, lon_scale[v, t], scale)
    for k, part in enumerate(circle_terms(scale, laps)):
        coef[k] = part
    eye = lax.broadcasted_iota(jnp.int32, (lev, lev), 0) == lax.broadcasted_iota(jnp.int32, (lev, lev), 1)
    for v in range(nv):
        for t in range(rows):
            line = jnp.broadcast_to(spread_ref[v, t : t + 1, :], (lev, lev))
            one = jnp.sum(jnp.where(eye, line, 0.0), axis=1, keepdims=True)
            column[v, t] = jnp.broadcast_to(one, (lev, BLK))

    def tile(shape, dim):
        return lax.broadcasted_iota(jnp.int32, shape, dim)

    lane8 = tile((8, BLK), 1).astype(F32) * (1.0 / BLK)
    order = tile((8, BLK), 0)
    ahead = order < 4
    rank = lax.rem(order, 4)
    to_end = 1.0 - lane8
    to_start = lane8 + 1.0 / BLK
    behind = lane8
    before = (BLK - 1.0) / BLK - lane8

    def power(tau):
        t2 = tau * tau
        return jnp.where(rank == 0, 1.0, jnp.where(rank == 1, tau, jnp.where(rank == 2, t2, t2 * tau)))

    def coefs(r):
        return [coef[k, pl.ds(r, 1), :] for k in range(5)]

    def wide_column(v, t):
        one = column[v, t]
        return jnp.concatenate([one] * blocks, axis=1)

    def first(v, g):
        pieces = []
        for u in range(group):
            t = g * group + u
            lam, e0, e1, e2, e3 = coefs(v * rows + t)
            x = inc_ref[v, t] * wide_column(v, t)
            stacked = jnp.concatenate([x[:, c * BLK : (c + 1) * BLK] for c in range(blocks)], axis=0)
            gap = jnp.abs(tile((BLK, BLK), 0) - tile((BLK, BLK), 1)).astype(F32) * (1.0 / BLK)
            far = float(laps) - gap
            near = jnp.exp(lam * gap) * (e0 + gap * (e1 + gap * (e2 + gap * e3)))
            around = jnp.exp(lam * far) * (e0 + far * (e1 + far * (e2 + far * e3)))
            inside[v, t] = dot3(split(stacked), split(near + around), ((1,), (0,)))
            tau = jnp.where(ahead, to_end, to_start)
            small = jnp.exp(lam * tau) * power(tau)
            nothing = jnp.zeros((8, BLK), F32)
            lines = []
            for c in range(blocks):
                lines.append(jnp.concatenate([small if d == c else nothing for d in range(blocks)], axis=1))
            whole = []
            for c in range(blocks):
                shifted = jnp.where(ahead, to_end + float(blocks - 1 - c), to_start + float(c))
                whole.append(jnp.exp(lam * shifted) * power(shifted))
            lines.append(jnp.concatenate(whole, axis=1))
            basis = jnp.concatenate(lines, axis=0)
            moments = dot3(split(basis), split(x), ((1,), (1,)))
            local_mom[v, t] = moments[: 8 * blocks]
            pieces.append(moments[8 * blocks :])
        mom_send[v, g] = jnp.concatenate(pieces, axis=1)

    def moment_copy(v, s):
        return pltpu.make_async_remote_copy(
            src_ref=mom_send.at[v],
            dst_ref=mom_recv.at[v, s - 1],
            send_sem=ms_sem.at[v, s - 1],
            recv_sem=mr_sem.at[v, s - 1],
            device_id={"lon": lax.rem(me_lon + s, n_lon)},
            device_id_type=MESH,
        )

    for v in range(nv):
        fields[v].wait()

        @pl.loop(0, rows // group)
        def _(g):
            first(v, g)

        if v == 0:
            pl.semaphore_wait(barrier, n_lat - 1 + n_lon - 1)
        for s in range(1, n_lon):
            moment_copy(v, s).start()

    def second(v, g):
        for u in range(group):
            t = g * group + u
            lam, e0, e1, e2, e3 = coefs(v * rows + t)

            def mixed(a0, a1, a2, a3):
                return jnp.where(rank == 0, a0, jnp.where(rank == 1, a1, jnp.where(rank == 2, a2, a3)))

            q0 = mixed(e0, e1, e2, e3)
            q1 = mixed(e1, 2.0 * e2, 3.0 * e3, 0.0)
            q2 = mixed(e2, 3.0 * e3, 0.0, 0.0)
            q3 = mixed(e3, 0.0, 0.0, 0.0)

            def reach(y):
                return jnp.exp(lam * y) * (q0 + y * (q1 + y * (q2 + y * q3)))

            by_gap = {}
            for gap in list(range(1, blocks)) + list(range(laps - blocks + 1, laps)):
                by_gap[gap] = reach(jnp.where(ahead, behind + float(gap - 1), before + float(laps - gap - 1)))
            nothing = jnp.zeros((8, BLK), F32)
            lines = []
            for c in range(blocks):
                lines.append(
                    jnp.concatenate(
                        [nothing if d == c else by_gap[(d - c) % laps] for d in range(blocks)], axis=1
                    )
                )
            sources = [local_mom[v, t]]
            for s in range(1, n_lon):
                line = []
                for d in range(blocks):
                    line.append(
                        reach(
                            jnp.where(
                                ahead,
                                behind + float(d + blocks * (s - 1)),
                                before + float(blocks - 1 - d + blocks * (n_lon - 1 - s)),
                            )
                        )
                    )
                lines.append(jnp.concatenate(line, axis=1))
                sources.append(mom_recv[v, s - 1, g][:, u * lev : (u + 1) * lev])
            table = jnp.concatenate(lines, axis=0)
            moments = jnp.concatenate(sources, axis=0)
            added = dot3(split(moments.T), split(table), ((1,), (0,)))
            own = inside[v, t]
            own = jnp.concatenate([own[c * lev : (c + 1) * lev] for c in range(blocks)], axis=1)
            total = own + added
            for c in range(blocks):
                zon[v, c, pl.ds(t, lev, stride=rows), :] = total[:, c * BLK : (c + 1) * BLK]

    parts = 2
    wide = blocks // parts

    def out_copy(d, v, level, h):
        return pltpu.make_async_remote_copy(
            src_ref=zon.at[v, h * wide : (h + 1) * wide, pl.ds(level * rows, rows), :],
            dst_ref=rx.at[h * wide : (h + 1) * wide, pl.ds(me * rows, rows), :],
            send_sem=s1_sem.at[h],
            recv_sem=r1_sem.at[h],
            device_id={"lat": d},
            device_id_type=MESH,
        )

    def send(v, h):
        @pl.loop(0, lev)
        def _(k):
            level = lax.rem(my_lev + k, lev)
            d = level * nv + v

            @pl.when(d != me)
            def _():
                out_copy(d, v, level, h).start()

    for v in range(nv):
        for s in range(1, n_lon):
            moment_copy(v, s).wait()

        @pl.loop(0, rows // group)
        def _(g):
            second(v, g)

        send(v, 0)
    for h in range(1, parts):
        for v in range(nv):
            send(v, h)

    loads[2].wait()
    mine = jnp.full((8, BLK), lat_scale[my_v, my_lev], F32)
    gain, pole, log_pole, norm = [part[:1] for part in pole_terms(mine)]
    g2 = gain * gain
    lead = g2 * g2 * (1.0 / 6)
    size = min(BLK, nlat)

    @pl.loop(0, nlat // size)
    def _(i):
        for j in range(nlat // size):
            away = (i - j) * size + tile((size, size), 0) - tile((size, size), 1)
            n = jnp.abs(away).astype(F32)
            value = lead[:, :size] * (n + 1.0) * (n + 2.0) * (n + 3.0) * jnp.exp(log_pole[:, :size] * n)
            fwd_mat[pl.ds(i * size, size), j * size : (j + 1) * size] = jnp.where(away >= 0, value, 0.0)
            bwd_mat[pl.ds(i * size, size), j * size : (j + 1) * size] = jnp.where(
                away <= 0, norm[:, :size] * value, 0.0
            )

    @pl.loop(0, nlat // size)
    def _(i):
        at = pl.ds(i * size, size)
        both = dot3(split(bwd_mat[at, :]), split(fwd_mat[...]), ((1,), (0,)))
        mat_hi[at, :], mat_lo[at, :] = split(both)

    rx[:, pl.ds(me * rows, rows), :] = zon[my_v, :, pl.ds(my_lev * rows, rows), :]
    some = pl.ds(0, (n_lat - 1) * rows)

    def drain(ref, h, sem):
        view = ref.at[h * wide : (h + 1) * wide, some, :]
        pltpu.make_async_copy(view, view, sem.at[h]).wait()

    slot = pl.ds((my_v * lev + my_lev) * rows, rows)

    def back_copy(d, h):
        return pltpu.make_async_remote_copy(
            src_ref=tx.at[h * wide : (h + 1) * wide, pl.ds(d * rows, rows), :],
            dst_ref=back.at[h * wide : (h + 1) * wide, slot, :],
            send_sem=s2_sem.at[h],
            recv_sem=r2_sem.at[h],
            device_id={"lat": d},
            device_id_type=MESH,
        )

    def columns(h):
        return range(h * wide, (h + 1) * wide)

    for h in range(parts):
        drain(rx, h, r1_sem)

        @pl.loop(0, nlat // size)
        def _(i):
            at = pl.ds(i * size, size)
            everything = jnp.concatenate([rx[c] for c in columns(h)], axis=1)
            result = dot3((mat_hi[at, :], mat_lo[at, :]), split(everything), ((1,), (0,)))
            for k, c in enumerate(columns(h)):
                tx[c, at, :] = result[:, k * BLK : (k + 1) * BLK]

        @pl.loop(1, n_lat)
        def _(k):
            back_copy(lax.rem(me + k, n_lat), h).start()

    back[:, slot, :] = tx[:, pl.ds(me * rows, rows), :]
    loads[3].wait()
    weights = [split(vert_ref[v]) for v in range(nv)]
    def store(v, h):
        at = pl.ds(h * wide * BLK, wide * BLK)
        return pltpu.make_async_copy(out_ref.at[v, :, :, at], out_hbm.at[v, :, :, at], out_sem.at[h, v])

    for h in range(parts):
        drain(back, h, r2_sem)
        for v in range(nv):

            @pl.loop(0, rows)
            def _(t):
                levels = jnp.concatenate(
                    [back[c, pl.ds(v * lev * rows + t, lev, stride=rows), :] for c in columns(h)], axis=1
                )
                scaling = jnp.concatenate([column[v, t]] * wide, axis=1)
                out_ref[v, t, :, h * wide * BLK : (h + 1) * wide * BLK] = (
                    dot3(weights[v], split(levels), ((1,), (0,))) * scaling
                )

            store(v, h).start()

    for h in range(parts):
        drain(tx, h, s1_sem)
        drain(tx, h, s2_sem)
        for v in range(nv):
            store(v, h).wait()


def per_device(n_lon, n_lat, increment, spread, lon_scale, lat_scale, vertical):
    nv, rows, lev, width = increment.shape
    blocks = width // BLK
    poles = nv * rows
    nlat = rows * n_lat
    group = min(4, rows)
    hbm = pl.BlockSpec(memory_space=pltpu.MemorySpace.HBM)
    return pl.pallas_call(
        functools.partial(kernel, n_lon, n_lat),
        out_shape=jax.ShapeDtypeStruct(increment.shape, F32),
        in_specs=[hbm] * 5,
        out_specs=hbm,
        scratch_shapes=[
            pltpu.SMEM((nv, rows), F32),
            pltpu.SMEM((nv, lev), F32),
            pltpu.VMEM(increment.shape, F32),
            pltpu.VMEM((nv, rows, lev), F32),
            pltpu.VMEM((nv, lev, lev), F32),
            pltpu.VMEM(increment.shape, F32),
            pltpu.VMEM((5, poles, BLK), F32),
            pltpu.VMEM((nv, rows, lev, BLK), F32),
            pltpu.VMEM((nv, rows, blocks * lev, BLK), F32),
            pltpu.VMEM((nv, rows, 8 * blocks, lev), F32),
            pltpu.VMEM((nv, rows // group, 8, group * lev), F32),
            pltpu.VMEM((nv, n_lon - 1, rows // group, 8, group * lev), F32),
            pltpu.VMEM((nv, blocks, lev * rows, BLK), F32),
            pltpu.VMEM((blocks, nlat, BLK), F32),
            pltpu.VMEM((blocks, nlat, BLK), F32),
            pltpu.VMEM((blocks, nv * lev * rows, BLK), F32),
            pltpu.VMEM((nlat, nlat), F32),
            pltpu.VMEM((nlat, nlat), F32),
            pltpu.VMEM((nlat, nlat), BF16),
            pltpu.VMEM((nlat, nlat), BF16),
            pltpu.SemaphoreType.DMA((4 + nv,)),
            pltpu.SemaphoreType.DMA((2, nv)),
            pltpu.SemaphoreType.DMA((nv, n_lon - 1)),
            pltpu.SemaphoreType.DMA((nv, n_lon - 1)),
            pltpu.SemaphoreType.DMA((2,)),
            pltpu.SemaphoreType.DMA((2,)),
            pltpu.SemaphoreType.DMA((2,)),
            pltpu.SemaphoreType.DMA((2,)),
        ],
        compiler_params=pltpu.CompilerParams(
            collective_id=0, has_side_effects=True, vmem_limit_bytes=60 * 1024 * 1024
        ),
    )(lon_scale, lat_scale, increment, spread, vertical)


def solution(mesh):
    in_specs = (P(None, "lat", None, "lon"), P(None, "lat", None), P(None, "lat"), P(), P())
    out_specs = P(None, "lat", None, "lon")
    body = functools.partial(per_device, mesh.shape["lon"], mesh.shape["lat"])
    return jax.shard_map(body, mesh=mesh, in_specs=in_specs, out_specs=out_specs, check_vma=False)
```

```python
import functools
import math

import jax
import jax.numpy as jnp
from jax import lax
from jax.experimental import pallas as pl
from jax.experimental.pallas import tpu as pltpu
from jax.sharding import PartitionSpec as P

MESH = pl.DeviceIdType.MESH
BLK = 128
RING = 8
F32 = jnp.float32
BF16 = jnp.bfloat16


def split(a):
    high = a.astype(BF16)
    return high, (a - high.astype(F32)).astype(BF16)


def dot3(a, b, dims):
    ah, al = a
    bh, bl = b

    def one(p, q):
        return lax.dot_general(p, q, (dims, ((), ())), preferred_element_type=F32)

    return one(ah, bh) + (one(ah, bl) + one(al, bh))


def pole_terms(scale):
    x = 1.0 / scale
    t = jnp.ones_like(x)
    for k in range(10, 1, -1):
        t = 1.0 - x * (1.0 / k) * t
    pole = 1.0 - x * t
    gain = 1.0 - pole
    s = gain / (2.0 - gain)
    s2 = s * s
    series = 1.0 / 3 + s2 * (1.0 / 5 + s2 * (1.0 / 7 + s2 * (1.0 / 9 + s2 * (1.0 / 11))))
    log_pole = -2.0 * s * (1.0 + s2 * series)
    norm = jnp.sqrt((2.0 * math.sqrt(math.pi)) * jnp.sqrt(8.0 * pole) / gain)
    return gain, pole, log_pole, norm


def circle_terms(scale, laps):
    gain, pole, log_pole, norm = pole_terms(scale)
    q = pole * pole
    r = 1.0 / (1.0 + pole)
    r2 = r * r
    r4 = r2 * r2
    p3 = r4
    p2 = (3.0 + q) * r4 * r
    p1 = (3.0 + 6.0 * q + q * q) * r4 * r2
    p0 = (1.0 + 9.0 * q + 9.0 * q * q + q * q * q) * r4 * r2 * r
    u = gain * BLK
    c0 = gain * p0
    c1 = gain * u * (p1 - 0.5 * p2 * gain + p3 * gain * gain * (1.0 / 3))
    c2 = gain * u * u * (0.5 * p2 - 0.5 * p3 * gain)
    c3 = gain * u * u * u * p3 * (1.0 / 6)
    lam = BLK * log_pole
    beta = jnp.exp(laps * lam)
    b0 = 1.0 / (1.0 - beta)
    b1 = beta * b0 * b0
    b2 = b1 * b0 * (1.0 + beta)
    b3 = b1 * b0 * b0 * (1.0 + beta * (4.0 + beta))
    n = float(laps)
    e3 = c3 * b0
    e2 = c2 * b0 + 3.0 * n * c3 * b1
    e1 = c1 * b0 + 2.0 * n * c2 * b1 + 3.0 * n * n * c3 * b2
    e0 = c0 * b0 + n * c1 * b1 + n * n * c2 * b2 + n * n * n * c3 * b3
    return [lam, e0 * norm, e1 * norm, e2 * norm, e3 * norm]


def line_terms(scale, run):
    gain, pole, log_pole, norm = pole_terms(scale)
    g2 = gain * gain
    g4 = g2 * g2
    cubic = [g4, g4 * (11.0 / 6 * run), g4 * float(run**2), g4 * (1.0 / 6 * run**3)]
    return run * log_pole, cubic, norm


def kernel(
    n_lon, n_lat,
    lon_hbm, lat_hbm, inc_hbm, spread_hbm, vert_hbm, out_hbm,
    lon_scale, lat_scale, inc_ref, spread_ref, vert_ref, out_ref,
    coef, column, inside, local_mom, mom_send, mom_recv, zon,
    pair_raw, merged, rx, tx, coming, pair_out, back,
    down_hi, down_lo, up_hi, up_lo, runs, turns, mat_hi, mat_lo,
    in_sem, out_sem, ms_sem, mr_sem, ps_sem, pr_sem, s1_sem, r1_sem, s2_sem, r2_sem, rz_sem, so_sem, ro_sem,
):
    nv, rows, lev, width = inc_ref.shape
    blocks = width // BLK
    laps = blocks * n_lon
    poles = nv * rows
    group = min(4, rows)
    me_lon = lax.axis_index("lon")
    me = lax.axis_index("lat")
    groups = n_lat // RING
    halves = RING // 2
    block = groups * rows
    g_me, z_me = me // RING, lax.rem(me, RING)
    duo, odd = z_me // 2, lax.rem(z_me, 2)
    side = 2 * odd - 1
    mate = z_me - side
    my_v, my_lev = odd, duo * groups + g_me

    loads = [
        pltpu.make_async_copy(lon_hbm, lon_scale, in_sem.at[0]),
        pltpu.make_async_copy(spread_hbm, spread_ref, in_sem.at[1]),
        pltpu.make_async_copy(lat_hbm, lat_scale, in_sem.at[2]),
        pltpu.make_async_copy(vert_hbm, vert_ref, in_sem.at[3]),
    ]
    fields = [pltpu.make_async_copy(inc_hbm.at[v], inc_ref.at[v], in_sem.at[4 + v]) for v in range(nv)]
    for load in loads[:2] + fields + loads[2:]:
        load.start()

    barrier = pltpu.get_barrier_semaphore()

    for s in range(1, n_lon):
        pl.semaphore_signal(
            barrier, inc=1, device_id={"lon": lax.rem(me_lon + s, n_lon)}, device_id_type=MESH
        )

    @pl.loop(1, n_lat)
    def _(k):
        pl.semaphore_signal(barrier, inc=1, device_id={"lat": lax.rem(me + k, n_lat)}, device_id_type=MESH)

    loads[0].wait()
    loads[1].wait()
    row_of = lax.broadcasted_iota(jnp.int32, (poles, BLK), 0)
    scale = jnp.zeros((poles, BLK), F32)
    for v in range(nv):
        for t in range(rows):
            scale = jnp.where(row_of == v * rows + t, lon_scale[v, t], scale)
    for k, part in enumerate(circle_terms(scale, laps)):
        coef[k] = part
    eye = lax.broadcasted_iota(jnp.int32, (lev, lev), 0) == lax.broadcasted_iota(jnp.int32, (lev, lev), 1)
    for v in range(nv):
        for t in range(rows):
            line = jnp.broadcast_to(spread_ref[v, t : t + 1, :], (lev, lev))
            one = jnp.sum(jnp.where(eye, line, 0.0), axis=1, keepdims=True)
            column[v, t] = jnp.broadcast_to(one, (lev, BLK))

    def tile(shape, dim):
        return lax.broadcasted_iota(jnp.int32, shape, dim)

    lane8 = tile((8, BLK), 1).astype(F32) * (1.0 / BLK)
    order = tile((8, BLK), 0)
    ahead = order < 4
    rank = lax.rem(order, 4)
    to_end = 1.0 - lane8
    to_start = lane8 + 1.0 / BLK
    behind = lane8
    before = (BLK - 1.0) / BLK - lane8

    def power(tau):
        t2 = tau * tau
        return jnp.where(rank == 0, 1.0, jnp.where(rank == 1, tau, jnp.where(rank == 2, t2, t2 * tau)))

    def coefs(r):
        return [coef[k, pl.ds(r, 1), :] for k in range(5)]

    def wide_column(v, t):
        one = column[v, t]
        return jnp.concatenate([one] * blocks, axis=1)

    def first(v, g):
        pieces = []
        for u in range(group):
            t = g * group + u
            lam, e0, e1, e2, e3 = coefs(v * rows + t)
            x = inc_ref[v, t] * wide_column(v, t)
            stacked = jnp.concatenate([x[:, c * BLK : (c + 1) * BLK] for c in range(blocks)], axis=0)
            gap = jnp.abs(tile((BLK, BLK), 0) - tile((BLK, BLK), 1)).astype(F32) * (1.0 / BLK)
            far = float(laps) - gap
            near = jnp.exp(lam * gap) * (e0 + gap * (e1 + gap * (e2 + gap * e3)))
            around = jnp.exp(lam * far) * (e0 + far * (e1 + far * (e2 + far * e3)))
            inside[v, t] = dot3(split(stacked), split(near + around), ((1,), (0,)))
            tau = jnp.where(ahead, to_end, to_start)
            small = jnp.exp(lam * tau) * power(tau)
            nothing = jnp.zeros((8, BLK), F32)
            lines = []
            for c in range(blocks):
                lines.append(jnp.concatenate([small if d == c else nothing for d in range(blocks)], axis=1))
            whole = []
            for c in range(blocks):
                shifted = jnp.where(ahead, to_end + float(blocks - 1 - c), to_start + float(c))
                whole.append(jnp.exp(lam * shifted) * power(shifted))
            lines.append(jnp.concatenate(whole, axis=1))
            basis = jnp.concatenate(lines, axis=0)
            moments = dot3(split(basis), split(x), ((1,), (1,)))
            local_mom[v, t] = moments[: 8 * blocks]
            pieces.append(moments[8 * blocks :])
        mom_send[v, g] = jnp.concatenate(pieces, axis=1)

    def moment_copy(v, s):
        return pltpu.make_async_remote_copy(
            src_ref=mom_send.at[v],
            dst_ref=mom_recv.at[v, s - 1],
            send_sem=ms_sem.at[v, s - 1],
            recv_sem=mr_sem.at[v, s - 1],
            device_id={"lon": lax.rem(me_lon + s, n_lon)},
            device_id_type=MESH,
        )

    for v in range(nv):
        fields[v].wait()

        @pl.loop(0, rows // group)
        def _(g):
            first(v, g)

        if v == 0:
            pl.semaphore_wait(barrier, n_lat - 1 + n_lon - 1)
        for s in range(1, n_lon):
            moment_copy(v, s).start()

    def second(v, g):
        for u in range(group):
            t = g * group + u
            lam, e0, e1, e2, e3 = coefs(v * rows + t)

            def mixed(a0, a1, a2, a3):
                return jnp.where(rank == 0, a0, jnp.where(rank == 1, a1, jnp.where(rank == 2, a2, a3)))

            q0 = mixed(e0, e1, e2, e3)
            q1 = mixed(e1, 2.0 * e2, 3.0 * e3, 0.0)
            q2 = mixed(e2, 3.0 * e3, 0.0, 0.0)
            q3 = mixed(e3, 0.0, 0.0, 0.0)

            def reach(y):
                return jnp.exp(lam * y) * (q0 + y * (q1 + y * (q2 + y * q3)))

            by_gap = {}
            for gap in list(range(1, blocks)) + list(range(laps - blocks + 1, laps)):
                by_gap[gap] = reach(jnp.where(ahead, behind + float(gap - 1), before + float(laps - gap - 1)))
            nothing = jnp.zeros((8, BLK), F32)
            lines = []
            for c in range(blocks):
                lines.append(
                    jnp.concatenate(
                        [nothing if d == c else by_gap[(d - c) % laps] for d in range(blocks)], axis=1
                    )
                )
            sources = [local_mom[v, t]]
            for s in range(1, n_lon):
                line = []
                for d in range(blocks):
                    line.append(
                        reach(
                            jnp.where(
                                ahead,
                                behind + float(d + blocks * (s - 1)),
                                before + float(blocks - 1 - d + blocks * (n_lon - 1 - s)),
                            )
                        )
                    )
                lines.append(jnp.concatenate(line, axis=1))
                sources.append(mom_recv[v, s - 1, g][:, u * lev : (u + 1) * lev])
            table = jnp.concatenate(lines, axis=0)
            moments = jnp.concatenate(sources, axis=0)
            added = dot3(split(moments.T), split(table), ((1,), (0,)))
            own = inside[v, t]
            own = jnp.concatenate([own[c * lev : (c + 1) * lev] for c in range(blocks)], axis=1)
            total = own + added
            for c in range(blocks):
                zon[v, c, pl.ds(t, lev, stride=rows), :] = total[:, c * BLK : (c + 1) * BLK]

    parts = 2
    wide = blocks // parts
    run = 2 * rows

    def part(h):
        return pl.ds(h * wide, wide)

    def columns(h):
        return range(h * wide, (h + 1) * wide)

    def row_of_set(w):
        return (w // 2) * block

    def lead(j):
        return lax.rem(z_me + side * j + RING, RING)

    def mate_lead(j):
        return lax.rem(z_me - side * (j + 1) + RING, RING)

    def spot(shape, dim, swap):
        at = tile(shape, dim)
        return lax.rem(at, rows) + rows * jnp.abs(at // block - swap)

    def pair_of(shape, dim):
        return lax.rem(tile(shape, dim), block) // rows

    def graded(tau, kind):
        t2 = tau * tau
        return jnp.where(kind == 0, 1.0, jnp.where(kind == 1, tau, jnp.where(kind == 2, t2, t2 * tau)))

    def set_matrices(lam, cubic, norm, swap):
        unit = 1.0 / run
        shape = (block, 2 * block)
        kind = lax.rem(tile(shape, 0), rows)
        pos = spot(shape, 1, swap).astype(F32)
        tau = jnp.where(kind < 4, run - pos, pos + 1.0) * unit
        same = pair_of(shape, 0) == pair_of(shape, 1)
        basis = jnp.where(same, jnp.exp(lam * tau) * graded(tau, lax.rem(kind, 4)), 0.0)
        shape = (2 * block, 2 * block)
        away = spot(shape, 0, swap) - spot(shape, 1, swap)
        gap = jnp.abs(away).astype(F32) * unit
        same = pair_of(shape, 0) == pair_of(shape, 1)
        value = cubic[0] + gap * (cubic[1] + gap * (cubic[2] + gap * cubic[3]))
        value = jnp.where(same, jnp.exp(lam * gap) * value, 0.0)
        ahead_of = split(jnp.where(away >= 0, value, 0.0))
        behind_of = split(jnp.where(away <= 0, value, 0.0) * norm)
        down = jnp.where(kind < 4, basis, dot3(split(basis), ahead_of, ((1,), (0,))))
        near = dot3(behind_of, ahead_of, ((1,), (0,)))
        shape = (2 * block, block)
        kind = lax.rem(tile(shape, 1), rows)
        pos = spot(shape, 0, swap).astype(F32)
        tau = jnp.where(kind < 4, pos, run - 1.0 - pos) * unit
        same = pair_of(shape, 0) == pair_of(shape, 1)
        basis = jnp.where(same, jnp.exp(lam[:, :block] * tau) * graded(tau, lax.rem(kind, 4)), 0.0)
        up = jnp.where(kind < 4, dot3(behind_of, split(basis), ((1,), (0,))), basis * norm[:, :block])
        return down, near, up

    loads[2].wait()

    @pl.loop(1, 4)
    def _(j):
        w = lead(j)
        which = pair_of((8, 2 * block), 1)
        scales = jnp.ones((8, 2 * block), F32)
        for q in range(groups):
            scales = jnp.where(which == q, lat_scale[lax.rem(w, 2), (w // 2) * groups + q], scales)
        lam, cubic, norm = line_terms(scales, run)
        down, near, up = set_matrices(lam[:1], [p[:1] for p in cubic], norm[:1], odd)
        down_hi[j - 1], down_lo[j - 1] = split(down)
        up_hi[j - 1], up_lo[j - 1] = split(jnp.concatenate([near, up], axis=1))

    for v in range(nv):
        for s in range(1, n_lon):
            moment_copy(v, s).wait()

        @pl.loop(0, rows // group)
        def _(g):
            second(v, g)

    def pair_copy(j, h):
        w = mate_lead(j)
        return pltpu.make_async_remote_copy(
            src_ref=zon.at[lax.rem(w, 2), part(h), pl.ds(row_of_set(w), block), :],
            dst_ref=pair_raw.at[j - 1, part(h)],
            send_sem=ps_sem.at[h, j - 1],
            recv_sem=pr_sem.at[h, j - 1],
            device_id={"lat": g_me * RING + mate},
            device_id_type=MESH,
        )

    def raw_copy(w, q, h):
        return pltpu.make_async_remote_copy(
            src_ref=zon.at[lax.rem(w, 2), part(h), pl.ds(row_of_set(w) + q * rows, rows), :],
            dst_ref=rx.at[part(h), pl.ds((odd * groups + g_me) * rows, rows), :],
            send_sem=s1_sem.at[h],
            recv_sem=r1_sem.at[h],
            device_id={"lat": q * RING + w},
            device_id_type=MESH,
        )

    def merged_copy(j, q, h):
        w = lead(j)
        away = lax.rem(duo - w // 2 + halves, halves)
        return pltpu.make_async_remote_copy(
            src_ref=merged.at[j - 1, part(h), pl.ds(q * rows, rows), :],
            dst_ref=rx.at[part(h), pl.ds((2 * groups + 3 * g_me + away - 1) * rows, rows), :],
            send_sem=s1_sem.at[h],
            recv_sem=r1_sem.at[h],
            device_id={"lat": q * RING + w},
            device_id_type=MESH,
        )

    for h in range(parts):
        for j in (3, 2, 1):
            pair_copy(j, h).start()

        @pl.loop(0, groups)
        def _(k):
            raw_copy(mate, lax.rem(g_me + k, groups), h).start()

        @pl.loop(1, groups)
        def _(k):
            raw_copy(z_me, lax.rem(g_me + k, groups), h).start()

    def both_tiles(j, h):
        w = lead(j)
        at = pl.ds(row_of_set(w), block)
        mine = jnp.concatenate([zon[lax.rem(w, 2), c, at, :] for c in columns(h)], axis=1)
        other = jnp.concatenate([pair_raw[j - 1, c] for c in columns(h)], axis=1)
        return [mine, other]

    def merge(h):
        for j in (3, 2, 1):
            pair_copy(j, h).wait_recv()
            tiles = jnp.concatenate(both_tiles(j, h), axis=0)
            moments = dot3((down_hi[j - 1], down_lo[j - 1]), split(tiles), ((1,), (0,)))
            for k, c in enumerate(columns(h)):
                merged[j - 1, c] = moments[:, k * BLK : (k + 1) * BLK]

            @pl.loop(0, groups)
            def _(k):
                merged_copy(j, lax.rem(g_me + k, groups), h).start()

    merge(0)

    shape = (8, 2 * block)
    own_scale = jnp.full(shape, lat_scale[my_v, my_lev], F32)
    lam, cubic, norm = line_terms(own_scale, run)
    down, near, up = set_matrices(lam[:1], [p[:1] for p in cubic], norm[:1], 0)
    lam = lam[:, :1]
    cubic = [p[:, :1] for p in cubic]
    count = halves * groups
    states = 8 * count
    lane_slot = tile((8, states), 1) // 8
    lane_kind = lax.rem(tile((8, states), 1), 8)
    row_kind = tile((8, states), 0)

    def run_of(slot):
        other = slot - groups
        q = jnp.where(slot < groups, slot, other // 3)
        away = jnp.where(slot < groups, 0, lax.rem(other, 3) + 1)
        return q * halves + lax.rem(duo + away, halves)

    lane_run = jnp.zeros((8, states), F32)
    for n in range(count):
        q, away = (n, 0) if n < groups else ((n - groups) // 3, (n - groups) % 3 + 1)
        place = q * halves + lax.rem(duo + away, halves)
        lane_run = jnp.where(lane_slot == n, place.astype(F32), lane_run)
    a, b = lax.rem(row_kind, 4), lax.rem(lane_kind, 4)
    m = a + b
    mf = m.astype(F32)
    choose = jnp.where(m == 2, jnp.where(a == 1, 2.0, 1.0), jnp.where(m == 3, jnp.where((a == 1) | (a == 2), 3.0, 1.0), 1.0))

    def pick(shift):
        total = jnp.zeros((8, states), F32)
        for n in range(4 - shift):
            total = jnp.where(m == n, cubic[n + shift], total)
        return total * choose

    taylor = [pick(0), pick(1) * (mf + 1.0), pick(2) * ((mf + 1.0) * (mf + 2.0) * 0.5), pick(3)]
    turn = jnp.zeros((8, states), F32)
    for n in range(run):
        power_of = graded((n + 1.0) / run, a) * graded(n / run, b)
        turn = turn + jnp.exp(lam * ((2.0 * n + 1.0) / run)) * power_of
    turn = jnp.where((row_kind >= 4) & (lane_kind < 4), turn, 0.0)

    @pl.loop(0, count)
    def _(slot):
        here = run_of(slot).astype(F32)
        step = jnp.where(row_kind < 4, here - lane_run, lane_run - here) - 1.0
        live = ((row_kind < 4) == (lane_kind < 4)) & (step >= 0.0)
        reach = jnp.maximum(step, 0.0)
        value = taylor[0] + reach * (taylor[1] + reach * (taylor[2] + reach * taylor[3]))
        at = pl.ds(pl.multiple_of(slot * 8, 8), 8)
        runs[at, :] = jnp.where(live, jnp.exp(lam * reach) * value, 0.0)
        turns[at, :] = jnp.where(lane_slot == slot, turn, 0.0)

    down, up = split(down), split(up)
    steps = split(runs[...])
    turned = dot3(split(turns[...]), steps, ((1,), (0,)))
    whole = runs[...] + dot3(steps, split(turned), ((1,), (0,)))
    inner = dot3(split(whole[:, :block]), down, ((1,), (0,)))
    top = dot3(up, split(jnp.concatenate([inner[:block], whole[:block, block:]], axis=1)), ((1,), (0,)))
    top = jnp.concatenate([top[:, : 2 * block] + near, top[:, 2 * block :]], axis=1)
    bottom = jnp.concatenate([inner[block:], whole[block:, block:]], axis=1)
    mat_hi[: 2 * block, :], mat_lo[: 2 * block, :] = split(top)
    mat_hi[2 * block :, :], mat_lo[2 * block :, :] = split(bottom)

    for h in range(1, parts):
        merge(h)

    def drain(ref, h, count, sem):
        view = ref.at[part(h), pl.ds(0, count * rows), :]
        pltpu.make_async_copy(view, view, sem).wait()

    slot = pl.ds((my_v * lev + my_lev) * rows, rows)
    own = pl.ds((odd * groups + g_me) * rows, rows)

    def reply_raw(e, q, h):
        return pltpu.make_async_remote_copy(
            src_ref=tx.at[part(h), pl.ds((e * groups + q) * rows, rows), :],
            dst_ref=back.at[part(h), slot, :],
            send_sem=s2_sem.at[h],
            recv_sem=r2_sem.at[h],
            device_id={"lat": q * RING + 2 * duo + e},
            device_id_type=MESH,
        )

    def reply_state(away, q, h):
        z = 2 * lax.rem(duo + away, halves) + {1: 0, 2: 1 - odd, 3: 1}[away]
        j = {1: 2 - odd, 2: 3, 3: 1 + odd}[away]
        return pltpu.make_async_remote_copy(
            src_ref=tx.at[part(h), pl.ds((2 * groups + 3 * q + away - 1) * rows, rows), :],
            dst_ref=coming.at[j - 1, part(h), pl.ds(g_me * rows, rows), :],
            send_sem=s2_sem.at[h],
            recv_sem=rz_sem.at[h, j - 1],
            device_id={"lat": q * RING + z},
            device_id_type=MESH,
        )

    for h in range(parts):
        rx[part(h), own, :] = zon[my_v, part(h), pl.ds(my_lev * rows, rows), :]
        drain(rx, h, 5 * groups - 1, r1_sem.at[h])
        everything = jnp.concatenate([rx[c] for c in columns(h)], axis=1)
        result = dot3((mat_hi[...], mat_lo[...]), split(everything), ((1,), (0,)))
        for k, c in enumerate(columns(h)):
            tx[c] = result[:, k * BLK : (k + 1) * BLK]
        for away in (2, 1, 3):

            @pl.loop(0, groups)
            def _(k):
                reply_state(away, lax.rem(g_me + k, groups), h).start()

        @pl.loop(0, groups)
        def _(k):
            reply_raw(1 - odd, lax.rem(g_me + k, groups), h).start()

        @pl.loop(1, groups)
        def _(k):
            reply_raw(odd, lax.rem(g_me + k, groups), h).start()

        back[part(h), slot, :] = tx[part(h), own, :]

    def pair_back(j, h):
        w = lead(j)
        return pltpu.make_async_remote_copy(
            src_ref=pair_out.at[j - 1, part(h)],
            dst_ref=back.at[part(h), pl.ds(lax.rem(w, 2) * lev * rows + row_of_set(w), block), :],
            send_sem=so_sem.at[h, j - 1],
            recv_sem=ro_sem.at[h, j - 1],
            device_id={"lat": g_me * RING + mate},
            device_id_type=MESH,
        )

    for h in range(parts):
        for j in (1, 2, 3):
            view = coming.at[j - 1, part(h)]
            pltpu.make_async_copy(view, view, rz_sem.at[h, j - 1]).wait()
            coefficients = jnp.concatenate([coming[j - 1, c] for c in columns(h)], axis=1)
            inputs = jnp.concatenate(both_tiles(j, h) + [coefficients], axis=0)
            finished = dot3((up_hi[j - 1], up_lo[j - 1]), split(inputs), ((1,), (0,)))
            for k, c in enumerate(columns(h)):
                pair_out[j - 1, c] = finished[block:, k * BLK : (k + 1) * BLK]
            pair_back(j, h).start()
            w = lead(j)
            at = pl.ds(lax.rem(w, 2) * lev * rows + row_of_set(w), block)
            for k, c in enumerate(columns(h)):
                back[c, at, :] = finished[:block, k * BLK : (k + 1) * BLK]

    loads[3].wait()
    weights = [split(vert_ref[v]) for v in range(nv)]

    def store(v, h):
        at = pl.ds(h * wide * BLK, wide * BLK)
        return pltpu.make_async_copy(out_ref.at[v, :, :, at], out_hbm.at[v, :, :, at], out_sem.at[h, v])

    for h in range(parts):
        drain(back, h, 2 * groups - 1, r2_sem.at[h])
        for j in (1, 2, 3):
            pair_back(j, h).wait_recv()
        for v in range(nv):

            @pl.loop(0, rows)
            def _(t):
                levels = jnp.concatenate(
                    [back[c, pl.ds(v * lev * rows + t, lev, stride=rows), :] for c in columns(h)], axis=1
                )
                scaling = jnp.concatenate([column[v, t]] * wide, axis=1)
                out_ref[v, t, :, h * wide * BLK : (h + 1) * wide * BLK] = (
                    dot3(weights[v], split(levels), ((1,), (0,))) * scaling
                )

            store(v, h).start()

    for h in range(parts):
        drain(tx, h, 5 * groups - 1, s1_sem.at[h])
        drain(tx, h, 5 * groups - 1, s2_sem.at[h])
        for j in (1, 2, 3):
            pair_copy(j, h).wait_send()
            pair_back(j, h).wait_send()
        for v in range(nv):
            store(v, h).wait()


def per_device(n_lon, n_lat, increment, spread, lon_scale, lat_scale, vertical):
    nv, rows, lev, width = increment.shape
    blocks = width // BLK
    poles = nv * rows
    block = n_lat // RING * rows
    group = min(4, rows)
    hbm = pl.BlockSpec(memory_space=pltpu.MemorySpace.HBM)
    return pl.pallas_call(
        functools.partial(kernel, n_lon, n_lat),
        out_shape=jax.ShapeDtypeStruct(increment.shape, F32),
        in_specs=[hbm] * 5,
        out_specs=hbm,
        scratch_shapes=[
            pltpu.SMEM((nv, rows), F32),
            pltpu.SMEM((nv, lev), F32),
            pltpu.VMEM(increment.shape, F32),
            pltpu.VMEM((nv, rows, lev), F32),
            pltpu.VMEM((nv, lev, lev), F32),
            pltpu.VMEM(increment.shape, F32),
            pltpu.VMEM((5, poles, BLK), F32),
            pltpu.VMEM((nv, rows, lev, BLK), F32),
            pltpu.VMEM((nv, rows, blocks * lev, BLK), F32),
            pltpu.VMEM((nv, rows, 8 * blocks, lev), F32),
            pltpu.VMEM((nv, rows // group, 8, group * lev), F32),
            pltpu.VMEM((nv, n_lon - 1, rows // group, 8, group * lev), F32),
            pltpu.VMEM((nv, blocks, lev * rows, BLK), F32),
            pltpu.VMEM((3, blocks, block, BLK), F32),
            pltpu.VMEM((3, blocks, block, BLK), F32),
            pltpu.VMEM((blocks, 5 * block, BLK), F32),
            pltpu.VMEM((blocks, 5 * block, BLK), F32),
            pltpu.VMEM((3, blocks, block, BLK), F32),
            pltpu.VMEM((3, blocks, block, BLK), F32),
            pltpu.VMEM((blocks, nv * lev * rows, BLK), F32),
            pltpu.VMEM((3, block, 2 * block), BF16),
            pltpu.VMEM((3, block, 2 * block), BF16),
            pltpu.VMEM((3, 2 * block, 3 * block), BF16),
            pltpu.VMEM((3, 2 * block, 3 * block), BF16),
            pltpu.VMEM((4 * block, 4 * block), F32),
            pltpu.VMEM((4 * block, 4 * block), F32),
            pltpu.VMEM((5 * block, 5 * block), BF16),
            pltpu.VMEM((5 * block, 5 * block), BF16),
            pltpu.SemaphoreType.DMA((4 + nv,)),
            pltpu.SemaphoreType.DMA((2, nv)),
            pltpu.SemaphoreType.DMA((nv, n_lon - 1)),
            pltpu.SemaphoreType.DMA((nv, n_lon - 1)),
            pltpu.SemaphoreType.DMA((2, 3)),
            pltpu.SemaphoreType.DMA((2, 3)),
            pltpu.SemaphoreType.DMA((2,)),
            pltpu.SemaphoreType.DMA((2,)),
            pltpu.SemaphoreType.DMA((2,)),
            pltpu.SemaphoreType.DMA((2,)),
            pltpu.SemaphoreType.DMA((2, 3)),
            pltpu.SemaphoreType.DMA((2, 3)),
            pltpu.SemaphoreType.DMA((2, 3)),
        ],
        compiler_params=pltpu.CompilerParams(
            collective_id=0, has_side_effects=True, vmem_limit_bytes=60 * 1024 * 1024
        ),
    )(lon_scale, lat_scale, increment, spread, vertical)


def solution(mesh):
    in_specs = (P(None, "lat", None, "lon"), P(None, "lat", None), P(None, "lat"), P(), P())
    out_specs = P(None, "lat", None, "lon")
    body = functools.partial(per_device, mesh.shape["lon"], mesh.shape["lat"])
    return jax.shard_map(body, mesh=mesh, in_specs=in_specs, out_specs=out_specs, check_vma=False)
```

```python
import functools
import math

import jax
import jax.numpy as jnp
from jax import lax
from jax.experimental import pallas as pl
from jax.experimental.pallas import tpu as pltpu
from jax.sharding import PartitionSpec as P

MESH = pl.DeviceIdType.MESH
BLK = 128
PARTS = ((0, 2), (2, 4))
ORDER = "P0 R0 m0 P1 R1 B m1 o0 q0 o1 q1 f0 f1 x0 x1"
RING = 8
F32 = jnp.float32
BF16 = jnp.bfloat16


def split(a):
    high = a.astype(BF16)
    return high, (a - high.astype(F32)).astype(BF16)


def left(pair, dim=1):
    high, low = pair
    return jnp.concatenate([high, high, low], axis=dim)


def right(pair, dim=0):
    high, low = pair
    return jnp.concatenate([high, low, high], axis=dim)


def joined(a, b, dims=((1,), (0,))):
    return lax.dot_general(a, b, (dims, ((), ())), preferred_element_type=F32)


def dot3(a, b, dims=((1,), (0,))):
    return joined(left(a, dims[0][0]), right(b, dims[1][0]), dims)


def pole_terms(scale):
    x = 1.0 / scale
    t = jnp.ones_like(x)
    for k in range(10, 1, -1):
        t = 1.0 - x * (1.0 / k) * t
    pole = 1.0 - x * t
    gain = 1.0 - pole
    s = gain / (2.0 - gain)
    s2 = s * s
    series = 1.0 / 3 + s2 * (1.0 / 5 + s2 * (1.0 / 7 + s2 * (1.0 / 9 + s2 * (1.0 / 11))))
    log_pole = -2.0 * s * (1.0 + s2 * series)
    norm = jnp.sqrt((2.0 * math.sqrt(math.pi)) * jnp.sqrt(8.0 * pole) / gain)
    return gain, pole, log_pole, norm


def circle_terms(scale, laps):
    gain, pole, log_pole, norm = pole_terms(scale)
    q = pole * pole
    r = 1.0 / (1.0 + pole)
    r2 = r * r
    r4 = r2 * r2
    p3 = r4
    p2 = (3.0 + q) * r4 * r
    p1 = (3.0 + 6.0 * q + q * q) * r4 * r2
    p0 = (1.0 + 9.0 * q + 9.0 * q * q + q * q * q) * r4 * r2 * r
    u = gain * BLK
    c0 = gain * p0
    c1 = gain * u * (p1 - 0.5 * p2 * gain + p3 * gain * gain * (1.0 / 3))
    c2 = gain * u * u * (0.5 * p2 - 0.5 * p3 * gain)
    c3 = gain * u * u * u * p3 * (1.0 / 6)
    lam = BLK * log_pole
    beta = jnp.exp(laps * lam)
    b0 = 1.0 / (1.0 - beta)
    b1 = beta * b0 * b0
    b2 = b1 * b0 * (1.0 + beta)
    b3 = b1 * b0 * b0 * (1.0 + beta * (4.0 + beta))
    n = float(laps)
    e3 = c3 * b0
    e2 = c2 * b0 + 3.0 * n * c3 * b1
    e1 = c1 * b0 + 2.0 * n * c2 * b1 + 3.0 * n * n * c3 * b2
    e0 = c0 * b0 + n * c1 * b1 + n * n * c2 * b2 + n * n * n * c3 * b3
    return [lam, e0 * norm, e1 * norm, e2 * norm, e3 * norm]


def line_terms(scale, run):
    gain, pole, log_pole, norm = pole_terms(scale)
    g2 = gain * gain
    g4 = g2 * g2
    cubic = [g4, g4 * (11.0 / 6 * run), g4 * float(run**2), g4 * (1.0 / 6 * run**3)]
    return run * log_pole, cubic, norm


def kernel(
    n_lon, n_lat,
    lon_hbm, lat_hbm, inc_hbm, spread_hbm, vert_hbm, out_hbm,
    lon_scale, lat_scale, inc_ref, spread_ref, vert_ref, out_ref,
    coef, column, inside, tables, local_mom, mom_send, mom_recv, zon,
    pair_raw, merged, rx, tx, coming, pair_out, back,
    down_mat, up_mat, runs, turns, own_mat,
    in_sem, out_sem, ms_sem, mr_sem, ps_sem, pr_sem, s1_sem, r1_sem, s2_sem, r2_sem, rz_sem, so_sem, ro_sem,
):
    nv, rows, lev, width = inc_ref.shape
    blocks = width // BLK
    laps = blocks * n_lon
    poles = nv * rows
    group = min(4, rows)
    me_lon = lax.axis_index("lon")
    me = lax.axis_index("lat")
    groups = n_lat // RING
    halves = RING // 2
    block = groups * rows
    g_me, z_me = me // RING, lax.rem(me, RING)
    duo, odd = z_me // 2, lax.rem(z_me, 2)
    side = 2 * odd - 1
    mate = z_me - side
    my_v, my_lev = odd, duo * groups + g_me

    loads = [
        pltpu.make_async_copy(lon_hbm, lon_scale, in_sem.at[0]),
        pltpu.make_async_copy(spread_hbm, spread_ref, in_sem.at[1]),
        pltpu.make_async_copy(lat_hbm, lat_scale, in_sem.at[2]),
        pltpu.make_async_copy(vert_hbm, vert_ref, in_sem.at[3]),
    ]
    fields = [pltpu.make_async_copy(inc_hbm.at[v], inc_ref.at[v], in_sem.at[4 + v]) for v in range(nv)]
    for load in loads[:2] + fields + loads[2:]:
        load.start()

    barrier = pltpu.get_barrier_semaphore()

    for s in range(1, n_lon):
        pl.semaphore_signal(
            barrier, inc=1, device_id={"lon": lax.rem(me_lon + s, n_lon)}, device_id_type=MESH
        )

    @pl.loop(1, n_lat)
    def _(k):
        pl.semaphore_signal(barrier, inc=1, device_id={"lat": lax.rem(me + k, n_lat)}, device_id_type=MESH)

    loads[0].wait()
    loads[1].wait()
    row_of = lax.broadcasted_iota(jnp.int32, (poles, BLK), 0)
    scale = jnp.zeros((poles, BLK), F32)
    for v in range(nv):
        for t in range(rows):
            scale = jnp.where(row_of == v * rows + t, lon_scale[v, t], scale)
    for k, part in enumerate(circle_terms(scale, laps)):
        coef[k] = part
    eye = lax.broadcasted_iota(jnp.int32, (lev, lev), 0) == lax.broadcasted_iota(jnp.int32, (lev, lev), 1)
    for v in range(nv):
        for t in range(rows):
            line = jnp.broadcast_to(spread_ref[v, t : t + 1, :], (lev, lev))
            one = jnp.sum(jnp.where(eye, line, 0.0), axis=1, keepdims=True)
            column[v, t] = jnp.broadcast_to(one, (lev, BLK))

    def tile(shape, dim):
        return lax.broadcasted_iota(jnp.int32, shape, dim)

    lane8 = tile((8, BLK), 1).astype(F32) * (1.0 / BLK)
    order = tile((8, BLK), 0)
    ahead = order < 4
    rank = lax.rem(order, 4)
    to_end = 1.0 - lane8
    to_start = lane8 + 1.0 / BLK
    behind = lane8
    before = (BLK - 1.0) / BLK - lane8

    def power(tau):
        t2 = tau * tau
        return jnp.where(rank == 0, 1.0, jnp.where(rank == 1, tau, jnp.where(rank == 2, t2, t2 * tau)))

    def coefs(r):
        return [coef[k, pl.ds(r, 1), :] for k in range(5)]

    def wide_column(v, t):
        one = column[v, t]
        return jnp.concatenate([one] * blocks, axis=1)

    def first(v, g):
        pieces = []
        for u in range(group):
            t = g * group + u
            lam = coefs(v * rows + t)[0]
            x = inc_ref[v, t] * wide_column(v, t)
            inc_ref[v, t] = x
            tau = jnp.where(ahead, to_end, to_start)
            small = jnp.exp(lam * tau) * power(tau)
            nothing = jnp.zeros((8, BLK), F32)
            lines = []
            for c in range(blocks):
                lines.append(jnp.concatenate([small if d == c else nothing for d in range(blocks)], axis=1))
            whole = []
            for c in range(blocks):
                shifted = jnp.where(ahead, to_end + float(blocks - 1 - c), to_start + float(c))
                whole.append(jnp.exp(lam * shifted) * power(shifted))
            lines.append(jnp.concatenate(whole, axis=1))
            basis = jnp.concatenate(lines, axis=0)
            moments = dot3(split(basis), split(x), ((1,), (1,)))
            local_mom[v, t] = moments[: 8 * blocks]
            pieces.append(moments[8 * blocks :])
        mom_send[v, g] = jnp.concatenate(pieces, axis=1)

    def table_of(v, t, lam, e0, e1, e2, e3):
        def mixed(a0, a1, a2, a3):
            return jnp.where(rank == 0, a0, jnp.where(rank == 1, a1, jnp.where(rank == 2, a2, a3)))

        q0 = mixed(e0, e1, e2, e3)
        q1 = mixed(e1, 2.0 * e2, 3.0 * e3, 0.0)
        q2 = mixed(e2, 3.0 * e3, 0.0, 0.0)
        q3 = mixed(e3, 0.0, 0.0, 0.0)

        def reach(y):
            return jnp.exp(lam * y) * (q0 + y * (q1 + y * (q2 + y * q3)))

        by_gap = {}
        for gap in list(range(1, blocks)) + list(range(laps - blocks + 1, laps)):
            by_gap[gap] = reach(jnp.where(ahead, behind + float(gap - 1), before + float(laps - gap - 1)))
        nothing = jnp.zeros((8, BLK), F32)
        lines = []
        for c in range(blocks):
            lines.append(
                jnp.concatenate(
                    [nothing if d == c else by_gap[(d - c) % laps] for d in range(blocks)], axis=1
                )
            )
        for s in range(1, n_lon):
            line = []
            for d in range(blocks):
                line.append(
                    reach(
                        jnp.where(
                            ahead,
                            behind + float(d + blocks * (s - 1)),
                            before + float(blocks - 1 - d + blocks * (n_lon - 1 - s)),
                        )
                    )
                )
            lines.append(jnp.concatenate(line, axis=1))
        high, low = split(jnp.concatenate(lines, axis=0))
        tables[v, t, 0] = high
        tables[v, t, 1] = low

    def middle(v, g):
        for u in range(group):
            t = g * group + u
            lam, e0, e1, e2, e3 = coefs(v * rows + t)
            x = inc_ref[v, t]
            stacked = jnp.concatenate([x[:, c * BLK : (c + 1) * BLK] for c in range(blocks)], axis=0)
            gap = jnp.abs(tile((BLK, BLK), 0) - tile((BLK, BLK), 1)).astype(F32) * (1.0 / BLK)
            far = float(laps) - gap
            near = jnp.exp(lam * gap) * (e0 + gap * (e1 + gap * (e2 + gap * e3)))
            around = jnp.exp(lam * far) * (e0 + far * (e1 + far * (e2 + far * e3)))
            inside[v, t] = dot3(split(stacked), split(near + around))
            table_of(v, t, lam, e0, e1, e2, e3)

    def moment_copy(v, s):
        return pltpu.make_async_remote_copy(
            src_ref=mom_send.at[v],
            dst_ref=mom_recv.at[v, s - 1],
            send_sem=ms_sem.at[v, s - 1],
            recv_sem=mr_sem.at[v, s - 1],
            device_id={"lon": lax.rem(me_lon + s, n_lon)},
            device_id_type=MESH,
        )

    for v in range(nv):
        fields[v].wait()

        @pl.loop(0, rows // group)
        def _(g):
            first(v, g)

        if v == 0:
            pl.semaphore_wait(barrier, n_lat - 1 + n_lon - 1)
        for s in range(1, n_lon):
            moment_copy(v, s).start()

    def second(v, g):
        for u in range(group):
            t = g * group + u
            sources = [local_mom[v, t]]
            for s in range(1, n_lon):
                sources.append(mom_recv[v, s - 1, g][:, u * lev : (u + 1) * lev])
            moments = jnp.concatenate(sources, axis=0)
            added = dot3(split(moments.T), (tables[v, t, 0], tables[v, t, 1]))
            own = inside[v, t]
            own = jnp.concatenate([own[c * lev : (c + 1) * lev] for c in range(blocks)], axis=1)
            total = own + added
            for c in range(blocks):
                zon[v, c, pl.ds(t, lev, stride=rows), :] = total[:, c * BLK : (c + 1) * BLK]

    parts = len(PARTS)
    run = 2 * rows

    def part(h):
        return pl.ds(PARTS[h][0], PARTS[h][1] - PARTS[h][0])

    def columns(h):
        return range(*PARTS[h])

    def row_of_set(w):
        return (w // 2) * block

    def lead(j):
        return lax.rem(z_me + side * j + RING, RING)

    def mate_lead(j):
        return lax.rem(z_me - side * (j + 1) + RING, RING)

    def spot(shape, dim, swap):
        at = tile(shape, dim)
        return lax.rem(at, rows) + rows * jnp.abs(at // block - swap)

    def pair_of(shape, dim):
        return lax.rem(tile(shape, dim), block) // rows

    def graded(tau, kind):
        t2 = tau * tau
        return jnp.where(kind == 0, 1.0, jnp.where(kind == 1, tau, jnp.where(kind == 2, t2, t2 * tau)))

    def set_matrices(lam, cubic, norm, swap):
        unit = 1.0 / run
        shape = (block, 2 * block)
        kind = lax.rem(tile(shape, 0), rows)
        pos = spot(shape, 1, swap).astype(F32)
        tau = jnp.where(kind < 4, run - pos, pos + 1.0) * unit
        same = pair_of(shape, 0) == pair_of(shape, 1)
        basis = jnp.where(same, jnp.exp(lam * tau) * graded(tau, lax.rem(kind, 4)), 0.0)
        shape = (2 * block, 2 * block)
        away = spot(shape, 0, swap) - spot(shape, 1, swap)
        gap = jnp.abs(away).astype(F32) * unit
        same = pair_of(shape, 0) == pair_of(shape, 1)
        value = cubic[0] + gap * (cubic[1] + gap * (cubic[2] + gap * cubic[3]))
        value = jnp.where(same, jnp.exp(lam * gap) * value, 0.0)
        ahead_of = split(jnp.where(away >= 0, value, 0.0))
        behind_of = split(jnp.where(away <= 0, value, 0.0) * norm)
        down = jnp.where(kind < 4, basis, dot3(split(basis), ahead_of))
        near = dot3(behind_of, ahead_of)
        shape = (2 * block, block)
        kind = lax.rem(tile(shape, 1), rows)
        pos = spot(shape, 0, swap).astype(F32)
        tau = jnp.where(kind < 4, pos, run - 1.0 - pos) * unit
        same = pair_of(shape, 0) == pair_of(shape, 1)
        basis = jnp.where(same, jnp.exp(lam[:, :block] * tau) * graded(tau, lax.rem(kind, 4)), 0.0)
        up = jnp.where(kind < 4, dot3(behind_of, split(basis)), basis * norm[:, :block])
        return down, near, up

    loads[2].wait()

    @pl.loop(1, 4)
    def _(j):
        w = lead(j)
        which = pair_of((8, 2 * block), 1)
        scales = jnp.ones((8, 2 * block), F32)
        for q in range(groups):
            scales = jnp.where(which == q, lat_scale[lax.rem(w, 2), (w // 2) * groups + q], scales)
        lam, cubic, norm = line_terms(scales, run)
        down, near, up = set_matrices(lam[:1], [p[:1] for p in cubic], norm[:1], odd)
        down_mat[j - 1] = left(split(down))
        up_mat[j - 1] = left(split(jnp.concatenate([near, up], axis=1)))

    for v in range(nv):

        @pl.loop(0, rows // group)
        def _(g):
            middle(v, g)

    for v in range(nv):
        for s in range(1, n_lon):
            moment_copy(v, s).wait()

        @pl.loop(0, rows // group)
        def _(g):
            second(v, g)

    def pair_copy(j, h):
        w = mate_lead(j)
        return pltpu.make_async_remote_copy(
            src_ref=zon.at[lax.rem(w, 2), part(h), pl.ds(row_of_set(w), block), :],
            dst_ref=pair_raw.at[j - 1, part(h)],
            send_sem=ps_sem.at[h, j - 1],
            recv_sem=pr_sem.at[h, j - 1],
            device_id={"lat": g_me * RING + mate},
            device_id_type=MESH,
        )

    def raw_copy(w, q, h):
        return pltpu.make_async_remote_copy(
            src_ref=zon.at[lax.rem(w, 2), part(h), pl.ds(row_of_set(w) + q * rows, rows), :],
            dst_ref=rx.at[part(h), pl.ds((odd * groups + g_me) * rows, rows), :],
            send_sem=s1_sem.at[h],
            recv_sem=r1_sem.at[h],
            device_id={"lat": q * RING + w},
            device_id_type=MESH,
        )

    def merged_copy(j, q, h):
        w = lead(j)
        away = lax.rem(duo - w // 2 + halves, halves)
        return pltpu.make_async_remote_copy(
            src_ref=merged.at[j - 1, part(h), pl.ds(q * rows, rows), :],
            dst_ref=rx.at[part(h), pl.ds((2 * groups + 3 * g_me + away - 1) * rows, rows), :],
            send_sem=s1_sem.at[h],
            recv_sem=r1_sem.at[h],
            device_id={"lat": q * RING + w},
            device_id_type=MESH,
        )

    def send_pairs(h):
        for j in (3, 2, 1):
            pair_copy(j, h).start()

    def send_raw(h):
        @pl.loop(0, groups)
        def _(k):
            raw_copy(mate, lax.rem(g_me + k, groups), h).start()

        @pl.loop(1, groups)
        def _(k):
            raw_copy(z_me, lax.rem(g_me + k, groups), h).start()

    def both_tiles(j, h):
        w = lead(j)
        at = pl.ds(row_of_set(w), block)
        mine = jnp.concatenate([zon[lax.rem(w, 2), c, at, :] for c in columns(h)], axis=1)
        other = jnp.concatenate([pair_raw[j - 1, c] for c in columns(h)], axis=1)
        return [mine, other]

    def merge(h, which=(3, 2, 1)):
        for j in which:
            pair_copy(j, h).wait_recv()
            tiles = jnp.concatenate(both_tiles(j, h), axis=0)
            moments = joined(down_mat[j - 1], right(split(tiles)))
            for k, c in enumerate(columns(h)):
                merged[j - 1, c] = moments[:, k * BLK : (k + 1) * BLK]

            @pl.loop(0, groups)
            def _(k):
                merged_copy(j, lax.rem(g_me + k, groups), h).start()

    def build():
        shape = (8, 2 * block)
        own_scale = jnp.full(shape, lat_scale[my_v, my_lev], F32)
        lam, cubic, norm = line_terms(own_scale, run)
        down, near, up = set_matrices(lam[:1], [p[:1] for p in cubic], norm[:1], 0)
        lam = lam[:, :1]
        cubic = [p[:, :1] for p in cubic]
        count = halves * groups
        states = 8 * count
        lane_slot = tile((8, states), 1) // 8
        lane_kind = lax.rem(tile((8, states), 1), 8)
        row_kind = tile((8, states), 0)

        def run_of(slot):
            other = slot - groups
            q = jnp.where(slot < groups, slot, other // 3)
            away = jnp.where(slot < groups, 0, lax.rem(other, 3) + 1)
            return q * halves + lax.rem(duo + away, halves)

        lane_run = jnp.zeros((8, states), F32)
        for n in range(count):
            q, away = (n, 0) if n < groups else ((n - groups) // 3, (n - groups) % 3 + 1)
            place = q * halves + lax.rem(duo + away, halves)
            lane_run = jnp.where(lane_slot == n, place.astype(F32), lane_run)
        a, b = lax.rem(row_kind, 4), lax.rem(lane_kind, 4)
        m = a + b
        mf = m.astype(F32)
        choose = jnp.where(m == 2, jnp.where(a == 1, 2.0, 1.0), jnp.where(m == 3, jnp.where((a == 1) | (a == 2), 3.0, 1.0), 1.0))

        def pick(shift):
            total = jnp.zeros((8, states), F32)
            for n in range(4 - shift):
                total = jnp.where(m == n, cubic[n + shift], total)
            return total * choose

        taylor = [pick(0), pick(1) * (mf + 1.0), pick(2) * ((mf + 1.0) * (mf + 2.0) * 0.5), pick(3)]
        turn = jnp.zeros((8, states), F32)
        for n in range(run):
            power_of = graded((n + 1.0) / run, a) * graded(n / run, b)
            turn = turn + jnp.exp(lam * ((2.0 * n + 1.0) / run)) * power_of
        turn = jnp.where((row_kind >= 4) & (lane_kind < 4), turn, 0.0)

        @pl.loop(0, count)
        def _(slot):
            here = run_of(slot).astype(F32)
            step = jnp.where(row_kind < 4, here - lane_run, lane_run - here) - 1.0
            live = ((row_kind < 4) == (lane_kind < 4)) & (step >= 0.0)
            reach = jnp.maximum(step, 0.0)
            value = taylor[0] + reach * (taylor[1] + reach * (taylor[2] + reach * taylor[3]))
            at = pl.ds(pl.multiple_of(slot * 8, 8), 8)
            runs[at, :] = jnp.where(live, jnp.exp(lam * reach) * value, 0.0)
            turns[at, :] = jnp.where(lane_slot == slot, turn, 0.0)

        down, up = split(down), split(up)
        steps = split(runs[...])
        turned = dot3(split(turns[...]), steps)
        whole = runs[...] + dot3(steps, split(turned))
        inner = dot3(split(whole[:, :block]), down)
        top = dot3(up, split(jnp.concatenate([inner[:block], whole[:block, block:]], axis=1)))
        top = jnp.concatenate([top[:, : 2 * block] + near, top[:, 2 * block :]], axis=1)
        bottom = jnp.concatenate([inner[block:], whole[block:, block:]], axis=1)
        own_mat[: 2 * block, :] = left(split(top))
        own_mat[2 * block :, :] = left(split(bottom))

    def drain(ref, h, count, sem):
        view = ref.at[part(h), pl.ds(0, count * rows), :]
        pltpu.make_async_copy(view, view, sem).wait()

    slot = pl.ds((my_v * lev + my_lev) * rows, rows)
    own = pl.ds((odd * groups + g_me) * rows, rows)

    def reply_raw(e, q, h):
        return pltpu.make_async_remote_copy(
            src_ref=tx.at[part(h), pl.ds((e * groups + q) * rows, rows), :],
            dst_ref=back.at[part(h), slot, :],
            send_sem=s2_sem.at[h],
            recv_sem=r2_sem.at[h],
            device_id={"lat": q * RING + 2 * duo + e},
            device_id_type=MESH,
        )

    def reply_state(away, q, h):
        z = 2 * lax.rem(duo + away, halves) + {1: 0, 2: 1 - odd, 3: 1}[away]
        j = {1: 2 - odd, 2: 3, 3: 1 + odd}[away]
        return pltpu.make_async_remote_copy(
            src_ref=tx.at[part(h), pl.ds((2 * groups + 3 * q + away - 1) * rows, rows), :],
            dst_ref=coming.at[j - 1, part(h), pl.ds(g_me * rows, rows), :],
            send_sem=s2_sem.at[h],
            recv_sem=rz_sem.at[h, j - 1],
            device_id={"lat": q * RING + z},
            device_id_type=MESH,
        )

    def owner(h):
        rx[part(h), own, :] = zon[my_v, part(h), pl.ds(my_lev * rows, rows), :]
        drain(rx, h, 5 * groups - 1, r1_sem.at[h])
        everything = jnp.concatenate([rx[c] for c in columns(h)], axis=1)
        result = joined(own_mat[...], right(split(everything)))
        for k, c in enumerate(columns(h)):
            tx[c] = result[:, k * BLK : (k + 1) * BLK]
        for away in (2, 1, 3):

            @pl.loop(0, groups)
            def _(k):
                reply_state(away, lax.rem(g_me + k, groups), h).start()

    def reply_rows(h):
        @pl.loop(0, groups)
        def _(k):
            reply_raw(1 - odd, lax.rem(g_me + k, groups), h).start()

        @pl.loop(1, groups)
        def _(k):
            reply_raw(odd, lax.rem(g_me + k, groups), h).start()

        back[part(h), slot, :] = tx[part(h), own, :]

    def pair_back(j, h):
        w = lead(j)
        return pltpu.make_async_remote_copy(
            src_ref=pair_out.at[j - 1, part(h)],
            dst_ref=back.at[part(h), pl.ds(lax.rem(w, 2) * lev * rows + row_of_set(w), block), :],
            send_sem=so_sem.at[h, j - 1],
            recv_sem=ro_sem.at[h, j - 1],
            device_id={"lat": g_me * RING + mate},
            device_id_type=MESH,
        )

    def finish(h, which=(1, 2, 3)):
        for j in which:
            view = coming.at[j - 1, part(h)]
            pltpu.make_async_copy(view, view, rz_sem.at[h, j - 1]).wait()
            coefficients = jnp.concatenate([coming[j - 1, c] for c in columns(h)], axis=1)
            inputs = jnp.concatenate(both_tiles(j, h) + [coefficients], axis=0)
            finished = joined(up_mat[j - 1], right(split(inputs)))
            for k, c in enumerate(columns(h)):
                pair_out[j - 1, c] = finished[block:, k * BLK : (k + 1) * BLK]
            pair_back(j, h).start()
            w = lead(j)
            at = pl.ds(lax.rem(w, 2) * lev * rows + row_of_set(w), block)
            for k, c in enumerate(columns(h)):
                back[c, at, :] = finished[:block, k * BLK : (k + 1) * BLK]

    def store(v, h):
        at = pl.ds(PARTS[h][0] * BLK, (PARTS[h][1] - PARTS[h][0]) * BLK)
        return pltpu.make_async_copy(out_ref.at[v, :, :, at], out_hbm.at[v, :, :, at], out_sem.at[h, v])

    def mix(h):
        weights = [left(split(vert_ref[v])) for v in range(nv)]
        first_lane, last_lane = PARTS[h][0] * BLK, PARTS[h][1] * BLK
        drain(back, h, 2 * groups - 1, r2_sem.at[h])
        for j in (1, 2, 3):
            pair_back(j, h).wait_recv()
        for v in range(nv):

            @pl.loop(0, rows)
            def _(t):
                levels = jnp.concatenate(
                    [back[c, pl.ds(v * lev * rows + t, lev, stride=rows), :] for c in columns(h)], axis=1
                )
                scaling = jnp.concatenate([column[v, t]] * len(columns(h)), axis=1)
                out_ref[v, t, :, first_lane:last_lane] = (
                    joined(weights[v], right(split(levels))) * scaling
                )

            store(v, h).start()

    tasks = dict(P=send_pairs, R=send_raw, m=merge, o=owner, q=reply_rows, f=finish, x=mix)
    loads[3].wait()
    for task in ORDER.split():
        if task == "B":
            build()
        elif len(task) == 3:
            tasks[task[0]](int(task[1]), (int(task[2]),))
        else:
            tasks[task[0]](int(task[1]))

    for h in range(parts):
        drain(tx, h, 5 * groups - 1, s1_sem.at[h])
        drain(tx, h, 5 * groups - 1, s2_sem.at[h])
        for j in (1, 2, 3):
            pair_copy(j, h).wait_send()
            pair_back(j, h).wait_send()
        for v in range(nv):
            store(v, h).wait()


def per_device(n_lon, n_lat, increment, spread, lon_scale, lat_scale, vertical):
    nv, rows, lev, width = increment.shape
    blocks = width // BLK
    poles = nv * rows
    block = n_lat // RING * rows
    group = min(4, rows)
    hbm = pl.BlockSpec(memory_space=pltpu.MemorySpace.HBM)
    return pl.pallas_call(
        functools.partial(kernel, n_lon, n_lat),
        out_shape=jax.ShapeDtypeStruct(increment.shape, F32),
        in_specs=[hbm] * 5,
        out_specs=hbm,
        scratch_shapes=[
            pltpu.SMEM((nv, rows), F32),
            pltpu.SMEM((nv, lev), F32),
            pltpu.VMEM(increment.shape, F32),
            pltpu.VMEM((nv, rows, lev), F32),
            pltpu.VMEM((nv, lev, lev), F32),
            pltpu.VMEM(increment.shape, F32),
            pltpu.VMEM((5, poles, BLK), F32),
            pltpu.VMEM((nv, rows, lev, BLK), F32),
            pltpu.VMEM((nv, rows, blocks * lev, BLK), F32),
            pltpu.VMEM((nv, rows, 2, 8 * (blocks + n_lon - 1), width), BF16),
            pltpu.VMEM((nv, rows, 8 * blocks, lev), F32),
            pltpu.VMEM((nv, rows // group, 8, group * lev), F32),
            pltpu.VMEM((nv, n_lon - 1, rows // group, 8, group * lev), F32),
            pltpu.VMEM((nv, blocks, lev * rows, BLK), F32),
            pltpu.VMEM((3, blocks, block, BLK), F32),
            pltpu.VMEM((3, blocks, block, BLK), F32),
            pltpu.VMEM((blocks, 5 * block, BLK), F32),
            pltpu.VMEM((blocks, 5 * block, BLK), F32),
            pltpu.VMEM((3, blocks, block, BLK), F32),
            pltpu.VMEM((3, blocks, block, BLK), F32),
            pltpu.VMEM((blocks, nv * lev * rows, BLK), F32),
            pltpu.VMEM((3, block, 6 * block), BF16),
            pltpu.VMEM((3, 2 * block, 9 * block), BF16),
            pltpu.VMEM((4 * block, 4 * block), F32),
            pltpu.VMEM((4 * block, 4 * block), F32),
            pltpu.VMEM((5 * block, 15 * block), BF16),
            pltpu.SemaphoreType.DMA((4 + nv,)),
            pltpu.SemaphoreType.DMA((len(PARTS), nv)),
            pltpu.SemaphoreType.DMA((nv, n_lon - 1)),
            pltpu.SemaphoreType.DMA((nv, n_lon - 1)),
            pltpu.SemaphoreType.DMA((len(PARTS), 3)),
            pltpu.SemaphoreType.DMA((len(PARTS), 3)),
            pltpu.SemaphoreType.DMA((len(PARTS),)),
            pltpu.SemaphoreType.DMA((len(PARTS),)),
            pltpu.SemaphoreType.DMA((len(PARTS),)),
            pltpu.SemaphoreType.DMA((len(PARTS),)),
            pltpu.SemaphoreType.DMA((len(PARTS), 3)),
            pltpu.SemaphoreType.DMA((len(PARTS), 3)),
            pltpu.SemaphoreType.DMA((len(PARTS), 3)),
        ],
        compiler_params=pltpu.CompilerParams(
            collective_id=0, has_side_effects=True, vmem_limit_bytes=60 * 1024 * 1024
        ),
    )(lon_scale, lat_scale, increment, spread, vertical)


def solution(mesh):
    in_specs = (P(None, "lat", None, "lon"), P(None, "lat", None), P(None, "lat"), P(), P())
    out_specs = P(None, "lat", None, "lon")
    body = functools.partial(per_device, mesh.shape["lon"], mesh.shape["lat"])
    return jax.shard_map(body, mesh=mesh, in_specs=in_specs, out_specs=out_specs, check_vma=False)
```

```python
import functools
import math

import jax
import jax.numpy as jnp
from jax import lax
from jax.experimental import pallas as pl
from jax.experimental.pallas import tpu as pltpu
from jax.sharding import PartitionSpec as P

MESH = pl.DeviceIdType.MESH
BLK = 128
PARTS = ((0, 2), (2, 4))
RING = 8
F32 = jnp.float32
BF16 = jnp.bfloat16


def split(a):
    high = a.astype(BF16)
    return high, (a - high.astype(F32)).astype(BF16)


def left(pair, dim=1):
    high, low = pair
    return jnp.concatenate([high, high, low], axis=dim)


def right(pair, dim=0):
    high, low = pair
    return jnp.concatenate([high, low, high], axis=dim)


def joined(a, b, dims=((1,), (0,))):
    return lax.dot_general(a, b, (dims, ((), ())), preferred_element_type=F32)


def dot3(a, b, dims=((1,), (0,))):
    return joined(left(a, dims[0][0]), right(b, dims[1][0]), dims)


def pole_terms(scale):
    x = 1.0 / scale
    t = jnp.ones_like(x)
    for k in range(10, 1, -1):
        t = 1.0 - x * (1.0 / k) * t
    pole = 1.0 - x * t
    gain = 1.0 - pole
    s = gain / (2.0 - gain)
    s2 = s * s
    series = 1.0 / 3 + s2 * (1.0 / 5 + s2 * (1.0 / 7 + s2 * (1.0 / 9 + s2 * (1.0 / 11))))
    log_pole = -2.0 * s * (1.0 + s2 * series)
    norm = jnp.sqrt((2.0 * math.sqrt(math.pi)) * jnp.sqrt(8.0 * pole) / gain)
    return gain, pole, log_pole, norm


def circle_terms(scale, laps):
    gain, pole, log_pole, norm = pole_terms(scale)
    q = pole * pole
    r = 1.0 / (1.0 + pole)
    r2 = r * r
    r4 = r2 * r2
    p3 = r4
    p2 = (3.0 + q) * r4 * r
    p1 = (3.0 + 6.0 * q + q * q) * r4 * r2
    p0 = (1.0 + 9.0 * q + 9.0 * q * q + q * q * q) * r4 * r2 * r
    u = gain * BLK
    c0 = gain * p0
    c1 = gain * u * (p1 - 0.5 * p2 * gain + p3 * gain * gain * (1.0 / 3))
    c2 = gain * u * u * (0.5 * p2 - 0.5 * p3 * gain)
    c3 = gain * u * u * u * p3 * (1.0 / 6)
    lam = BLK * log_pole
    beta = jnp.exp(laps * lam)
    b0 = 1.0 / (1.0 - beta)
    b1 = beta * b0 * b0
    b2 = b1 * b0 * (1.0 + beta)
    b3 = b1 * b0 * b0 * (1.0 + beta * (4.0 + beta))
    n = float(laps)
    e3 = c3 * b0
    e2 = c2 * b0 + 3.0 * n * c3 * b1
    e1 = c1 * b0 + 2.0 * n * c2 * b1 + 3.0 * n * n * c3 * b2
    e0 = c0 * b0 + n * c1 * b1 + n * n * c2 * b2 + n * n * n * c3 * b3
    return [lam, e0 * norm, e1 * norm, e2 * norm, e3 * norm]


def line_terms(scale, run):
    gain, pole, log_pole, norm = pole_terms(scale)
    g2 = gain * gain
    g4 = g2 * g2
    cubic = [g4, g4 * (11.0 / 6 * run), g4 * float(run**2), g4 * (1.0 / 6 * run**3)]
    return run * log_pole, cubic, norm


def kernel(
    n_lon, n_lat,
    lon_hbm, lat_hbm, inc_hbm, spread_hbm, vert_hbm, out_hbm,
    lon_scale, lat_scale, inc_ref, spread_ref, vert_ref, out_ref,
    coef, column, inside, tables, local_mom, mom_send, mom_recv, zon,
    pair_raw, merged, rx, tx, coming, pair_out, back,
    down_mat, up_mat, runs, turns, own_mat,
    in_sem, out_sem, ms_sem, mr_sem, ps_sem, pr_sem, s1_sem, r1_sem, s2_sem, r2_sem, rz_sem, so_sem, ro_sem,
):
    nv, rows, lev, width = inc_ref.shape
    blocks = width // BLK
    laps = blocks * n_lon
    poles = nv * rows
    group = min(4, rows)
    me_lon = lax.axis_index("lon")
    me = lax.axis_index("lat")
    groups = n_lat // RING
    halves = RING // 2
    block = groups * rows
    g_me, z_me = me // RING, lax.rem(me, RING)
    duo, odd = z_me // 2, lax.rem(z_me, 2)
    side = 2 * odd - 1
    mate = z_me - side
    my_v, my_lev = odd, duo * groups + g_me

    loads = [
        pltpu.make_async_copy(lon_hbm, lon_scale, in_sem.at[0]),
        pltpu.make_async_copy(spread_hbm, spread_ref, in_sem.at[1]),
        pltpu.make_async_copy(lat_hbm, lat_scale, in_sem.at[2]),
        pltpu.make_async_copy(vert_hbm, vert_ref, in_sem.at[3]),
    ]
    fields = [pltpu.make_async_copy(inc_hbm.at[v], inc_ref.at[v], in_sem.at[4 + v]) for v in range(nv)]
    for load in loads[:2] + fields + loads[2:]:
        load.start()

    barrier = pltpu.get_barrier_semaphore()

    for s in range(1, n_lon):
        pl.semaphore_signal(
            barrier, inc=1, device_id={"lon": lax.rem(me_lon + s, n_lon)}, device_id_type=MESH
        )

    greeted = (0, -1, 1, 2, 3, -2)
    for off in greeted:
        z = lax.rem(z_me + side * off + RING, RING)

        @pl.loop(0 if off else 1, groups)
        def _(k):
            d = lax.rem(g_me + k, groups) * RING + z
            pl.semaphore_signal(barrier, inc=1, device_id={"lat": d}, device_id_type=MESH)

    loads[0].wait()
    loads[1].wait()
    row_of = lax.broadcasted_iota(jnp.int32, (poles, BLK), 0)
    scale = jnp.zeros((poles, BLK), F32)
    for v in range(nv):
        for t in range(rows):
            scale = jnp.where(row_of == v * rows + t, lon_scale[v, t], scale)
    for k, part in enumerate(circle_terms(scale, laps)):
        coef[k] = part
    eye = lax.broadcasted_iota(jnp.int32, (lev, lev), 0) == lax.broadcasted_iota(jnp.int32, (lev, lev), 1)
    for v in range(nv):
        for t in range(rows):
            line = jnp.broadcast_to(spread_ref[v, t : t + 1, :], (lev, lev))
            one = jnp.sum(jnp.where(eye, line, 0.0), axis=1, keepdims=True)
            column[v, t] = jnp.broadcast_to(one, (lev, BLK))

    def tile(shape, dim):
        return lax.broadcasted_iota(jnp.int32, shape, dim)

    lane8 = tile((8, BLK), 1).astype(F32) * (1.0 / BLK)
    order = tile((8, BLK), 0)
    ahead = order < 4
    rank = lax.rem(order, 4)
    to_end = 1.0 - lane8
    to_start = lane8 + 1.0 / BLK
    behind = lane8
    before = (BLK - 1.0) / BLK - lane8

    def power(tau):
        t2 = tau * tau
        return jnp.where(rank == 0, 1.0, jnp.where(rank == 1, tau, jnp.where(rank == 2, t2, t2 * tau)))

    def coefs(r):
        return [coef[k, pl.ds(r, 1), :] for k in range(5)]

    def wide_column(v, t):
        one = column[v, t]
        return jnp.concatenate([one] * blocks, axis=1)

    def first(v, g):
        pieces = []
        for u in range(group):
            t = g * group + u
            lam = coefs(v * rows + t)[0]
            x = inc_ref[v, t] * wide_column(v, t)
            inc_ref[v, t] = x
            tau = jnp.where(ahead, to_end, to_start)
            small = jnp.exp(lam * tau) * power(tau)
            nothing = jnp.zeros((8, BLK), F32)
            lines = []
            for c in range(blocks):
                lines.append(jnp.concatenate([small if d == c else nothing for d in range(blocks)], axis=1))
            whole = []
            for c in range(blocks):
                shifted = jnp.where(ahead, to_end + float(blocks - 1 - c), to_start + float(c))
                whole.append(jnp.exp(lam * shifted) * power(shifted))
            lines.append(jnp.concatenate(whole, axis=1))
            basis = jnp.concatenate(lines, axis=0)
            moments = dot3(split(basis), split(x), ((1,), (1,)))
            local_mom[v, t] = moments[: 8 * blocks]
            pieces.append(moments[8 * blocks :])
        mom_send[v, g] = jnp.concatenate(pieces, axis=1)

    def table_of(v, t, lam, e0, e1, e2, e3):
        def mixed(a0, a1, a2, a3):
            return jnp.where(rank == 0, a0, jnp.where(rank == 1, a1, jnp.where(rank == 2, a2, a3)))

        q0 = mixed(e0, e1, e2, e3)
        q1 = mixed(e1, 2.0 * e2, 3.0 * e3, 0.0)
        q2 = mixed(e2, 3.0 * e3, 0.0, 0.0)
        q3 = mixed(e3, 0.0, 0.0, 0.0)

        def reach(y):
            return jnp.exp(lam * y) * (q0 + y * (q1 + y * (q2 + y * q3)))

        by_gap = {}
        for gap in list(range(1, blocks)) + list(range(laps - blocks + 1, laps)):
            by_gap[gap] = reach(jnp.where(ahead, behind + float(gap - 1), before + float(laps - gap - 1)))
        nothing = jnp.zeros((8, BLK), F32)
        lines = []
        for c in range(blocks):
            lines.append(
                jnp.concatenate(
                    [nothing if d == c else by_gap[(d - c) % laps] for d in range(blocks)], axis=1
                )
            )
        for s in range(1, n_lon):
            line = []
            for d in range(blocks):
                line.append(
                    reach(
                        jnp.where(
                            ahead,
                            behind + float(d + blocks * (s - 1)),
                            before + float(blocks - 1 - d + blocks * (n_lon - 1 - s)),
                        )
                    )
                )
            lines.append(jnp.concatenate(line, axis=1))
        high, low = split(jnp.concatenate(lines, axis=0))
        tables[v, t, 0] = high
        tables[v, t, 1] = low

    def middle(v, g):
        for u in range(group):
            t = g * group + u
            lam, e0, e1, e2, e3 = coefs(v * rows + t)
            x = inc_ref[v, t]
            stacked = jnp.concatenate([x[:, c * BLK : (c + 1) * BLK] for c in range(blocks)], axis=0)
            gap = jnp.abs(tile((BLK, BLK), 0) - tile((BLK, BLK), 1)).astype(F32) * (1.0 / BLK)
            far = float(laps) - gap
            near = jnp.exp(lam * gap) * (e0 + gap * (e1 + gap * (e2 + gap * e3)))
            around = jnp.exp(lam * far) * (e0 + far * (e1 + far * (e2 + far * e3)))
            inside[v, t] = dot3(split(stacked), split(near + around))
            table_of(v, t, lam, e0, e1, e2, e3)

    def moment_copy(v, s):
        return pltpu.make_async_remote_copy(
            src_ref=mom_send.at[v],
            dst_ref=mom_recv.at[v, s - 1],
            send_sem=ms_sem.at[v, s - 1],
            recv_sem=mr_sem.at[v, s - 1],
            device_id={"lon": lax.rem(me_lon + s, n_lon)},
            device_id_type=MESH,
        )

    for v in range(nv):
        fields[v].wait()

        @pl.loop(0, rows // group)
        def _(g):
            first(v, g)

        if v == 0:
            pl.semaphore_wait(barrier, len(greeted) * groups - 1 + n_lon - 1)
        for s in range(1, n_lon):
            moment_copy(v, s).start()

    def second(v, g):
        for u in range(group):
            t = g * group + u
            sources = [local_mom[v, t]]
            for s in range(1, n_lon):
                sources.append(mom_recv[v, s - 1, g][:, u * lev : (u + 1) * lev])
            moments = jnp.concatenate(sources, axis=0)
            added = dot3(split(moments.T), (tables[v, t, 0], tables[v, t, 1]))
            own = inside[v, t]
            own = jnp.concatenate([own[c * lev : (c + 1) * lev] for c in range(blocks)], axis=1)
            total = own + added
            for c in range(blocks):
                zon[v, c, pl.ds(t, lev, stride=rows), :] = total[:, c * BLK : (c + 1) * BLK]

    parts = len(PARTS)
    run = 2 * rows

    def part(h):
        return pl.ds(PARTS[h][0], PARTS[h][1] - PARTS[h][0])

    def columns(h):
        return range(*PARTS[h])

    def row_of_set(w):
        return (w // 2) * block

    def lead(j):
        return lax.rem(z_me + side * j + RING, RING)

    def mate_lead(j):
        return lax.rem(z_me - side * (j + 1) + RING, RING)

    def spot(shape, dim, swap):
        at = tile(shape, dim)
        return lax.rem(at, rows) + rows * jnp.abs(at // block - swap)

    def pair_of(shape, dim):
        return lax.rem(tile(shape, dim), block) // rows

    def graded(tau, kind):
        t2 = tau * tau
        return jnp.where(kind == 0, 1.0, jnp.where(kind == 1, tau, jnp.where(kind == 2, t2, t2 * tau)))

    def set_matrices(lam, cubic, norm, swap):
        unit = 1.0 / run
        shape = (block, 2 * block)
        kind = lax.rem(tile(shape, 0), rows)
        pos = spot(shape, 1, swap).astype(F32)
        tau = jnp.where(kind < 4, run - pos, pos + 1.0) * unit
        same = pair_of(shape, 0) == pair_of(shape, 1)
        basis = jnp.where(same, jnp.exp(lam * tau) * graded(tau, lax.rem(kind, 4)), 0.0)
        shape = (2 * block, 2 * block)
        away = spot(shape, 0, swap) - spot(shape, 1, swap)
        gap = jnp.abs(away).astype(F32) * unit
        same = pair_of(shape, 0) == pair_of(shape, 1)
        value = cubic[0] + gap * (cubic[1] + gap * (cubic[2] + gap * cubic[3]))
        value = jnp.where(same, jnp.exp(lam * gap) * value, 0.0)
        ahead_of = split(jnp.where(away >= 0, value, 0.0))
        behind_of = split(jnp.where(away <= 0, value, 0.0) * norm)
        down = jnp.where(kind < 4, basis, dot3(split(basis), ahead_of))
        near = dot3(behind_of, ahead_of)
        shape = (2 * block, block)
        kind = lax.rem(tile(shape, 1), rows)
        pos = spot(shape, 0, swap).astype(F32)
        tau = jnp.where(kind < 4, pos, run - 1.0 - pos) * unit
        same = pair_of(shape, 0) == pair_of(shape, 1)
        basis = jnp.where(same, jnp.exp(lam[:, :block] * tau) * graded(tau, lax.rem(kind, 4)), 0.0)
        up = jnp.where(kind < 4, dot3(behind_of, split(basis)), basis * norm[:, :block])
        return down, near, up

    loads[2].wait()

    @pl.loop(1, 4)
    def _(j):
        w = lead(j)
        which = pair_of((8, 2 * block), 1)
        scales = jnp.ones((8, 2 * block), F32)
        for q in range(groups):
            scales = jnp.where(which == q, lat_scale[lax.rem(w, 2), (w // 2) * groups + q], scales)
        lam, cubic, norm = line_terms(scales, run)
        down, near, up = set_matrices(lam[:1], [p[:1] for p in cubic], norm[:1], odd)
        down_mat[j - 1] = left(split(down))
        up_mat[j - 1] = left(split(jnp.concatenate([near, up], axis=1)))

    for v in range(nv):

        @pl.loop(0, rows // group)
        def _(g):
            middle(v, g)

    for v in range(nv):
        for s in range(1, n_lon):
            moment_copy(v, s).wait()

        @pl.loop(0, rows // group)
        def _(g):
            second(v, g)

    def pair_copy(j, h):
        w = mate_lead(j)
        return pltpu.make_async_remote_copy(
            src_ref=zon.at[lax.rem(w, 2), part(h), pl.ds(row_of_set(w), block), :],
            dst_ref=pair_raw.at[j - 1, part(h)],
            send_sem=ps_sem.at[h, j - 1],
            recv_sem=pr_sem.at[h, j - 1],
            device_id={"lat": g_me * RING + mate},
            device_id_type=MESH,
        )

    def raw_copy(w, q, h):
        return pltpu.make_async_remote_copy(
            src_ref=zon.at[lax.rem(w, 2), part(h), pl.ds(row_of_set(w) + q * rows, rows), :],
            dst_ref=rx.at[part(h), pl.ds((odd * groups + g_me) * rows, rows), :],
            send_sem=s1_sem.at[h],
            recv_sem=r1_sem.at[h],
            device_id={"lat": q * RING + w},
            device_id_type=MESH,
        )

    def merged_copy(j, q, h):
        w = lead(j)
        away = lax.rem(duo - w // 2 + halves, halves)
        return pltpu.make_async_remote_copy(
            src_ref=merged.at[j - 1, part(h), pl.ds(q * rows, rows), :],
            dst_ref=rx.at[part(h), pl.ds((2 * groups + 3 * g_me + away - 1) * rows, rows), :],
            send_sem=s1_sem.at[h],
            recv_sem=r1_sem.at[h],
            device_id={"lat": q * RING + w},
            device_id_type=MESH,
        )

    def send_pairs(h):
        for j in (3, 2, 1):
            pair_copy(j, h).start()

    def send_raw(h):
        @pl.loop(0, groups)
        def _(k):
            raw_copy(mate, lax.rem(g_me + k, groups), h).start()

        @pl.loop(1, groups)
        def _(k):
            raw_copy(z_me, lax.rem(g_me + k, groups), h).start()

    def both_tiles(j, h):
        w = lead(j)
        at = pl.ds(row_of_set(w), block)
        mine = jnp.concatenate([zon[lax.rem(w, 2), c, at, :] for c in columns(h)], axis=1)
        other = jnp.concatenate([pair_raw[j - 1, c] for c in columns(h)], axis=1)
        return [mine, other]

    def merge(h):
        for j in (3, 2, 1):
            pair_copy(j, h).wait_recv()
            tiles = jnp.concatenate(both_tiles(j, h), axis=0)
            moments = joined(down_mat[j - 1], right(split(tiles)))
            for k, c in enumerate(columns(h)):
                merged[j - 1, c] = moments[:, k * BLK : (k + 1) * BLK]

            @pl.loop(0, groups)
            def _(k):
                merged_copy(j, lax.rem(g_me + k, groups), h).start()

    def build():
        shape = (8, 2 * block)
        own_scale = jnp.full(shape, lat_scale[my_v, my_lev], F32)
        lam, cubic, norm = line_terms(own_scale, run)
        down, near, up = set_matrices(lam[:1], [p[:1] for p in cubic], norm[:1], 0)
        lam = lam[:, :1]
        cubic = [p[:, :1] for p in cubic]
        count = halves * groups
        states = 8 * count
        lane_slot = tile((8, states), 1) // 8
        lane_kind = lax.rem(tile((8, states), 1), 8)
        row_kind = tile((8, states), 0)

        def run_of(slot):
            other = slot - groups
            q = jnp.where(slot < groups, slot, other // 3)
            away = jnp.where(slot < groups, 0, lax.rem(other, 3) + 1)
            return q * halves + lax.rem(duo + away, halves)

        lane_run = jnp.zeros((8, states), F32)
        for n in range(count):
            q, away = (n, 0) if n < groups else ((n - groups) // 3, (n - groups) % 3 + 1)
            place = q * halves + lax.rem(duo + away, halves)
            lane_run = jnp.where(lane_slot == n, place.astype(F32), lane_run)
        a, b = lax.rem(row_kind, 4), lax.rem(lane_kind, 4)
        m = a + b
        mf = m.astype(F32)
        choose = jnp.where(m == 2, jnp.where(a == 1, 2.0, 1.0), jnp.where(m == 3, jnp.where((a == 1) | (a == 2), 3.0, 1.0), 1.0))

        def pick(shift):
            total = jnp.zeros((8, states), F32)
            for n in range(4 - shift):
                total = jnp.where(m == n, cubic[n + shift], total)
            return total * choose

        taylor = [pick(0), pick(1) * (mf + 1.0), pick(2) * ((mf + 1.0) * (mf + 2.0) * 0.5), pick(3)]
        turn = jnp.zeros((8, states), F32)
        for n in range(run):
            power_of = graded((n + 1.0) / run, a) * graded(n / run, b)
            turn = turn + jnp.exp(lam * ((2.0 * n + 1.0) / run)) * power_of
        turn = jnp.where((row_kind >= 4) & (lane_kind < 4), turn, 0.0)

        @pl.loop(0, count)
        def _(slot):
            here = run_of(slot).astype(F32)
            step = jnp.where(row_kind < 4, here - lane_run, lane_run - here) - 1.0
            live = ((row_kind < 4) == (lane_kind < 4)) & (step >= 0.0)
            reach = jnp.maximum(step, 0.0)
            value = taylor[0] + reach * (taylor[1] + reach * (taylor[2] + reach * taylor[3]))
            at = pl.ds(pl.multiple_of(slot * 8, 8), 8)
            runs[at, :] = jnp.where(live, jnp.exp(lam * reach) * value, 0.0)
            turns[at, :] = jnp.where(lane_slot == slot, turn, 0.0)

        down, up = split(down), split(up)
        steps = split(runs[...])
        turned = dot3(split(turns[...]), steps)
        whole = runs[...] + dot3(steps, split(turned))
        inner = dot3(split(whole[:, :block]), down)
        top = dot3(up, split(jnp.concatenate([inner[:block], whole[:block, block:]], axis=1)))
        top = jnp.concatenate([top[:, : 2 * block] + near, top[:, 2 * block :]], axis=1)
        bottom = jnp.concatenate([inner[block:], whole[block:, block:]], axis=1)
        own_mat[: 2 * block, :] = left(split(top))
        own_mat[2 * block :, :] = left(split(bottom))

    def drain(ref, h, count, sem):
        view = ref.at[part(h), pl.ds(0, count * rows), :]
        pltpu.make_async_copy(view, view, sem).wait()

    slot = pl.ds((my_v * lev + my_lev) * rows, rows)
    own = pl.ds((odd * groups + g_me) * rows, rows)

    def reply_raw(e, q, h):
        return pltpu.make_async_remote_copy(
            src_ref=tx.at[part(h), pl.ds((e * groups + q) * rows, rows), :],
            dst_ref=back.at[part(h), slot, :],
            send_sem=s2_sem.at[h],
            recv_sem=r2_sem.at[h],
            device_id={"lat": q * RING + 2 * duo + e},
            device_id_type=MESH,
        )

    def reply_state(away, q, h):
        z = 2 * lax.rem(duo + away, halves) + {1: 0, 2: 1 - odd, 3: 1}[away]
        j = {1: 2 - odd, 2: 3, 3: 1 + odd}[away]
        return pltpu.make_async_remote_copy(
            src_ref=tx.at[part(h), pl.ds((2 * groups + 3 * q + away - 1) * rows, rows), :],
            dst_ref=coming.at[j - 1, part(h), pl.ds(g_me * rows, rows), :],
            send_sem=s2_sem.at[h],
            recv_sem=rz_sem.at[h, j - 1],
            device_id={"lat": q * RING + z},
            device_id_type=MESH,
        )

    def owner(h):
        rx[part(h), own, :] = zon[my_v, part(h), pl.ds(my_lev * rows, rows), :]
        drain(rx, h, 5 * groups - 1, r1_sem.at[h])
        everything = jnp.concatenate([rx[c] for c in columns(h)], axis=1)
        result = joined(own_mat[...], right(split(everything)))
        for k, c in enumerate(columns(h)):
            tx[c] = result[:, k * BLK : (k + 1) * BLK]
        for away in (2, 1, 3):

            @pl.loop(0, groups)
            def _(k):
                reply_state(away, lax.rem(g_me + k, groups), h).start()

    def reply_rows(h):
        @pl.loop(0, groups)
        def _(k):
            reply_raw(1 - odd, lax.rem(g_me + k, groups), h).start()

        @pl.loop(1, groups)
        def _(k):
            reply_raw(odd, lax.rem(g_me + k, groups), h).start()

        back[part(h), slot, :] = tx[part(h), own, :]

    def pair_back(j, h):
        w = lead(j)
        return pltpu.make_async_remote_copy(
            src_ref=pair_out.at[j - 1, part(h)],
            dst_ref=back.at[part(h), pl.ds(lax.rem(w, 2) * lev * rows + row_of_set(w), block), :],
            send_sem=so_sem.at[h, j - 1],
            recv_sem=ro_sem.at[h, j - 1],
            device_id={"lat": g_me * RING + mate},
            device_id_type=MESH,
        )

    def finish(h):
        for j in (1, 3, 2):
            view = coming.at[j - 1, part(h)]
            pltpu.make_async_copy(view, view, rz_sem.at[h, j - 1]).wait()
            coefficients = jnp.concatenate([coming[j - 1, c] for c in columns(h)], axis=1)
            inputs = jnp.concatenate(both_tiles(j, h) + [coefficients], axis=0)
            finished = joined(up_mat[j - 1], right(split(inputs)))
            for k, c in enumerate(columns(h)):
                pair_out[j - 1, c] = finished[block:, k * BLK : (k + 1) * BLK]
            pair_back(j, h).start()
            w = lead(j)
            at = pl.ds(lax.rem(w, 2) * lev * rows + row_of_set(w), block)
            for k, c in enumerate(columns(h)):
                back[c, at, :] = finished[:block, k * BLK : (k + 1) * BLK]

    def store(v, h):
        at = pl.ds(PARTS[h][0] * BLK, (PARTS[h][1] - PARTS[h][0]) * BLK)
        return pltpu.make_async_copy(out_ref.at[v, :, :, at], out_hbm.at[v, :, :, at], out_sem.at[h, v])

    def mix(h):
        first_lane, last_lane = PARTS[h][0] * BLK, PARTS[h][1] * BLK
        drain(back, h, 2 * groups - 1, r2_sem.at[h])
        for v, expected in ((odd, (1, 3)), (1 - odd, (2,))):
            for j in expected:
                pair_back(j, h).wait_recv()
            weights = left(split(vert_ref[v]))
            for t in range(rows):
                levels = jnp.concatenate(
                    [back[c, pl.ds(v * (lev * rows) + t, lev, stride=rows), :] for c in columns(h)], axis=1
                )
                scaling = jnp.concatenate([column[v, t]] * len(columns(h)), axis=1)
                out_ref[v, t, :, first_lane:last_lane] = joined(weights, right(split(levels))) * scaling
            store(v, h).start()

    loads[3].wait()
    send_pairs(0)
    send_raw(0)
    merge(0)
    send_pairs(1)
    send_raw(1)
    build()
    merge(1)
    for h in range(parts):
        owner(h)
        reply_rows(h)
    for h in range(parts):
        finish(h)
    for h in range(parts):
        mix(h)

    for h in range(parts):
        drain(tx, h, 5 * groups - 1, s1_sem.at[h])
        drain(tx, h, 5 * groups - 1, s2_sem.at[h])
        for j in (1, 2, 3):
            pair_copy(j, h).wait_send()
            pair_back(j, h).wait_send()
        for v in range(nv):
            store(v, h).wait()


def per_device(n_lon, n_lat, increment, spread, lon_scale, lat_scale, vertical):
    nv, rows, lev, width = increment.shape
    blocks = width // BLK
    poles = nv * rows
    block = n_lat // RING * rows
    group = min(4, rows)
    hbm = pl.BlockSpec(memory_space=pltpu.MemorySpace.HBM)
    return pl.pallas_call(
        functools.partial(kernel, n_lon, n_lat),
        out_shape=jax.ShapeDtypeStruct(increment.shape, F32),
        in_specs=[hbm] * 5,
        out_specs=hbm,
        scratch_shapes=[
            pltpu.SMEM((nv, rows), F32),
            pltpu.SMEM((nv, lev), F32),
            pltpu.VMEM(increment.shape, F32),
            pltpu.VMEM((nv, rows, lev), F32),
            pltpu.VMEM((nv, lev, lev), F32),
            pltpu.VMEM(increment.shape, F32),
            pltpu.VMEM((5, poles, BLK), F32),
            pltpu.VMEM((nv, rows, lev, BLK), F32),
            pltpu.VMEM((nv, rows, blocks * lev, BLK), F32),
            pltpu.VMEM((nv, rows, 2, 8 * (blocks + n_lon - 1), width), BF16),
            pltpu.VMEM((nv, rows, 8 * blocks, lev), F32),
            pltpu.VMEM((nv, rows // group, 8, group * lev), F32),
            pltpu.VMEM((nv, n_lon - 1, rows // group, 8, group * lev), F32),
            pltpu.VMEM((nv, blocks, lev * rows, BLK), F32),
            pltpu.VMEM((3, blocks, block, BLK), F32),
            pltpu.VMEM((3, blocks, block, BLK), F32),
            pltpu.VMEM((blocks, 5 * block, BLK), F32),
            pltpu.VMEM((blocks, 5 * block, BLK), F32),
            pltpu.VMEM((3, blocks, block, BLK), F32),
            pltpu.VMEM((3, blocks, block, BLK), F32),
            pltpu.VMEM((blocks, nv * lev * rows, BLK), F32),
            pltpu.VMEM((3, block, 6 * block), BF16),
            pltpu.VMEM((3, 2 * block, 9 * block), BF16),
            pltpu.VMEM((4 * block, 4 * block), F32),
            pltpu.VMEM((4 * block, 4 * block), F32),
            pltpu.VMEM((5 * block, 15 * block), BF16),
            pltpu.SemaphoreType.DMA((4 + nv,)),
            pltpu.SemaphoreType.DMA((len(PARTS), nv)),
            pltpu.SemaphoreType.DMA((nv, n_lon - 1)),
            pltpu.SemaphoreType.DMA((nv, n_lon - 1)),
            pltpu.SemaphoreType.DMA((len(PARTS), 3)),
            pltpu.SemaphoreType.DMA((len(PARTS), 3)),
            pltpu.SemaphoreType.DMA((len(PARTS),)),
            pltpu.SemaphoreType.DMA((len(PARTS),)),
            pltpu.SemaphoreType.DMA((len(PARTS),)),
            pltpu.SemaphoreType.DMA((len(PARTS),)),
            pltpu.SemaphoreType.DMA((len(PARTS), 3)),
            pltpu.SemaphoreType.DMA((len(PARTS), 3)),
            pltpu.SemaphoreType.DMA((len(PARTS), 3)),
        ],
        compiler_params=pltpu.CompilerParams(
            collective_id=0, has_side_effects=True, vmem_limit_bytes=60 * 1024 * 1024
        ),
    )(lon_scale, lat_scale, increment, spread, vertical)


def solution(mesh):
    in_specs = (P(None, "lat", None, "lon"), P(None, "lat", None), P(None, "lat"), P(), P())
    out_specs = P(None, "lat", None, "lon")
    body = functools.partial(per_device, mesh.shape["lon"], mesh.shape["lat"])
    return jax.shard_map(body, mesh=mesh, in_specs=in_specs, out_specs=out_specs, check_vma=False)
```

```python
import functools
import math

import jax
import jax.numpy as jnp
from jax import lax
from jax.experimental import pallas as pl
from jax.experimental.pallas import tpu as pltpu
from jax.sharding import PartitionSpec as P

MESH = pl.DeviceIdType.MESH
BLK = 128
PARTS = ((0, 2), (2, 4))
RING = 8
F32 = jnp.float32
BF16 = jnp.bfloat16


def split(a):
    high = a.astype(BF16)
    return high, (a - high.astype(F32)).astype(BF16)


def left(pair, dim=1):
    high, low = pair
    return jnp.concatenate([high, high, low], axis=dim)


def right(pair, dim=0):
    high, low = pair
    return jnp.concatenate([high, low, high], axis=dim)


def joined(a, b, dims=((1,), (0,))):
    return lax.dot_general(a, b, (dims, ((), ())), preferred_element_type=F32)


def dot3(a, b, dims=((1,), (0,))):
    return joined(left(a, dims[0][0]), right(b, dims[1][0]), dims)


def pole_terms(scale):
    x = 1.0 / scale
    t = jnp.ones_like(x)
    for k in range(10, 1, -1):
        t = 1.0 - x * (1.0 / k) * t
    pole = 1.0 - x * t
    gain = 1.0 - pole
    s = gain / (2.0 - gain)
    s2 = s * s
    series = 1.0 / 3 + s2 * (1.0 / 5 + s2 * (1.0 / 7 + s2 * (1.0 / 9 + s2 * (1.0 / 11))))
    log_pole = -2.0 * s * (1.0 + s2 * series)
    norm = jnp.sqrt((2.0 * math.sqrt(math.pi)) * jnp.sqrt(8.0 * pole) / gain)
    return gain, pole, log_pole, norm


def circle_terms(scale, laps):
    gain, pole, log_pole, norm = pole_terms(scale)
    q = pole * pole
    r = 1.0 / (1.0 + pole)
    r2 = r * r
    r4 = r2 * r2
    p3 = r4
    p2 = (3.0 + q) * r4 * r
    p1 = (3.0 + 6.0 * q + q * q) * r4 * r2
    p0 = (1.0 + 9.0 * q + 9.0 * q * q + q * q * q) * r4 * r2 * r
    u = gain * BLK
    c0 = gain * p0
    c1 = gain * u * (p1 - 0.5 * p2 * gain + p3 * gain * gain * (1.0 / 3))
    c2 = gain * u * u * (0.5 * p2 - 0.5 * p3 * gain)
    c3 = gain * u * u * u * p3 * (1.0 / 6)
    lam = BLK * log_pole
    beta = jnp.exp(laps * lam)
    b0 = 1.0 / (1.0 - beta)
    b1 = beta * b0 * b0
    b2 = b1 * b0 * (1.0 + beta)
    b3 = b1 * b0 * b0 * (1.0 + beta * (4.0 + beta))
    n = float(laps)
    e3 = c3 * b0
    e2 = c2 * b0 + 3.0 * n * c3 * b1
    e1 = c1 * b0 + 2.0 * n * c2 * b1 + 3.0 * n * n * c3 * b2
    e0 = c0 * b0 + n * c1 * b1 + n * n * c2 * b2 + n * n * n * c3 * b3
    return [lam, e0 * norm, e1 * norm, e2 * norm, e3 * norm]


def line_terms(scale, run):
    gain, pole, log_pole, norm = pole_terms(scale)
    g2 = gain * gain
    g4 = g2 * g2
    cubic = [g4, g4 * (11.0 / 6 * run), g4 * float(run**2), g4 * (1.0 / 6 * run**3)]
    return run * log_pole, cubic, norm


def kernel(
    n_lon, n_lat,
    lon_hbm, lat_hbm, inc_hbm, spread_hbm, vert_hbm, out_hbm,
    lon_scale, lat_scale, inc_ref, spread_ref, vert_ref, out_ref,
    coef, column, inside, tables, local_mom, mom_send, mom_recv, zon,
    pair_raw, merged, rx, tx, coming, pair_out, back,
    down_mat, up_mat, runs, turns, own_mat,
    in_sem, out_sem, ms_sem, mr_sem, ps_sem, pr_sem, s1_sem, r1_sem, s2_sem, r2_sem, rz_sem, so_sem, ro_sem,
):
    nv, rows, lev, width = inc_ref.shape
    blocks = width // BLK
    laps = blocks * n_lon
    poles = nv * rows
    group = min(4, rows)
    me_lon = lax.axis_index("lon")
    me = lax.axis_index("lat")
    groups = n_lat // RING
    halves = RING // 2
    block = groups * rows
    g_me, z_me = me // RING, lax.rem(me, RING)
    duo, odd = z_me // 2, lax.rem(z_me, 2)
    side = 2 * odd - 1
    mate = z_me - side
    my_v, my_lev = odd, duo * groups + g_me

    loads = [
        pltpu.make_async_copy(lon_hbm, lon_scale, in_sem.at[0]),
        pltpu.make_async_copy(spread_hbm, spread_ref, in_sem.at[1]),
        pltpu.make_async_copy(lat_hbm, lat_scale, in_sem.at[2]),
        pltpu.make_async_copy(vert_hbm, vert_ref, in_sem.at[3]),
    ]
    fields = [pltpu.make_async_copy(inc_hbm.at[v], inc_ref.at[v], in_sem.at[4 + v]) for v in range(nv)]
    for load in loads[:2] + fields + loads[2:]:
        load.start()

    barrier = pltpu.get_barrier_semaphore()

    for s in range(1, n_lon):
        pl.semaphore_signal(
            barrier, inc=1, device_id={"lon": lax.rem(me_lon + s, n_lon)}, device_id_type=MESH
        )

    greeted = (0, -1, 1, 2, 3, -2)
    for off in greeted:
        z = lax.rem(z_me + side * off + RING, RING)

        @pl.loop(0 if off else 1, groups)
        def _(k):
            d = lax.rem(g_me + k, groups) * RING + z
            pl.semaphore_signal(barrier, inc=1, device_id={"lat": d}, device_id_type=MESH)

    loads[0].wait()
    loads[1].wait()
    row_of = lax.broadcasted_iota(jnp.int32, (poles, BLK), 0)
    scale = jnp.zeros((poles, BLK), F32)
    for v in range(nv):
        for t in range(rows):
            scale = jnp.where(row_of == v * rows + t, lon_scale[v, t], scale)
    for k, part in enumerate(circle_terms(scale, laps)):
        coef[k] = part
    eye = lax.broadcasted_iota(jnp.int32, (lev, lev), 0) == lax.broadcasted_iota(jnp.int32, (lev, lev), 1)
    for v in range(nv):
        for t in range(rows):
            line = jnp.broadcast_to(spread_ref[v, t : t + 1, :], (lev, lev))
            one = jnp.sum(jnp.where(eye, line, 0.0), axis=1, keepdims=True)
            column[v, t] = jnp.broadcast_to(one, (lev, BLK))

    def tile(shape, dim):
        return lax.broadcasted_iota(jnp.int32, shape, dim)

    lane8 = tile((8, BLK), 1).astype(F32) * (1.0 / BLK)
    order = tile((8, BLK), 0)
    ahead = order < 4
    rank = lax.rem(order, 4)
    to_end = 1.0 - lane8
    to_start = lane8 + 1.0 / BLK
    behind = lane8
    before = (BLK - 1.0) / BLK - lane8

    def power(tau):
        t2 = tau * tau
        return jnp.where(rank == 0, 1.0, jnp.where(rank == 1, tau, jnp.where(rank == 2, t2, t2 * tau)))

    def coefs(r):
        return [coef[k, pl.ds(r, 1), :] for k in range(5)]

    def wide_column(v, t):
        one = column[v, t]
        return jnp.concatenate([one] * blocks, axis=1)

    def first(v, g):
        pieces = []
        for u in range(group):
            t = g * group + u
            lam = coefs(v * rows + t)[0]
            x = inc_ref[v, t] * wide_column(v, t)
            inc_ref[v, t] = x
            tau = jnp.where(ahead, to_end, to_start)
            small = jnp.exp(lam * tau) * power(tau)
            nothing = jnp.zeros((8, BLK), F32)
            lines = []
            for c in range(blocks):
                lines.append(jnp.concatenate([small if d == c else nothing for d in range(blocks)], axis=1))
            whole = []
            for c in range(blocks):
                shifted = jnp.where(ahead, to_end + float(blocks - 1 - c), to_start + float(c))
                whole.append(jnp.exp(lam * shifted) * power(shifted))
            lines.append(jnp.concatenate(whole, axis=1))
            basis = jnp.concatenate(lines, axis=0)
            moments = dot3(split(basis), split(x), ((1,), (1,)))
            local_mom[v, t] = moments[: 8 * blocks]
            pieces.append(moments[8 * blocks :])
        mom_send[v, g] = jnp.concatenate(pieces, axis=1)

    def table_of(v, t, lam, e0, e1, e2, e3):
        def mixed(a0, a1, a2, a3):
            return jnp.where(rank == 0, a0, jnp.where(rank == 1, a1, jnp.where(rank == 2, a2, a3)))

        q0 = mixed(e0, e1, e2, e3)
        q1 = mixed(e1, 2.0 * e2, 3.0 * e3, 0.0)
        q2 = mixed(e2, 3.0 * e3, 0.0, 0.0)
        q3 = mixed(e3, 0.0, 0.0, 0.0)

        def reach(y):
            return jnp.exp(lam * y) * (q0 + y * (q1 + y * (q2 + y * q3)))

        by_gap = {}
        for gap in list(range(1, blocks)) + list(range(laps - blocks + 1, laps)):
            by_gap[gap] = reach(jnp.where(ahead, behind + float(gap - 1), before + float(laps - gap - 1)))
        nothing = jnp.zeros((8, BLK), F32)
        lines = []
        for c in range(blocks):
            lines.append(
                jnp.concatenate(
                    [nothing if d == c else by_gap[(d - c) % laps] for d in range(blocks)], axis=1
                )
            )
        for s in range(1, n_lon):
            line = []
            for d in range(blocks):
                line.append(
                    reach(
                        jnp.where(
                            ahead,
                            behind + float(d + blocks * (s - 1)),
                            before + float(blocks - 1 - d + blocks * (n_lon - 1 - s)),
                        )
                    )
                )
            lines.append(jnp.concatenate(line, axis=1))
        high, low = split(jnp.concatenate(lines, axis=0))
        tables[v, t, 0] = high
        tables[v, t, 1] = low

    def middle(v, g):
        for u in range(group):
            t = g * group + u
            lam, e0, e1, e2, e3 = coefs(v * rows + t)
            x = inc_ref[v, t]
            stacked = jnp.concatenate([x[:, c * BLK : (c + 1) * BLK] for c in range(blocks)], axis=0)
            gap = jnp.abs(tile((BLK, BLK), 0) - tile((BLK, BLK), 1)).astype(F32) * (1.0 / BLK)
            far = float(laps) - gap
            near = jnp.exp(lam * gap) * (e0 + gap * (e1 + gap * (e2 + gap * e3)))
            around = jnp.exp(lam * far) * (e0 + far * (e1 + far * (e2 + far * e3)))
            inside[v, t] = dot3(split(stacked), split(near + around))
            table_of(v, t, lam, e0, e1, e2, e3)

    def moment_copy(v, s):
        return pltpu.make_async_remote_copy(
            src_ref=mom_send.at[v],
            dst_ref=mom_recv.at[v, s - 1],
            send_sem=ms_sem.at[v, s - 1],
            recv_sem=mr_sem.at[v, s - 1],
            device_id={"lon": lax.rem(me_lon + s, n_lon)},
            device_id_type=MESH,
        )

    for v in range(nv):
        fields[v].wait()

        @pl.loop(0, rows // group)
        def _(g):
            first(v, g)

        if v == 0:
            pl.semaphore_wait(barrier, len(greeted) * groups - 1 + n_lon - 1)
        for s in range(1, n_lon):
            moment_copy(v, s).start()

    def second(v, g):
        for u in range(group):
            t = g * group + u
            sources = [local_mom[v, t]]
            for s in range(1, n_lon):
                sources.append(mom_recv[v, s - 1, g][:, u * lev : (u + 1) * lev])
            moments = jnp.concatenate(sources, axis=0)
            added = dot3(split(moments.T), (tables[v, t, 0], tables[v, t, 1]))
            own = inside[v, t]
            own = jnp.concatenate([own[c * lev : (c + 1) * lev] for c in range(blocks)], axis=1)
            total = own + added
            for c in range(blocks):
                zon[v, c, pl.ds(t, lev, stride=rows), :] = total[:, c * BLK : (c + 1) * BLK]

    parts = len(PARTS)
    run = 2 * rows

    def part(h):
        return pl.ds(PARTS[h][0], PARTS[h][1] - PARTS[h][0])

    def columns(h):
        return range(*PARTS[h])

    def row_of_set(w):
        return (w // 2) * block

    def lead(j):
        return lax.rem(z_me + side * j + RING, RING)

    def mate_lead(j):
        return lax.rem(z_me - side * (j + 1) + RING, RING)

    def spot(shape, dim, swap):
        at = tile(shape, dim)
        return lax.rem(at, rows) + rows * jnp.abs(at // block - swap)

    def pair_of(shape, dim):
        return lax.rem(tile(shape, dim), block) // rows

    def graded(tau, kind):
        t2 = tau * tau
        return jnp.where(kind == 0, 1.0, jnp.where(kind == 1, tau, jnp.where(kind == 2, t2, t2 * tau)))

    def set_matrices(lam, cubic, norm, swap):
        unit = 1.0 / run
        shape = (block, 2 * block)
        kind = lax.rem(tile(shape, 0), rows)
        pos = spot(shape, 1, swap).astype(F32)
        tau = jnp.where(kind < 4, run - pos, pos + 1.0) * unit
        same = pair_of(shape, 0) == pair_of(shape, 1)
        basis = jnp.where(same, jnp.exp(lam * tau) * graded(tau, lax.rem(kind, 4)), 0.0)
        shape = (2 * block, 2 * block)
        away = spot(shape, 0, swap) - spot(shape, 1, swap)
        gap = jnp.abs(away).astype(F32) * unit
        same = pair_of(shape, 0) == pair_of(shape, 1)
        value = cubic[0] + gap * (cubic[1] + gap * (cubic[2] + gap * cubic[3]))
        value = jnp.where(same, jnp.exp(lam * gap) * value, 0.0)
        ahead_of = split(jnp.where(away >= 0, value, 0.0))
        behind_of = split(jnp.where(away <= 0, value, 0.0) * norm)
        down = jnp.where(kind < 4, basis, dot3(split(basis), ahead_of))
        near = dot3(behind_of, ahead_of)
        shape = (2 * block, block)
        kind = lax.rem(tile(shape, 1), rows)
        pos = spot(shape, 0, swap).astype(F32)
        tau = jnp.where(kind < 4, pos, run - 1.0 - pos) * unit
        same = pair_of(shape, 0) == pair_of(shape, 1)
        basis = jnp.where(same, jnp.exp(lam[:, :block] * tau) * graded(tau, lax.rem(kind, 4)), 0.0)
        up = jnp.where(kind < 4, dot3(behind_of, split(basis)), basis * norm[:, :block])
        return down, near, up

    loads[2].wait()

    @pl.loop(1, 4)
    def _(j):
        w = lead(j)
        which = pair_of((8, 2 * block), 1)
        scales = jnp.ones((8, 2 * block), F32)
        for q in range(groups):
            scales = jnp.where(which == q, lat_scale[lax.rem(w, 2), (w // 2) * groups + q], scales)
        lam, cubic, norm = line_terms(scales, run)
        down, near, up = set_matrices(lam[:1], [p[:1] for p in cubic], norm[:1], odd)
        down_mat[j - 1] = left(split(down))
        up_mat[j - 1] = left(split(jnp.concatenate([near, up], axis=1)))

    for v in range(nv):

        @pl.loop(0, rows // group)
        def _(g):
            middle(v, g)

    def pair_copy(j, h):
        w = mate_lead(j)
        return pltpu.make_async_remote_copy(
            src_ref=zon.at[lax.rem(w, 2), part(h), pl.ds(row_of_set(w), block), :],
            dst_ref=pair_raw.at[j - 1, part(h)],
            send_sem=ps_sem.at[h, j - 1],
            recv_sem=pr_sem.at[h, j - 1],
            device_id={"lat": g_me * RING + mate},
            device_id_type=MESH,
        )

    def raw_copy(w, q, h):
        return pltpu.make_async_remote_copy(
            src_ref=zon.at[lax.rem(w, 2), part(h), pl.ds(row_of_set(w) + q * rows, rows), :],
            dst_ref=rx.at[part(h), pl.ds((odd * groups + g_me) * rows, rows), :],
            send_sem=s1_sem.at[h],
            recv_sem=r1_sem.at[h],
            device_id={"lat": q * RING + w},
            device_id_type=MESH,
        )

    def merged_copy(j, q, h):
        w = lead(j)
        away = lax.rem(duo - w // 2 + halves, halves)
        return pltpu.make_async_remote_copy(
            src_ref=merged.at[j - 1, part(h), pl.ds(q * rows, rows), :],
            dst_ref=rx.at[part(h), pl.ds((2 * groups + 3 * g_me + away - 1) * rows, rows), :],
            send_sem=s1_sem.at[h],
            recv_sem=r1_sem.at[h],
            device_id={"lat": q * RING + w},
            device_id_type=MESH,
        )

    def send_pairs(h, sets):
        for j in sets:
            pair_copy(j, h).start()

    def send_raw(h):
        @pl.loop(0, groups)
        def _(k):
            raw_copy(mate, lax.rem(g_me + k, groups), h).start()

        @pl.loop(1, groups)
        def _(k):
            raw_copy(z_me, lax.rem(g_me + k, groups), h).start()

    def both_tiles(j, h):
        w = lead(j)
        at = pl.ds(row_of_set(w), block)
        mine = jnp.concatenate([zon[lax.rem(w, 2), c, at, :] for c in columns(h)], axis=1)
        other = jnp.concatenate([pair_raw[j - 1, c] for c in columns(h)], axis=1)
        return [mine, other]

    def merge(h):
        for j in (3, 1, 2):
            pair_copy(j, h).wait_recv()
            tiles = jnp.concatenate(both_tiles(j, h), axis=0)
            moments = joined(down_mat[j - 1], right(split(tiles)))
            for k, c in enumerate(columns(h)):
                merged[j - 1, c] = moments[:, k * BLK : (k + 1) * BLK]

            @pl.loop(0, groups)
            def _(k):
                merged_copy(j, lax.rem(g_me + k, groups), h).start()

    def build():
        shape = (8, 2 * block)
        own_scale = jnp.full(shape, lat_scale[my_v, my_lev], F32)
        lam, cubic, norm = line_terms(own_scale, run)
        down, near, up = set_matrices(lam[:1], [p[:1] for p in cubic], norm[:1], 0)
        lam = lam[:, :1]
        cubic = [p[:, :1] for p in cubic]
        count = halves * groups
        states = 8 * count
        lane_slot = tile((8, states), 1) // 8
        lane_kind = lax.rem(tile((8, states), 1), 8)
        row_kind = tile((8, states), 0)

        def run_of(slot):
            other = slot - groups
            q = jnp.where(slot < groups, slot, other // 3)
            away = jnp.where(slot < groups, 0, lax.rem(other, 3) + 1)
            return q * halves + lax.rem(duo + away, halves)

        lane_run = jnp.zeros((8, states), F32)
        for n in range(count):
            q, away = (n, 0) if n < groups else ((n - groups) // 3, (n - groups) % 3 + 1)
            place = q * halves + lax.rem(duo + away, halves)
            lane_run = jnp.where(lane_slot == n, place.astype(F32), lane_run)
        a, b = lax.rem(row_kind, 4), lax.rem(lane_kind, 4)
        m = a + b
        mf = m.astype(F32)
        choose = jnp.where(m == 2, jnp.where(a == 1, 2.0, 1.0), jnp.where(m == 3, jnp.where((a == 1) | (a == 2), 3.0, 1.0), 1.0))

        def pick(shift):
            total = jnp.zeros((8, states), F32)
            for n in range(4 - shift):
                total = jnp.where(m == n, cubic[n + shift], total)
            return total * choose

        taylor = [pick(0), pick(1) * (mf + 1.0), pick(2) * ((mf + 1.0) * (mf + 2.0) * 0.5), pick(3)]
        turn = jnp.zeros((8, states), F32)
        for n in range(run):
            power_of = graded((n + 1.0) / run, a) * graded(n / run, b)
            turn = turn + jnp.exp(lam * ((2.0 * n + 1.0) / run)) * power_of
        turn = jnp.where((row_kind >= 4) & (lane_kind < 4), turn, 0.0)

        @pl.loop(0, count)
        def _(slot):
            here = run_of(slot).astype(F32)
            step = jnp.where(row_kind < 4, here - lane_run, lane_run - here) - 1.0
            live = ((row_kind < 4) == (lane_kind < 4)) & (step >= 0.0)
            reach = jnp.maximum(step, 0.0)
            value = taylor[0] + reach * (taylor[1] + reach * (taylor[2] + reach * taylor[3]))
            at = pl.ds(pl.multiple_of(slot * 8, 8), 8)
            runs[at, :] = jnp.where(live, jnp.exp(lam * reach) * value, 0.0)
            turns[at, :] = jnp.where(lane_slot == slot, turn, 0.0)

        down, up = split(down), split(up)
        steps = split(runs[...])
        turned = dot3(split(turns[...]), steps)
        whole = runs[...] + dot3(steps, split(turned))
        inner = dot3(split(whole[:, :block]), down)
        top = dot3(up, split(jnp.concatenate([inner[:block], whole[:block, block:]], axis=1)))
        top = jnp.concatenate([top[:, : 2 * block] + near, top[:, 2 * block :]], axis=1)
        bottom = jnp.concatenate([inner[block:], whole[block:, block:]], axis=1)
        own_mat[: 2 * block, :] = left(split(top))
        own_mat[2 * block :, :] = left(split(bottom))

    def drain(ref, h, count, sem):
        view = ref.at[part(h), pl.ds(0, count * rows), :]
        pltpu.make_async_copy(view, view, sem).wait()

    slot = pl.ds((my_v * lev + my_lev) * rows, rows)
    own = pl.ds((odd * groups + g_me) * rows, rows)

    def reply_raw(e, q, h):
        return pltpu.make_async_remote_copy(
            src_ref=tx.at[part(h), pl.ds((e * groups + q) * rows, rows), :],
            dst_ref=back.at[part(h), slot, :],
            send_sem=s2_sem.at[h],
            recv_sem=r2_sem.at[h],
            device_id={"lat": q * RING + 2 * duo + e},
            device_id_type=MESH,
        )

    def reply_state(away, q, h):
        z = 2 * lax.rem(duo + away, halves) + {1: 0, 2: 1 - odd, 3: 1}[away]
        j = {1: 2 - odd, 2: 3, 3: 1 + odd}[away]
        return pltpu.make_async_remote_copy(
            src_ref=tx.at[part(h), pl.ds((2 * groups + 3 * q + away - 1) * rows, rows), :],
            dst_ref=coming.at[j - 1, part(h), pl.ds(g_me * rows, rows), :],
            send_sem=s2_sem.at[h],
            recv_sem=rz_sem.at[h, j - 1],
            device_id={"lat": q * RING + z},
            device_id_type=MESH,
        )

    def owner(h):
        rx[part(h), own, :] = zon[my_v, part(h), pl.ds(my_lev * rows, rows), :]
        drain(rx, h, 5 * groups - 1, r1_sem.at[h])
        everything = jnp.concatenate([rx[c] for c in columns(h)], axis=1)
        result = joined(own_mat[...], right(split(everything)))
        for k, c in enumerate(columns(h)):
            tx[c] = result[:, k * BLK : (k + 1) * BLK]
        for away in (2, 1, 3):

            @pl.loop(0, groups)
            def _(k):
                reply_state(away, lax.rem(g_me + k, groups), h).start()

    def reply_rows(h):
        @pl.loop(0, groups)
        def _(k):
            reply_raw(1 - odd, lax.rem(g_me + k, groups), h).start()

        @pl.loop(1, groups)
        def _(k):
            reply_raw(odd, lax.rem(g_me + k, groups), h).start()

        back[part(h), slot, :] = tx[part(h), own, :]

    def pair_back(j, h):
        w = lead(j)
        return pltpu.make_async_remote_copy(
            src_ref=pair_out.at[j - 1, part(h)],
            dst_ref=back.at[part(h), pl.ds(lax.rem(w, 2) * lev * rows + row_of_set(w), block), :],
            send_sem=so_sem.at[h, j - 1],
            recv_sem=ro_sem.at[h, j - 1],
            device_id={"lat": g_me * RING + mate},
            device_id_type=MESH,
        )

    def finish(h):
        for j in (1, 3, 2):
            view = coming.at[j - 1, part(h)]
            pltpu.make_async_copy(view, view, rz_sem.at[h, j - 1]).wait()
            coefficients = jnp.concatenate([coming[j - 1, c] for c in columns(h)], axis=1)
            inputs = jnp.concatenate(both_tiles(j, h) + [coefficients], axis=0)
            finished = joined(up_mat[j - 1], right(split(inputs)))
            for k, c in enumerate(columns(h)):
                pair_out[j - 1, c] = finished[block:, k * BLK : (k + 1) * BLK]
            pair_back(j, h).start()
            w = lead(j)
            at = pl.ds(lax.rem(w, 2) * lev * rows + row_of_set(w), block)
            for k, c in enumerate(columns(h)):
                back[c, at, :] = finished[:block, k * BLK : (k + 1) * BLK]

    def store(v, h):
        at = pl.ds(PARTS[h][0] * BLK, (PARTS[h][1] - PARTS[h][0]) * BLK)
        return pltpu.make_async_copy(out_ref.at[v, :, :, at], out_hbm.at[v, :, :, at], out_sem.at[h, v])

    def mix(h):
        first_lane, last_lane = PARTS[h][0] * BLK, PARTS[h][1] * BLK
        drain(back, h, 2 * groups - 1, r2_sem.at[h])
        for v, expected in ((odd, (1, 3)), (1 - odd, (2,))):
            for j in expected:
                pair_back(j, h).wait_recv()
            weights = left(split(vert_ref[v]))
            for t in range(rows):
                levels = jnp.concatenate(
                    [back[c, pl.ds(v * (lev * rows) + t, lev, stride=rows), :] for c in columns(h)], axis=1
                )
                scaling = jnp.concatenate([column[v, t]] * len(columns(h)), axis=1)
                out_ref[v, t, :, first_lane:last_lane] = joined(weights, right(split(levels))) * scaling
            store(v, h).start()

    loads[3].wait()
    for v, sets in ((odd, (3, 1)), (1 - odd, (2,))):
        for s in range(1, n_lon):
            moment_copy(v, s).wait()

        @pl.loop(0, rows // group)
        def _(g):
            second(v, g)

        send_pairs(0, sets)
    send_raw(0)
    merge(0)
    send_pairs(1, (3, 1, 2))
    send_raw(1)
    build()
    merge(1)
    for h in range(parts):
        owner(h)
        reply_rows(h)
    for h in range(parts):
        finish(h)
    for h in range(parts):
        mix(h)

    for h in range(parts):
        drain(tx, h, 5 * groups - 1, s1_sem.at[h])
        drain(tx, h, 5 * groups - 1, s2_sem.at[h])
        for j in (1, 2, 3):
            pair_copy(j, h).wait_send()
            pair_back(j, h).wait_send()
        for v in range(nv):
            store(v, h).wait()


def per_device(n_lon, n_lat, increment, spread, lon_scale, lat_scale, vertical):
    nv, rows, lev, width = increment.shape
    blocks = width // BLK
    poles = nv * rows
    block = n_lat // RING * rows
    group = min(4, rows)
    hbm = pl.BlockSpec(memory_space=pltpu.MemorySpace.HBM)
    return pl.pallas_call(
        functools.partial(kernel, n_lon, n_lat),
        out_shape=jax.ShapeDtypeStruct(increment.shape, F32),
        in_specs=[hbm] * 5,
        out_specs=hbm,
        scratch_shapes=[
            pltpu.SMEM((nv, rows), F32),
            pltpu.SMEM((nv, lev), F32),
            pltpu.VMEM(increment.shape, F32),
            pltpu.VMEM((nv, rows, lev), F32),
            pltpu.VMEM((nv, lev, lev), F32),
            pltpu.VMEM(increment.shape, F32),
            pltpu.VMEM((5, poles, BLK), F32),
            pltpu.VMEM((nv, rows, lev, BLK), F32),
            pltpu.VMEM((nv, rows, blocks * lev, BLK), F32),
            pltpu.VMEM((nv, rows, 2, 8 * (blocks + n_lon - 1), width), BF16),
            pltpu.VMEM((nv, rows, 8 * blocks, lev), F32),
            pltpu.VMEM((nv, rows // group, 8, group * lev), F32),
            pltpu.VMEM((nv, n_lon - 1, rows // group, 8, group * lev), F32),
            pltpu.VMEM((nv, blocks, lev * rows, BLK), F32),
            pltpu.VMEM((3, blocks, block, BLK), F32),
            pltpu.VMEM((3, blocks, block, BLK), F32),
            pltpu.VMEM((blocks, 5 * block, BLK), F32),
            pltpu.VMEM((blocks, 5 * block, BLK), F32),
            pltpu.VMEM((3, blocks, block, BLK), F32),
            pltpu.VMEM((3, blocks, block, BLK), F32),
            pltpu.VMEM((blocks, nv * lev * rows, BLK), F32),
            pltpu.VMEM((3, block, 6 * block), BF16),
            pltpu.VMEM((3, 2 * block, 9 * block), BF16),
            pltpu.VMEM((4 * block, 4 * block), F32),
            pltpu.VMEM((4 * block, 4 * block), F32),
            pltpu.VMEM((5 * block, 15 * block), BF16),
            pltpu.SemaphoreType.DMA((4 + nv,)),
            pltpu.SemaphoreType.DMA((len(PARTS), nv)),
            pltpu.SemaphoreType.DMA((nv, n_lon - 1)),
            pltpu.SemaphoreType.DMA((nv, n_lon - 1)),
            pltpu.SemaphoreType.DMA((len(PARTS), 3)),
            pltpu.SemaphoreType.DMA((len(PARTS), 3)),
            pltpu.SemaphoreType.DMA((len(PARTS),)),
            pltpu.SemaphoreType.DMA((len(PARTS),)),
            pltpu.SemaphoreType.DMA((len(PARTS),)),
            pltpu.SemaphoreType.DMA((len(PARTS),)),
            pltpu.SemaphoreType.DMA((len(PARTS), 3)),
            pltpu.SemaphoreType.DMA((len(PARTS), 3)),
            pltpu.SemaphoreType.DMA((len(PARTS), 3)),
        ],
        compiler_params=pltpu.CompilerParams(
            collective_id=0, has_side_effects=True, vmem_limit_bytes=60 * 1024 * 1024
        ),
    )(lon_scale, lat_scale, increment, spread, vertical)


def solution(mesh):
    in_specs = (P(None, "lat", None, "lon"), P(None, "lat", None), P(None, "lat"), P(), P())
    out_specs = P(None, "lat", None, "lon")
    body = functools.partial(per_device, mesh.shape["lon"], mesh.shape["lat"])
    return jax.shard_map(body, mesh=mesh, in_specs=in_specs, out_specs=out_specs, check_vma=False)
```

```python
import functools
import math

import jax
import jax.numpy as jnp
from jax import lax
from jax.experimental import pallas as pl
from jax.experimental.pallas import tpu as pltpu
from jax.sharding import PartitionSpec as P

MESH = pl.DeviceIdType.MESH
BLK = 128
PARTS = ((0, 2), (2, 4))
RING = 8
F32 = jnp.float32
BF16 = jnp.bfloat16


def split(a):
    high = a.astype(BF16)
    return high, (a - high.astype(F32)).astype(BF16)


def left(pair, dim=1):
    high, low = pair
    return jnp.concatenate([high, high, low], axis=dim)


def right(pair, dim=0):
    high, low = pair
    return jnp.concatenate([high, low, high], axis=dim)


def joined(a, b, dims=((1,), (0,))):
    return lax.dot_general(a, b, (dims, ((), ())), preferred_element_type=F32)


def dot3(a, b, dims=((1,), (0,))):
    return joined(left(a, dims[0][0]), right(b, dims[1][0]), dims)


def pole_terms(scale):
    x = 1.0 / scale
    t = jnp.ones_like(x)
    for k in range(10, 1, -1):
        t = 1.0 - x * (1.0 / k) * t
    pole = 1.0 - x * t
    gain = 1.0 - pole
    s = gain / (2.0 - gain)
    s2 = s * s
    series = 1.0 / 3 + s2 * (1.0 / 5 + s2 * (1.0 / 7 + s2 * (1.0 / 9 + s2 * (1.0 / 11))))
    log_pole = -2.0 * s * (1.0 + s2 * series)
    norm = jnp.sqrt((2.0 * math.sqrt(math.pi)) * jnp.sqrt(8.0 * pole) / gain)
    return gain, pole, log_pole, norm


def circle_terms(scale, laps):
    gain, pole, log_pole, norm = pole_terms(scale)
    q = pole * pole
    r = 1.0 / (1.0 + pole)
    r2 = r * r
    r4 = r2 * r2
    p3 = r4
    p2 = (3.0 + q) * r4 * r
    p1 = (3.0 + 6.0 * q + q * q) * r4 * r2
    p0 = (1.0 + 9.0 * q + 9.0 * q * q + q * q * q) * r4 * r2 * r
    u = gain * BLK
    c0 = gain * p0
    c1 = gain * u * (p1 - 0.5 * p2 * gain + p3 * gain * gain * (1.0 / 3))
    c2 = gain * u * u * (0.5 * p2 - 0.5 * p3 * gain)
    c3 = gain * u * u * u * p3 * (1.0 / 6)
    lam = BLK * log_pole
    beta = jnp.exp(laps * lam)
    b0 = 1.0 / (1.0 - beta)
    b1 = beta * b0 * b0
    b2 = b1 * b0 * (1.0 + beta)
    b3 = b1 * b0 * b0 * (1.0 + beta * (4.0 + beta))
    n = float(laps)
    e3 = c3 * b0
    e2 = c2 * b0 + 3.0 * n * c3 * b1
    e1 = c1 * b0 + 2.0 * n * c2 * b1 + 3.0 * n * n * c3 * b2
    e0 = c0 * b0 + n * c1 * b1 + n * n * c2 * b2 + n * n * n * c3 * b3
    return [lam, e0 * norm, e1 * norm, e2 * norm, e3 * norm]


def line_terms(scale, run):
    gain, pole, log_pole, norm = pole_terms(scale)
    g2 = gain * gain
    g4 = g2 * g2
    cubic = [g4, g4 * (11.0 / 6 * run), g4 * float(run**2), g4 * (1.0 / 6 * run**3)]
    return run * log_pole, cubic, norm


def kernel(
    n_lon, n_lat,
    lon_hbm, lat_hbm, inc_hbm, spread_hbm, vert_hbm, out_hbm,
    lon_scale, lat_scale, inc_ref, spread_ref, vert_ref, out_ref,
    coef, column, inside, tables, local_mom, mom_send, mom_recv, zon,
    pair_raw, merged, rx, tx, coming, pair_out, back,
    down_mat, up_mat, runs, turns, own_mat,
    in_sem, out_sem, ms_sem, mr_sem, ps_sem, pr_sem, s1_sem, r1_sem, s2_sem, r2_sem, rz_sem, so_sem, ro_sem,
):
    nv, rows, lev, width = inc_ref.shape
    blocks = width // BLK
    laps = blocks * n_lon
    poles = nv * rows
    group = min(4, rows)
    me_lon = lax.axis_index("lon")
    me = lax.axis_index("lat")
    groups = n_lat // RING
    halves = RING // 2
    block = groups * rows
    g_me, z_me = me // RING, lax.rem(me, RING)
    duo, odd = z_me // 2, lax.rem(z_me, 2)
    side = 2 * odd - 1
    mate = z_me - side
    my_v, my_lev = odd, duo * groups + g_me

    loads = [
        pltpu.make_async_copy(lon_hbm, lon_scale, in_sem.at[0]),
        pltpu.make_async_copy(spread_hbm, spread_ref, in_sem.at[1]),
        pltpu.make_async_copy(lat_hbm, lat_scale, in_sem.at[2]),
        pltpu.make_async_copy(vert_hbm, vert_ref, in_sem.at[3]),
    ]
    fields = [pltpu.make_async_copy(inc_hbm.at[v], inc_ref.at[v], in_sem.at[4 + v]) for v in range(nv)]
    for load in loads[:2] + fields + loads[2:]:
        load.start()

    barrier = pltpu.get_barrier_semaphore()

    for s in range(1, n_lon):
        pl.semaphore_signal(
            barrier, inc=1, device_id={"lon": lax.rem(me_lon + s, n_lon)}, device_id_type=MESH
        )

    greeted = (0, -1, 1, 2, 3, -2)
    for off in greeted:
        z = lax.rem(z_me + side * off + RING, RING)

        @pl.loop(0 if off else 1, groups)
        def _(k):
            d = lax.rem(g_me + k, groups) * RING + z
            pl.semaphore_signal(barrier, inc=1, device_id={"lat": d}, device_id_type=MESH)

    loads[0].wait()
    loads[1].wait()
    row_of = lax.broadcasted_iota(jnp.int32, (poles, BLK), 0)
    scale = jnp.zeros((poles, BLK), F32)
    for v in range(nv):
        for t in range(rows):
            scale = jnp.where(row_of == v * rows + t, lon_scale[v, t], scale)
    for k, part in enumerate(circle_terms(scale, laps)):
        coef[k] = part
    eye = lax.broadcasted_iota(jnp.int32, (lev, lev), 0) == lax.broadcasted_iota(jnp.int32, (lev, lev), 1)
    for v in range(nv):
        for t in range(rows):
            line = jnp.broadcast_to(spread_ref[v, t : t + 1, :], (lev, lev))
            one = jnp.sum(jnp.where(eye, line, 0.0), axis=1, keepdims=True)
            column[v, t] = jnp.broadcast_to(one, (lev, BLK))

    def tile(shape, dim):
        return lax.broadcasted_iota(jnp.int32, shape, dim)

    lane8 = tile((8, BLK), 1).astype(F32) * (1.0 / BLK)
    order = tile((8, BLK), 0)
    ahead = order < 4
    rank = lax.rem(order, 4)
    to_end = 1.0 - lane8
    to_start = lane8 + 1.0 / BLK
    behind = lane8
    before = (BLK - 1.0) / BLK - lane8

    def power(tau):
        t2 = tau * tau
        return jnp.where(rank == 0, 1.0, jnp.where(rank == 1, tau, jnp.where(rank == 2, t2, t2 * tau)))

    def coefs(r):
        return [coef[k, pl.ds(r, 1), :] for k in range(5)]

    def wide_column(v, t):
        one = column[v, t]
        return jnp.concatenate([one] * blocks, axis=1)

    def first(v, g):
        pieces = []
        for u in range(group):
            t = g * group + u
            lam = coefs(v * rows + t)[0]
            x = inc_ref[v, t] * wide_column(v, t)
            inc_ref[v, t] = x
            tau = jnp.where(ahead, to_end, to_start)
            small = jnp.exp(lam * tau) * power(tau)
            nothing = jnp.zeros((8, BLK), F32)
            lines = []
            for c in range(blocks):
                lines.append(jnp.concatenate([small if d == c else nothing for d in range(blocks)], axis=1))
            whole = []
            for c in range(blocks):
                shifted = jnp.where(ahead, to_end + float(blocks - 1 - c), to_start + float(c))
                whole.append(jnp.exp(lam * shifted) * power(shifted))
            lines.append(jnp.concatenate(whole, axis=1))
            basis = jnp.concatenate(lines, axis=0)
            moments = dot3(split(basis), split(x), ((1,), (1,)))
            local_mom[v, t] = moments[: 8 * blocks]
            pieces.append(moments[8 * blocks :])
        mom_send[v, g] = jnp.concatenate(pieces, axis=1)

    def table_of(v, t, lam, e0, e1, e2, e3):
        def mixed(a0, a1, a2, a3):
            return jnp.where(rank == 0, a0, jnp.where(rank == 1, a1, jnp.where(rank == 2, a2, a3)))

        q0 = mixed(e0, e1, e2, e3)
        q1 = mixed(e1, 2.0 * e2, 3.0 * e3, 0.0)
        q2 = mixed(e2, 3.0 * e3, 0.0, 0.0)
        q3 = mixed(e3, 0.0, 0.0, 0.0)

        def reach(y):
            return jnp.exp(lam * y) * (q0 + y * (q1 + y * (q2 + y * q3)))

        by_gap = {}
        for gap in list(range(1, blocks)) + list(range(laps - blocks + 1, laps)):
            by_gap[gap] = reach(jnp.where(ahead, behind + float(gap - 1), before + float(laps - gap - 1)))
        nothing = jnp.zeros((8, BLK), F32)
        lines = []
        for c in range(blocks):
            lines.append(
                jnp.concatenate(
                    [nothing if d == c else by_gap[(d - c) % laps] for d in range(blocks)], axis=1
                )
            )
        for s in range(1, n_lon):
            line = []
            for d in range(blocks):
                line.append(
                    reach(
                        jnp.where(
                            ahead,
                            behind + float(d + blocks * (s - 1)),
                            before + float(blocks - 1 - d + blocks * (n_lon - 1 - s)),
                        )
                    )
                )
            lines.append(jnp.concatenate(line, axis=1))
        high, low = split(jnp.concatenate(lines, axis=0))
        tables[v, t, 0] = high
        tables[v, t, 1] = low

    def middle(v, g):
        for u in range(group):
            t = g * group + u
            lam, e0, e1, e2, e3 = coefs(v * rows + t)
            x = inc_ref[v, t]
            stacked = jnp.concatenate([x[:, c * BLK : (c + 1) * BLK] for c in range(blocks)], axis=0)
            gap = jnp.abs(tile((BLK, BLK), 0) - tile((BLK, BLK), 1)).astype(F32) * (1.0 / BLK)
            far = float(laps) - gap
            near = jnp.exp(lam * gap) * (e0 + gap * (e1 + gap * (e2 + gap * e3)))
            around = jnp.exp(lam * far) * (e0 + far * (e1 + far * (e2 + far * e3)))
            inside[v, t] = dot3(split(stacked), split(near + around))
            table_of(v, t, lam, e0, e1, e2, e3)

    def moment_copy(v, s):
        return pltpu.make_async_remote_copy(
            src_ref=mom_send.at[v],
            dst_ref=mom_recv.at[v, s - 1],
            send_sem=ms_sem.at[v, s - 1],
            recv_sem=mr_sem.at[v, s - 1],
            device_id={"lon": lax.rem(me_lon + s, n_lon)},
            device_id_type=MESH,
        )

    for v in range(nv):
        fields[v].wait()

        @pl.loop(0, rows // group)
        def _(g):
            first(v, g)

        if v == 0:
            pl.semaphore_wait(barrier, len(greeted) * groups - 1 + n_lon - 1)
        for s in range(1, n_lon):
            moment_copy(v, s).start()

    def second(v, g):
        for u in range(group):
            t = g * group + u
            sources = [local_mom[v, t]]
            for s in range(1, n_lon):
                sources.append(mom_recv[v, s - 1, g][:, u * lev : (u + 1) * lev])
            moments = jnp.concatenate(sources, axis=0)
            added = dot3(split(moments.T), (tables[v, t, 0], tables[v, t, 1]))
            own = inside[v, t]
            own = jnp.concatenate([own[c * lev : (c + 1) * lev] for c in range(blocks)], axis=1)
            total = own + added
            for c in range(blocks):
                zon[v, c, pl.ds(t, lev, stride=rows), :] = total[:, c * BLK : (c + 1) * BLK]

    parts = len(PARTS)
    run = 2 * rows

    def part(h):
        return pl.ds(PARTS[h][0], PARTS[h][1] - PARTS[h][0])

    def columns(h):
        return range(*PARTS[h])

    def row_of_set(w):
        return (w // 2) * block

    def lead(j):
        return lax.rem(z_me + side * j + RING, RING)

    def mate_lead(j):
        return lax.rem(z_me - side * (j + 1) + RING, RING)

    def spot(shape, dim, swap):
        at = tile(shape, dim)
        return lax.rem(at, rows) + rows * jnp.abs(at // block - swap)

    def pair_of(shape, dim):
        return lax.rem(tile(shape, dim), block) // rows

    def graded(tau, kind):
        t2 = tau * tau
        return jnp.where(kind == 0, 1.0, jnp.where(kind == 1, tau, jnp.where(kind == 2, t2, t2 * tau)))

    def set_matrices(lam, cubic, norm, swap):
        unit = 1.0 / run
        shape = (block, 2 * block)
        kind = lax.rem(tile(shape, 0), rows)
        pos = spot(shape, 1, swap).astype(F32)
        tau = jnp.where(kind < 4, run - pos, pos + 1.0) * unit
        same = pair_of(shape, 0) == pair_of(shape, 1)
        basis = jnp.where(same, jnp.exp(lam * tau) * graded(tau, lax.rem(kind, 4)), 0.0)
        shape = (2 * block, 2 * block)
        away = spot(shape, 0, swap) - spot(shape, 1, swap)
        gap = jnp.abs(away).astype(F32) * unit
        same = pair_of(shape, 0) == pair_of(shape, 1)
        value = cubic[0] + gap * (cubic[1] + gap * (cubic[2] + gap * cubic[3]))
        value = jnp.where(same, jnp.exp(lam * gap) * value, 0.0)
        ahead_of = split(jnp.where(away >= 0, value, 0.0))
        behind_of = split(jnp.where(away <= 0, value, 0.0) * norm)
        down = jnp.where(kind < 4, basis, dot3(split(basis), ahead_of))
        near = dot3(behind_of, ahead_of)
        shape = (2 * block, block)
        kind = lax.rem(tile(shape, 1), rows)
        pos = spot(shape, 0, swap).astype(F32)
        tau = jnp.where(kind < 4, pos, run - 1.0 - pos) * unit
        same = pair_of(shape, 0) == pair_of(shape, 1)
        basis = jnp.where(same, jnp.exp(lam[:, :block] * tau) * graded(tau, lax.rem(kind, 4)), 0.0)
        up = jnp.where(kind < 4, dot3(behind_of, split(basis)), basis * norm[:, :block])
        return down, near, up

    loads[2].wait()

    @pl.loop(1, 4)
    def _(j):
        w = lead(j)
        which = pair_of((8, 2 * block), 1)
        scales = jnp.ones((8, 2 * block), F32)
        for q in range(groups):
            scales = jnp.where(which == q, lat_scale[lax.rem(w, 2), (w // 2) * groups + q], scales)
        lam, cubic, norm = line_terms(scales, run)
        down, near, up = set_matrices(lam[:1], [p[:1] for p in cubic], norm[:1], odd)
        down_mat[j - 1] = left(split(down))
        up_mat[j - 1] = left(split(jnp.concatenate([near, up], axis=1)))

    for v in range(nv):

        @pl.loop(0, rows // group)
        def _(g):
            middle(v, g)

    def pair_copy(j, h):
        w = mate_lead(j)
        return pltpu.make_async_remote_copy(
            src_ref=zon.at[lax.rem(w, 2), part(h), pl.ds(row_of_set(w), block), :],
            dst_ref=pair_raw.at[j - 1, part(h)],
            send_sem=ps_sem.at[h, j - 1],
            recv_sem=pr_sem.at[h, j - 1],
            device_id={"lat": g_me * RING + mate},
            device_id_type=MESH,
        )

    def raw_copy(w, q, h):
        return pltpu.make_async_remote_copy(
            src_ref=zon.at[lax.rem(w, 2), part(h), pl.ds(row_of_set(w) + q * rows, rows), :],
            dst_ref=rx.at[part(h), pl.ds((odd * groups + g_me) * rows, rows), :],
            send_sem=s1_sem.at[h],
            recv_sem=r1_sem.at[h],
            device_id={"lat": q * RING + w},
            device_id_type=MESH,
        )

    def merged_copy(j, q, h):
        w = lead(j)
        away = lax.rem(duo - w // 2 + halves, halves)
        return pltpu.make_async_remote_copy(
            src_ref=merged.at[j - 1, part(h), pl.ds(q * rows, rows), :],
            dst_ref=rx.at[part(h), pl.ds((2 * groups + 3 * g_me + away - 1) * rows, rows), :],
            send_sem=s1_sem.at[h],
            recv_sem=r1_sem.at[h],
            device_id={"lat": q * RING + w},
            device_id_type=MESH,
        )

    def send_pairs(h, sets):
        for j in sets:
            pair_copy(j, h).start()

    def send_raw(h):
        @pl.loop(0, groups)
        def _(k):
            raw_copy(mate, lax.rem(g_me + k, groups), h).start()

    def send_own(h):
        @pl.loop(1, groups)
        def _(k):
            raw_copy(z_me, lax.rem(g_me + k, groups), h).start()

    def both_tiles(j, h):
        w = lead(j)
        at = pl.ds(row_of_set(w), block)
        mine = jnp.concatenate([zon[lax.rem(w, 2), c, at, :] for c in columns(h)], axis=1)
        other = jnp.concatenate([pair_raw[j - 1, c] for c in columns(h)], axis=1)
        return [mine, other]

    def merge(h):
        for j in (3, 1, 2):
            pair_copy(j, h).wait_recv()
            tiles = jnp.concatenate(both_tiles(j, h), axis=0)
            moments = joined(down_mat[j - 1], right(split(tiles)))
            for k, c in enumerate(columns(h)):
                merged[j - 1, c] = moments[:, k * BLK : (k + 1) * BLK]

            @pl.loop(0, groups)
            def _(k):
                merged_copy(j, lax.rem(g_me + k, groups), h).start()

    def build():
        shape = (8, 2 * block)
        own_scale = jnp.full(shape, lat_scale[my_v, my_lev], F32)
        lam, cubic, norm = line_terms(own_scale, run)
        down, near, up = set_matrices(lam[:1], [p[:1] for p in cubic], norm[:1], 0)
        lam = lam[:, :1]
        cubic = [p[:, :1] for p in cubic]
        count = halves * groups
        states = 8 * count
        lane_slot = tile((8, states), 1) // 8
        lane_kind = lax.rem(tile((8, states), 1), 8)
        row_kind = tile((8, states), 0)

        def run_of(slot):
            other = slot - groups
            q = jnp.where(slot < groups, slot, other // 3)
            away = jnp.where(slot < groups, 0, lax.rem(other, 3) + 1)
            return q * halves + lax.rem(duo + away, halves)

        lane_run = jnp.zeros((8, states), F32)
        for n in range(count):
            q, away = (n, 0) if n < groups else ((n - groups) // 3, (n - groups) % 3 + 1)
            place = q * halves + lax.rem(duo + away, halves)
            lane_run = jnp.where(lane_slot == n, place.astype(F32), lane_run)
        a, b = lax.rem(row_kind, 4), lax.rem(lane_kind, 4)
        m = a + b
        mf = m.astype(F32)
        choose = jnp.where(m == 2, jnp.where(a == 1, 2.0, 1.0), jnp.where(m == 3, jnp.where((a == 1) | (a == 2), 3.0, 1.0), 1.0))

        def pick(shift):
            total = jnp.zeros((8, states), F32)
            for n in range(4 - shift):
                total = jnp.where(m == n, cubic[n + shift], total)
            return total * choose

        taylor = [pick(0), pick(1) * (mf + 1.0), pick(2) * ((mf + 1.0) * (mf + 2.0) * 0.5), pick(3)]
        turn = jnp.zeros((8, states), F32)
        for n in range(run):
            power_of = graded((n + 1.0) / run, a) * graded(n / run, b)
            turn = turn + jnp.exp(lam * ((2.0 * n + 1.0) / run)) * power_of
        turn = jnp.where((row_kind >= 4) & (lane_kind < 4), turn, 0.0)

        @pl.loop(0, count)
        def _(slot):
            here = run_of(slot).astype(F32)
            step = jnp.where(row_kind < 4, here - lane_run, lane_run - here) - 1.0
            live = ((row_kind < 4) == (lane_kind < 4)) & (step >= 0.0)
            reach = jnp.maximum(step, 0.0)
            value = taylor[0] + reach * (taylor[1] + reach * (taylor[2] + reach * taylor[3]))
            at = pl.ds(pl.multiple_of(slot * 8, 8), 8)
            runs[at, :] = jnp.where(live, jnp.exp(lam * reach) * value, 0.0)
            turns[at, :] = jnp.where(lane_slot == slot, turn, 0.0)

        down, up = split(down), split(up)
        steps = split(runs[...])
        turned = dot3(split(turns[...]), steps)
        whole = runs[...] + dot3(steps, split(turned))
        inner = dot3(split(whole[:, :block]), down)
        top = dot3(up, split(jnp.concatenate([inner[:block], whole[:block, block:]], axis=1)))
        top = jnp.concatenate([top[:, : 2 * block] + near, top[:, 2 * block :]], axis=1)
        bottom = jnp.concatenate([inner[block:], whole[block:, block:]], axis=1)
        own_mat[: 2 * block, :] = left(split(top))
        own_mat[2 * block :, :] = left(split(bottom))

    def drain(ref, h, count, sem):
        view = ref.at[part(h), pl.ds(0, count * rows), :]
        pltpu.make_async_copy(view, view, sem).wait()

    slot = pl.ds((my_v * lev + my_lev) * rows, rows)
    own = pl.ds((odd * groups + g_me) * rows, rows)

    def reply_raw(e, q, h):
        return pltpu.make_async_remote_copy(
            src_ref=tx.at[part(h), pl.ds((e * groups + q) * rows, rows), :],
            dst_ref=back.at[part(h), slot, :],
            send_sem=s2_sem.at[h],
            recv_sem=r2_sem.at[h],
            device_id={"lat": q * RING + 2 * duo + e},
            device_id_type=MESH,
        )

    def reply_state(away, q, h):
        z = 2 * lax.rem(duo + away, halves) + {1: 0, 2: 1 - odd, 3: 1}[away]
        j = {1: 2 - odd, 2: 3, 3: 1 + odd}[away]
        return pltpu.make_async_remote_copy(
            src_ref=tx.at[part(h), pl.ds((2 * groups + 3 * q + away - 1) * rows, rows), :],
            dst_ref=coming.at[j - 1, part(h), pl.ds(g_me * rows, rows), :],
            send_sem=s2_sem.at[h],
            recv_sem=rz_sem.at[h, j - 1],
            device_id={"lat": q * RING + z},
            device_id_type=MESH,
        )

    def owner(h):
        rx[part(h), own, :] = zon[my_v, part(h), pl.ds(my_lev * rows, rows), :]
        drain(rx, h, 5 * groups - 1, r1_sem.at[h])
        everything = jnp.concatenate([rx[c] for c in columns(h)], axis=1)
        result = joined(own_mat[...], right(split(everything)))
        for k, c in enumerate(columns(h)):
            tx[c] = result[:, k * BLK : (k + 1) * BLK]
        for away in (2, 1, 3):

            @pl.loop(0, groups)
            def _(k):
                reply_state(away, lax.rem(g_me + k, groups), h).start()

    def reply_rows(h):
        @pl.loop(0, groups)
        def _(k):
            reply_raw(1 - odd, lax.rem(g_me + k, groups), h).start()

        @pl.loop(1, groups)
        def _(k):
            reply_raw(odd, lax.rem(g_me + k, groups), h).start()

        back[part(h), slot, :] = tx[part(h), own, :]

    def pair_back(j, h):
        w = lead(j)
        return pltpu.make_async_remote_copy(
            src_ref=pair_out.at[j - 1, part(h)],
            dst_ref=back.at[part(h), pl.ds(lax.rem(w, 2) * lev * rows + row_of_set(w), block), :],
            send_sem=so_sem.at[h, j - 1],
            recv_sem=ro_sem.at[h, j - 1],
            device_id={"lat": g_me * RING + mate},
            device_id_type=MESH,
        )

    def finish(h):
        for j in (1, 3, 2):
            view = coming.at[j - 1, part(h)]
            pltpu.make_async_copy(view, view, rz_sem.at[h, j - 1]).wait()
            coefficients = jnp.concatenate([coming[j - 1, c] for c in columns(h)], axis=1)
            inputs = jnp.concatenate(both_tiles(j, h) + [coefficients], axis=0)
            finished = joined(up_mat[j - 1], right(split(inputs)))
            for k, c in enumerate(columns(h)):
                pair_out[j - 1, c] = finished[block:, k * BLK : (k + 1) * BLK]
            pair_back(j, h).start()
            w = lead(j)
            at = pl.ds(lax.rem(w, 2) * lev * rows + row_of_set(w), block)
            for k, c in enumerate(columns(h)):
                back[c, at, :] = finished[:block, k * BLK : (k + 1) * BLK]

    def store(v, h):
        at = pl.ds(PARTS[h][0] * BLK, (PARTS[h][1] - PARTS[h][0]) * BLK)
        return pltpu.make_async_copy(out_ref.at[v, :, :, at], out_hbm.at[v, :, :, at], out_sem.at[h, v])

    def mix(h):
        first_lane, last_lane = PARTS[h][0] * BLK, PARTS[h][1] * BLK
        drain(back, h, 2 * groups - 1, r2_sem.at[h])
        for v, expected in ((odd, (1, 3)), (1 - odd, (2,))):
            for j in expected:
                pair_back(j, h).wait_recv()
            weights = left(split(vert_ref[v]))
            for t in range(rows):
                levels = jnp.concatenate(
                    [back[c, pl.ds(v * (lev * rows) + t, lev, stride=rows), :] for c in columns(h)], axis=1
                )
                scaling = jnp.concatenate([column[v, t]] * len(columns(h)), axis=1)
                out_ref[v, t, :, first_lane:last_lane] = joined(weights, right(split(levels))) * scaling
            store(v, h).start()

    loads[3].wait()
    for v, sets in ((odd, (3, 1)), (1 - odd, (2,))):
        for s in range(1, n_lon):
            moment_copy(v, s).wait()

        @pl.loop(0, rows // group)
        def _(g):
            second(v, g)

        send_pairs(0, sets)
        if len(sets) == 2:
            send_own(0)
    send_raw(0)
    merge(0)
    send_pairs(1, (3, 1, 2))
    send_raw(1)
    send_own(1)
    build()
    merge(1)
    for h in range(parts):
        owner(h)
        reply_rows(h)
    for h in range(parts):
        finish(h)
    for h in range(parts):
        mix(h)

    for h in range(parts):
        drain(tx, h, 5 * groups - 1, s1_sem.at[h])
        drain(tx, h, 5 * groups - 1, s2_sem.at[h])
        for j in (1, 2, 3):
            pair_copy(j, h).wait_send()
            pair_back(j, h).wait_send()
        for v in range(nv):
            store(v, h).wait()


def per_device(n_lon, n_lat, increment, spread, lon_scale, lat_scale, vertical):
    nv, rows, lev, width = increment.shape
    blocks = width // BLK
    poles = nv * rows
    block = n_lat // RING * rows
    group = min(4, rows)
    hbm = pl.BlockSpec(memory_space=pltpu.MemorySpace.HBM)
    return pl.pallas_call(
        functools.partial(kernel, n_lon, n_lat),
        out_shape=jax.ShapeDtypeStruct(increment.shape, F32),
        in_specs=[hbm] * 5,
        out_specs=hbm,
        scratch_shapes=[
            pltpu.SMEM((nv, rows), F32),
            pltpu.SMEM((nv, lev), F32),
            pltpu.VMEM(increment.shape, F32),
            pltpu.VMEM((nv, rows, lev), F32),
            pltpu.VMEM((nv, lev, lev), F32),
            pltpu.VMEM(increment.shape, F32),
            pltpu.VMEM((5, poles, BLK), F32),
            pltpu.VMEM((nv, rows, lev, BLK), F32),
            pltpu.VMEM((nv, rows, blocks * lev, BLK), F32),
            pltpu.VMEM((nv, rows, 2, 8 * (blocks + n_lon - 1), width), BF16),
            pltpu.VMEM((nv, rows, 8 * blocks, lev), F32),
            pltpu.VMEM((nv, rows // group, 8, group * lev), F32),
            pltpu.VMEM((nv, n_lon - 1, rows // group, 8, group * lev), F32),
            pltpu.VMEM((nv, blocks, lev * rows, BLK), F32),
            pltpu.VMEM((3, blocks, block, BLK), F32),
            pltpu.VMEM((3, blocks, block, BLK), F32),
            pltpu.VMEM((blocks, 5 * block, BLK), F32),
            pltpu.VMEM((blocks, 5 * block, BLK), F32),
            pltpu.VMEM((3, blocks, block, BLK), F32),
            pltpu.VMEM((3, blocks, block, BLK), F32),
            pltpu.VMEM((blocks, nv * lev * rows, BLK), F32),
            pltpu.VMEM((3, block, 6 * block), BF16),
            pltpu.VMEM((3, 2 * block, 9 * block), BF16),
            pltpu.VMEM((4 * block, 4 * block), F32),
            pltpu.VMEM((4 * block, 4 * block), F32),
            pltpu.VMEM((5 * block, 15 * block), BF16),
            pltpu.SemaphoreType.DMA((4 + nv,)),
            pltpu.SemaphoreType.DMA((len(PARTS), nv)),
            pltpu.SemaphoreType.DMA((nv, n_lon - 1)),
            pltpu.SemaphoreType.DMA((nv, n_lon - 1)),
            pltpu.SemaphoreType.DMA((len(PARTS), 3)),
            pltpu.SemaphoreType.DMA((len(PARTS), 3)),
            pltpu.SemaphoreType.DMA((len(PARTS),)),
            pltpu.SemaphoreType.DMA((len(PARTS),)),
            pltpu.SemaphoreType.DMA((len(PARTS),)),
            pltpu.SemaphoreType.DMA((len(PARTS),)),
            pltpu.SemaphoreType.DMA((len(PARTS), 3)),
            pltpu.SemaphoreType.DMA((len(PARTS), 3)),
            pltpu.SemaphoreType.DMA((len(PARTS), 3)),
        ],
        compiler_params=pltpu.CompilerParams(
            collective_id=0, has_side_effects=True, vmem_limit_bytes=60 * 1024 * 1024
        ),
    )(lon_scale, lat_scale, increment, spread, vertical)


def solution(mesh):
    in_specs = (P(None, "lat", None, "lon"), P(None, "lat", None), P(None, "lat"), P(), P())
    out_specs = P(None, "lat", None, "lon")
    body = functools.partial(per_device, mesh.shape["lon"], mesh.shape["lat"])
    return jax.shard_map(body, mesh=mesh, in_specs=in_specs, out_specs=out_specs, check_vma=False)
```

```python
import functools
import math

import jax
import jax.numpy as jnp
from jax import lax
from jax.experimental import pallas as pl
from jax.experimental.pallas import tpu as pltpu
from jax.sharding import PartitionSpec as P

MESH = pl.DeviceIdType.MESH
BLK = 128
PARTS = ((0, 2), (2, 4))
RING = 8
F32 = jnp.float32
BF16 = jnp.bfloat16


def split(a):
    high = a.astype(BF16)
    return high, (a - high.astype(F32)).astype(BF16)


def left(pair, dim=1):
    high, low = pair
    return jnp.concatenate([high, high, low], axis=dim)


def right(pair, dim=0):
    high, low = pair
    return jnp.concatenate([high, low, high], axis=dim)


def joined(a, b, dims=((1,), (0,))):
    return lax.dot_general(a, b, (dims, ((), ())), preferred_element_type=F32)


def dot3(a, b, dims=((1,), (0,))):
    return joined(left(a, dims[0][0]), right(b, dims[1][0]), dims)


def pole_terms(scale):
    x = 1.0 / scale
    t = jnp.ones_like(x)
    for k in range(10, 1, -1):
        t = 1.0 - x * (1.0 / k) * t
    pole = 1.0 - x * t
    gain = 1.0 - pole
    s = gain / (2.0 - gain)
    s2 = s * s
    series = 1.0 / 3 + s2 * (1.0 / 5 + s2 * (1.0 / 7 + s2 * (1.0 / 9 + s2 * (1.0 / 11))))
    log_pole = -2.0 * s * (1.0 + s2 * series)
    norm = jnp.sqrt((2.0 * math.sqrt(math.pi)) * jnp.sqrt(8.0 * pole) / gain)
    return gain, pole, log_pole, norm


def circle_terms(scale, laps):
    gain, pole, log_pole, norm = pole_terms(scale)
    q = pole * pole
    r = 1.0 / (1.0 + pole)
    r2 = r * r
    r4 = r2 * r2
    p3 = r4
    p2 = (3.0 + q) * r4 * r
    p1 = (3.0 + 6.0 * q + q * q) * r4 * r2
    p0 = (1.0 + 9.0 * q + 9.0 * q * q + q * q * q) * r4 * r2 * r
    u = gain * BLK
    c0 = gain * p0
    c1 = gain * u * (p1 - 0.5 * p2 * gain + p3 * gain * gain * (1.0 / 3))
    c2 = gain * u * u * (0.5 * p2 - 0.5 * p3 * gain)
    c3 = gain * u * u * u * p3 * (1.0 / 6)
    lam = BLK * log_pole
    beta = jnp.exp(laps * lam)
    b0 = 1.0 / (1.0 - beta)
    b1 = beta * b0 * b0
    b2 = b1 * b0 * (1.0 + beta)
    b3 = b1 * b0 * b0 * (1.0 + beta * (4.0 + beta))
    n = float(laps)
    e3 = c3 * b0
    e2 = c2 * b0 + 3.0 * n * c3 * b1
    e1 = c1 * b0 + 2.0 * n * c2 * b1 + 3.0 * n * n * c3 * b2
    e0 = c0 * b0 + n * c1 * b1 + n * n * c2 * b2 + n * n * n * c3 * b3
    return [lam, e0 * norm, e1 * norm, e2 * norm, e3 * norm]


def line_terms(scale, run):
    gain, pole, log_pole, norm = pole_terms(scale)
    g2 = gain * gain
    g4 = g2 * g2
    cubic = [g4, g4 * (11.0 / 6 * run), g4 * float(run**2), g4 * (1.0 / 6 * run**3)]
    return run * log_pole, cubic, norm


def kernel(
    n_lon, n_lat,
    lon_hbm, lat_hbm, inc_hbm, spread_hbm, vert_hbm, out_hbm,
    lon_scale, lat_scale, inc_ref, spread_ref, vert_ref, out_ref,
    coef, column, inside, tables, local_mom, mom_send, mom_recv, zon,
    pair_raw, merged, rx, tx, coming, pair_out, back,
    down_mat, up_mat, runs, turns, own_mat,
    in_sem, out_sem, ms_sem, mr_sem, ps_sem, pr_sem, s1_sem, r1_sem, s2_sem, r2_sem, rz_sem, so_sem, ro_sem,
):
    nv, rows, lev, width = inc_ref.shape
    blocks = width // BLK
    laps = blocks * n_lon
    poles = nv * rows
    group = min(4, rows)
    me_lon = lax.axis_index("lon")
    me = lax.axis_index("lat")
    groups = n_lat // RING
    halves = RING // 2
    block = groups * rows
    g_me, z_me = me // RING, lax.rem(me, RING)
    duo, odd = z_me // 2, lax.rem(z_me, 2)
    side = 2 * odd - 1
    mate = z_me - side
    my_v, my_lev = odd, duo * groups + g_me

    loads = [
        pltpu.make_async_copy(lon_hbm, lon_scale, in_sem.at[0]),
        pltpu.make_async_copy(spread_hbm, spread_ref, in_sem.at[1]),
        pltpu.make_async_copy(lat_hbm, lat_scale, in_sem.at[2]),
        pltpu.make_async_copy(vert_hbm, vert_ref, in_sem.at[3]),
    ]
    fields = [pltpu.make_async_copy(inc_hbm.at[v], inc_ref.at[v], in_sem.at[4 + v]) for v in range(nv)]
    for load in loads[:2] + fields + loads[2:]:
        load.start()

    barrier = pltpu.get_barrier_semaphore()

    for s in range(1, n_lon):
        pl.semaphore_signal(
            barrier, inc=1, device_id={"lon": lax.rem(me_lon + s, n_lon)}, device_id_type=MESH
        )

    greeted = (0, -1, 1, 2, 3, -2)
    for off in greeted:
        z = lax.rem(z_me + side * off + RING, RING)

        @pl.loop(0 if off else 1, groups)
        def _(k):
            d = lax.rem(g_me + k, groups) * RING + z
            pl.semaphore_signal(barrier, inc=1, device_id={"lat": d}, device_id_type=MESH)

    loads[0].wait()
    loads[1].wait()
    row_of = lax.broadcasted_iota(jnp.int32, (poles, BLK), 0)
    scale = jnp.zeros((poles, BLK), F32)
    for v in range(nv):
        for t in range(rows):
            scale = jnp.where(row_of == v * rows + t, lon_scale[v, t], scale)
    for k, part in enumerate(circle_terms(scale, laps)):
        coef[k] = part
    eye = lax.broadcasted_iota(jnp.int32, (lev, lev), 0) == lax.broadcasted_iota(jnp.int32, (lev, lev), 1)
    for v in range(nv):
        for t in range(rows):
            line = jnp.broadcast_to(spread_ref[v, t : t + 1, :], (lev, lev))
            one = jnp.sum(jnp.where(eye, line, 0.0), axis=1, keepdims=True)
            column[v, t] = jnp.broadcast_to(one, (lev, BLK))

    def tile(shape, dim):
        return lax.broadcasted_iota(jnp.int32, shape, dim)

    lane8 = tile((8, BLK), 1).astype(F32) * (1.0 / BLK)
    order = tile((8, BLK), 0)
    ahead = order < 4
    rank = lax.rem(order, 4)
    to_end = 1.0 - lane8
    to_start = lane8 + 1.0 / BLK
    behind = lane8
    before = (BLK - 1.0) / BLK - lane8

    def power(tau):
        t2 = tau * tau
        return jnp.where(rank == 0, 1.0, jnp.where(rank == 1, tau, jnp.where(rank == 2, t2, t2 * tau)))

    def coefs(r):
        return [coef[k, pl.ds(r, 1), :] for k in range(5)]

    def wide_column(v, t):
        one = column[v, t]
        return jnp.concatenate([one] * blocks, axis=1)

    def first(v, g):
        pieces = []
        for u in range(group):
            t = g * group + u
            lam = coefs(v * rows + t)[0]
            x = inc_ref[v, t] * wide_column(v, t)
            inc_ref[v, t] = x
            tau = jnp.where(ahead, to_end, to_start)
            small = jnp.exp(lam * tau) * power(tau)
            nothing = jnp.zeros((8, BLK), F32)
            lines = []
            for c in range(blocks):
                lines.append(jnp.concatenate([small if d == c else nothing for d in range(blocks)], axis=1))
            whole = []
            for c in range(blocks):
                shifted = jnp.where(ahead, to_end + float(blocks - 1 - c), to_start + float(c))
                whole.append(jnp.exp(lam * shifted) * power(shifted))
            lines.append(jnp.concatenate(whole, axis=1))
            basis = jnp.concatenate(lines, axis=0)
            moments = dot3(split(basis), split(x), ((1,), (1,)))
            local_mom[v, t] = moments[: 8 * blocks]
            pieces.append(moments[8 * blocks :])
        mom_send[v, g] = jnp.concatenate(pieces, axis=1)

    def table_of(v, t, lam, e0, e1, e2, e3):
        def mixed(a0, a1, a2, a3):
            return jnp.where(rank == 0, a0, jnp.where(rank == 1, a1, jnp.where(rank == 2, a2, a3)))

        q0 = mixed(e0, e1, e2, e3)
        q1 = mixed(e1, 2.0 * e2, 3.0 * e3, 0.0)
        q2 = mixed(e2, 3.0 * e3, 0.0, 0.0)
        q3 = mixed(e3, 0.0, 0.0, 0.0)

        def reach(y):
            return jnp.exp(lam * y) * (q0 + y * (q1 + y * (q2 + y * q3)))

        by_gap = {}
        for gap in list(range(1, blocks)) + list(range(laps - blocks + 1, laps)):
            by_gap[gap] = reach(jnp.where(ahead, behind + float(gap - 1), before + float(laps - gap - 1)))
        nothing = jnp.zeros((8, BLK), F32)
        lines = []
        for c in range(blocks):
            lines.append(
                jnp.concatenate(
                    [nothing if d == c else by_gap[(d - c) % laps] for d in range(blocks)], axis=1
                )
            )
        for s in range(1, n_lon):
            line = []
            for d in range(blocks):
                line.append(
                    reach(
                        jnp.where(
                            ahead,
                            behind + float(d + blocks * (s - 1)),
                            before + float(blocks - 1 - d + blocks * (n_lon - 1 - s)),
                        )
                    )
                )
            lines.append(jnp.concatenate(line, axis=1))
        high, low = split(jnp.concatenate(lines, axis=0))
        tables[v, t, 0] = high
        tables[v, t, 1] = low

    def middle(v, g):
        for u in range(group):
            t = g * group + u
            lam, e0, e1, e2, e3 = coefs(v * rows + t)
            x = inc_ref[v, t]
            stacked = jnp.concatenate([x[:, c * BLK : (c + 1) * BLK] for c in range(blocks)], axis=0)
            gap = jnp.abs(tile((BLK, BLK), 0) - tile((BLK, BLK), 1)).astype(F32) * (1.0 / BLK)
            far = float(laps) - gap
            near = jnp.exp(lam * gap) * (e0 + gap * (e1 + gap * (e2 + gap * e3)))
            around = jnp.exp(lam * far) * (e0 + far * (e1 + far * (e2 + far * e3)))
            inside[v, t] = dot3(split(stacked), split(near + around))
            table_of(v, t, lam, e0, e1, e2, e3)

    def moment_copy(v, s):
        return pltpu.make_async_remote_copy(
            src_ref=mom_send.at[v],
            dst_ref=mom_recv.at[v, s - 1],
            send_sem=ms_sem.at[v, s - 1],
            recv_sem=mr_sem.at[v, s - 1],
            device_id={"lon": lax.rem(me_lon + s, n_lon)},
            device_id_type=MESH,
        )

    for v in range(nv):
        fields[v].wait()

        @pl.loop(0, rows // group)
        def _(g):
            first(v, g)

        if v == 0:
            pl.semaphore_wait(barrier, len(greeted) * groups - 1 + n_lon - 1)
        for s in range(1, n_lon):
            moment_copy(v, s).start()

    def second(v, g):
        for u in range(group):
            t = g * group + u
            sources = [local_mom[v, t]]
            for s in range(1, n_lon):
                sources.append(mom_recv[v, s - 1, g][:, u * lev : (u + 1) * lev])
            moments = jnp.concatenate(sources, axis=0)
            added = dot3(split(moments.T), (tables[v, t, 0], tables[v, t, 1]))
            own = inside[v, t]
            own = jnp.concatenate([own[c * lev : (c + 1) * lev] for c in range(blocks)], axis=1)
            total = own + added
            for c in range(blocks):
                zon[v, c, pl.ds(t, lev, stride=rows), :] = total[:, c * BLK : (c + 1) * BLK]

    parts = len(PARTS)
    run = 2 * rows

    def part(h):
        return pl.ds(PARTS[h][0], PARTS[h][1] - PARTS[h][0])

    def columns(h):
        return range(*PARTS[h])

    def row_of_set(w):
        return (w // 2) * block

    def lead(j):
        return lax.rem(z_me + side * j + RING, RING)

    def mate_lead(j):
        return lax.rem(z_me - side * (j + 1) + RING, RING)

    def spot(shape, dim, swap):
        at = tile(shape, dim)
        return lax.rem(at, rows) + rows * jnp.abs(at // block - swap)

    def pair_of(shape, dim):
        return lax.rem(tile(shape, dim), block) // rows

    def graded(tau, kind):
        t2 = tau * tau
        return jnp.where(kind == 0, 1.0, jnp.where(kind == 1, tau, jnp.where(kind == 2, t2, t2 * tau)))

    def set_matrices(lam, cubic, norm, swap):
        unit = 1.0 / run
        shape = (block, 2 * block)
        kind = lax.rem(tile(shape, 0), rows)
        pos = spot(shape, 1, swap).astype(F32)
        tau = jnp.where(kind < 4, run - pos, pos + 1.0) * unit
        same = pair_of(shape, 0) == pair_of(shape, 1)
        basis = jnp.where(same, jnp.exp(lam * tau) * graded(tau, lax.rem(kind, 4)), 0.0)
        shape = (2 * block, 2 * block)
        away = spot(shape, 0, swap) - spot(shape, 1, swap)
        gap = jnp.abs(away).astype(F32) * unit
        same = pair_of(shape, 0) == pair_of(shape, 1)
        value = cubic[0] + gap * (cubic[1] + gap * (cubic[2] + gap * cubic[3]))
        value = jnp.where(same, jnp.exp(lam * gap) * value, 0.0)
        ahead_of = split(jnp.where(away >= 0, value, 0.0))
        behind_of = split(jnp.where(away <= 0, value, 0.0) * norm)
        down = jnp.where(kind < 4, basis, dot3(split(basis), ahead_of))
        near = dot3(behind_of, ahead_of)
        shape = (2 * block, block)
        kind = lax.rem(tile(shape, 1), rows)
        pos = spot(shape, 0, swap).astype(F32)
        tau = jnp.where(kind < 4, pos, run - 1.0 - pos) * unit
        same = pair_of(shape, 0) == pair_of(shape, 1)
        basis = jnp.where(same, jnp.exp(lam[:, :block] * tau) * graded(tau, lax.rem(kind, 4)), 0.0)
        up = jnp.where(kind < 4, dot3(behind_of, split(basis)), basis * norm[:, :block])
        return down, near, up

    for v in range(nv):

        @pl.loop(0, rows // group)
        def _(g):
            middle(v, g)

    def pair_copy(j, h):
        w = mate_lead(j)
        return pltpu.make_async_remote_copy(
            src_ref=zon.at[lax.rem(w, 2), part(h), pl.ds(row_of_set(w), block), :],
            dst_ref=pair_raw.at[j - 1, part(h)],
            send_sem=ps_sem.at[h, j - 1],
            recv_sem=pr_sem.at[h, j - 1],
            device_id={"lat": g_me * RING + mate},
            device_id_type=MESH,
        )

    def raw_copy(w, q, h):
        return pltpu.make_async_remote_copy(
            src_ref=zon.at[lax.rem(w, 2), part(h), pl.ds(row_of_set(w) + q * rows, rows), :],
            dst_ref=rx.at[part(h), pl.ds((odd * groups + g_me) * rows, rows), :],
            send_sem=s1_sem.at[h],
            recv_sem=r1_sem.at[h],
            device_id={"lat": q * RING + w},
            device_id_type=MESH,
        )

    def merged_copy(j, q, h):
        w = lead(j)
        away = lax.rem(duo - w // 2 + halves, halves)
        return pltpu.make_async_remote_copy(
            src_ref=merged.at[j - 1, part(h), pl.ds(q * rows, rows), :],
            dst_ref=rx.at[part(h), pl.ds((2 * groups + 3 * g_me + away - 1) * rows, rows), :],
            send_sem=s1_sem.at[h],
            recv_sem=r1_sem.at[h],
            device_id={"lat": q * RING + w},
            device_id_type=MESH,
        )

    def send_pairs(h, sets):
        for j in sets:
            pair_copy(j, h).start()

    def send_raw(h):
        @pl.loop(0, groups)
        def _(k):
            raw_copy(mate, lax.rem(g_me + k, groups), h).start()

    def send_own(h):
        @pl.loop(1, groups)
        def _(k):
            raw_copy(z_me, lax.rem(g_me + k, groups), h).start()

    def both_tiles(j, h):
        w = lead(j)
        at = pl.ds(row_of_set(w), block)
        mine = jnp.concatenate([zon[lax.rem(w, 2), c, at, :] for c in columns(h)], axis=1)
        other = jnp.concatenate([pair_raw[j - 1, c] for c in columns(h)], axis=1)
        return [mine, other]

    def merge(h):
        for j in (3, 1, 2):
            pair_copy(j, h).wait_recv()
            tiles = jnp.concatenate(both_tiles(j, h), axis=0)
            moments = joined(down_mat[j - 1], right(split(tiles)))
            for k, c in enumerate(columns(h)):
                merged[j - 1, c] = moments[:, k * BLK : (k + 1) * BLK]

            @pl.loop(0, groups)
            def _(k):
                merged_copy(j, lax.rem(g_me + k, groups), h).start()

    def build():
        shape = (8, 2 * block)
        own_scale = jnp.full(shape, lat_scale[my_v, my_lev], F32)
        lam, cubic, norm = line_terms(own_scale, run)
        down, near, up = set_matrices(lam[:1], [p[:1] for p in cubic], norm[:1], 0)
        lam = lam[:, :1]
        cubic = [p[:, :1] for p in cubic]
        count = halves * groups
        states = 8 * count
        lane_slot = tile((8, states), 1) // 8
        lane_kind = lax.rem(tile((8, states), 1), 8)
        row_kind = tile((8, states), 0)

        def run_of(slot):
            other = slot - groups
            q = jnp.where(slot < groups, slot, other // 3)
            away = jnp.where(slot < groups, 0, lax.rem(other, 3) + 1)
            return q * halves + lax.rem(duo + away, halves)

        lane_run = jnp.zeros((8, states), F32)
        for n in range(count):
            q, away = (n, 0) if n < groups else ((n - groups) // 3, (n - groups) % 3 + 1)
            place = q * halves + lax.rem(duo + away, halves)
            lane_run = jnp.where(lane_slot == n, place.astype(F32), lane_run)
        a, b = lax.rem(row_kind, 4), lax.rem(lane_kind, 4)
        m = a + b
        mf = m.astype(F32)
        choose = jnp.where(m == 2, jnp.where(a == 1, 2.0, 1.0), jnp.where(m == 3, jnp.where((a == 1) | (a == 2), 3.0, 1.0), 1.0))

        def pick(shift):
            total = jnp.zeros((8, states), F32)
            for n in range(4 - shift):
                total = jnp.where(m == n, cubic[n + shift], total)
            return total * choose

        taylor = [pick(0), pick(1) * (mf + 1.0), pick(2) * ((mf + 1.0) * (mf + 2.0) * 0.5), pick(3)]
        turn = jnp.zeros((8, states), F32)
        for n in range(run):
            power_of = graded((n + 1.0) / run, a) * graded(n / run, b)
            turn = turn + jnp.exp(lam * ((2.0 * n + 1.0) / run)) * power_of
        turn = jnp.where((row_kind >= 4) & (lane_kind < 4), turn, 0.0)

        @pl.loop(0, count)
        def _(slot):
            here = run_of(slot).astype(F32)
            step = jnp.where(row_kind < 4, here - lane_run, lane_run - here) - 1.0
            live = ((row_kind < 4) == (lane_kind < 4)) & (step >= 0.0)
            reach = jnp.maximum(step, 0.0)
            value = taylor[0] + reach * (taylor[1] + reach * (taylor[2] + reach * taylor[3]))
            at = pl.ds(pl.multiple_of(slot * 8, 8), 8)
            runs[at, :] = jnp.where(live, jnp.exp(lam * reach) * value, 0.0)
            turns[at, :] = jnp.where(lane_slot == slot, turn, 0.0)

        down, up = split(down), split(up)
        steps = split(runs[...])
        turned = dot3(split(turns[...]), steps)
        whole = runs[...] + dot3(steps, split(turned))
        inner = dot3(split(whole[:, :block]), down)
        top = dot3(up, split(jnp.concatenate([inner[:block], whole[:block, block:]], axis=1)))
        top = jnp.concatenate([top[:, : 2 * block] + near, top[:, 2 * block :]], axis=1)
        bottom = jnp.concatenate([inner[block:], whole[block:, block:]], axis=1)
        own_mat[: 2 * block, :] = left(split(top))
        own_mat[2 * block :, :] = left(split(bottom))

    def drain(ref, h, count, sem):
        view = ref.at[part(h), pl.ds(0, count * rows), :]
        pltpu.make_async_copy(view, view, sem).wait()

    slot = pl.ds((my_v * lev + my_lev) * rows, rows)
    own = pl.ds((odd * groups + g_me) * rows, rows)

    def reply_raw(e, q, h):
        return pltpu.make_async_remote_copy(
            src_ref=tx.at[part(h), pl.ds((e * groups + q) * rows, rows), :],
            dst_ref=back.at[part(h), slot, :],
            send_sem=s2_sem.at[h],
            recv_sem=r2_sem.at[h],
            device_id={"lat": q * RING + 2 * duo + e},
            device_id_type=MESH,
        )

    def reply_state(away, q, h):
        z = 2 * lax.rem(duo + away, halves) + {1: 0, 2: 1 - odd, 3: 1}[away]
        j = {1: 2 - odd, 2: 3, 3: 1 + odd}[away]
        return pltpu.make_async_remote_copy(
            src_ref=tx.at[part(h), pl.ds((2 * groups + 3 * q + away - 1) * rows, rows), :],
            dst_ref=coming.at[j - 1, part(h), pl.ds(g_me * rows, rows), :],
            send_sem=s2_sem.at[h],
            recv_sem=rz_sem.at[h, j - 1],
            device_id={"lat": q * RING + z},
            device_id_type=MESH,
        )

    def owner(h):
        rx[part(h), own, :] = zon[my_v, part(h), pl.ds(my_lev * rows, rows), :]
        drain(rx, h, 5 * groups - 1, r1_sem.at[h])
        everything = jnp.concatenate([rx[c] for c in columns(h)], axis=1)
        result = joined(own_mat[...], right(split(everything)))
        for k, c in enumerate(columns(h)):
            tx[c] = result[:, k * BLK : (k + 1) * BLK]
        for away in (2, 1, 3):

            @pl.loop(0, groups)
            def _(k):
                reply_state(away, lax.rem(g_me + k, groups), h).start()

    def reply_rows(h):
        @pl.loop(0, groups)
        def _(k):
            reply_raw(1 - odd, lax.rem(g_me + k, groups), h).start()

        @pl.loop(1, groups)
        def _(k):
            reply_raw(odd, lax.rem(g_me + k, groups), h).start()

        back[part(h), slot, :] = tx[part(h), own, :]

    def pair_back(j, h):
        w = lead(j)
        return pltpu.make_async_remote_copy(
            src_ref=pair_out.at[j - 1, part(h)],
            dst_ref=back.at[part(h), pl.ds(lax.rem(w, 2) * lev * rows + row_of_set(w), block), :],
            send_sem=so_sem.at[h, j - 1],
            recv_sem=ro_sem.at[h, j - 1],
            device_id={"lat": g_me * RING + mate},
            device_id_type=MESH,
        )

    def finish(h):
        for j in (1, 3, 2):
            view = coming.at[j - 1, part(h)]
            pltpu.make_async_copy(view, view, rz_sem.at[h, j - 1]).wait()
            coefficients = jnp.concatenate([coming[j - 1, c] for c in columns(h)], axis=1)
            inputs = jnp.concatenate(both_tiles(j, h) + [coefficients], axis=0)
            finished = joined(up_mat[j - 1], right(split(inputs)))
            for k, c in enumerate(columns(h)):
                pair_out[j - 1, c] = finished[block:, k * BLK : (k + 1) * BLK]
            pair_back(j, h).start()
            w = lead(j)
            at = pl.ds(lax.rem(w, 2) * lev * rows + row_of_set(w), block)
            for k, c in enumerate(columns(h)):
                back[c, at, :] = finished[:block, k * BLK : (k + 1) * BLK]

    def store(v, h):
        at = pl.ds(PARTS[h][0] * BLK, (PARTS[h][1] - PARTS[h][0]) * BLK)
        return pltpu.make_async_copy(out_ref.at[v, :, :, at], out_hbm.at[v, :, :, at], out_sem.at[h, v])

    def mix(h):
        first_lane, last_lane = PARTS[h][0] * BLK, PARTS[h][1] * BLK
        drain(back, h, 2 * groups - 1, r2_sem.at[h])
        for v, expected in ((odd, (1, 3)), (1 - odd, (2,))):
            for j in expected:
                pair_back(j, h).wait_recv()
            weights = left(split(vert_ref[v]))
            for t in range(rows):
                levels = jnp.concatenate(
                    [back[c, pl.ds(v * (lev * rows) + t, lev, stride=rows), :] for c in columns(h)], axis=1
                )
                scaling = jnp.concatenate([column[v, t]] * len(columns(h)), axis=1)
                out_ref[v, t, :, first_lane:last_lane] = joined(weights, right(split(levels))) * scaling
            store(v, h).start()

    loads[3].wait()
    for v, sets in ((odd, (3, 1)), (1 - odd, (2,))):
        for s in range(1, n_lon):
            moment_copy(v, s).wait()

        @pl.loop(0, rows // group)
        def _(g):
            second(v, g)

        send_pairs(0, sets)
        if len(sets) == 2:
            send_own(0)
    send_raw(0)
    loads[2].wait()

    @pl.loop(1, 4)
    def _(j):
        w = lead(j)
        which = pair_of((8, 2 * block), 1)
        scales = jnp.ones((8, 2 * block), F32)
        for q in range(groups):
            scales = jnp.where(which == q, lat_scale[lax.rem(w, 2), (w // 2) * groups + q], scales)
        lam, cubic, norm = line_terms(scales, run)
        down, near, up = set_matrices(lam[:1], [p[:1] for p in cubic], norm[:1], odd)
        down_mat[j - 1] = left(split(down))
        up_mat[j - 1] = left(split(jnp.concatenate([near, up], axis=1)))

    merge(0)
    send_pairs(1, (3, 1, 2))
    send_raw(1)
    send_own(1)
    build()
    merge(1)
    for h in range(parts):
        owner(h)
        reply_rows(h)
    for h in range(parts):
        finish(h)
    for h in range(parts):
        mix(h)

    for h in range(parts):
        drain(tx, h, 5 * groups - 1, s1_sem.at[h])
        drain(tx, h, 5 * groups - 1, s2_sem.at[h])
        for j in (1, 2, 3):
            pair_copy(j, h).wait_send()
            pair_back(j, h).wait_send()
        for v in range(nv):
            store(v, h).wait()


def per_device(n_lon, n_lat, increment, spread, lon_scale, lat_scale, vertical):
    nv, rows, lev, width = increment.shape
    blocks = width // BLK
    poles = nv * rows
    block = n_lat // RING * rows
    group = min(4, rows)
    hbm = pl.BlockSpec(memory_space=pltpu.MemorySpace.HBM)
    return pl.pallas_call(
        functools.partial(kernel, n_lon, n_lat),
        out_shape=jax.ShapeDtypeStruct(increment.shape, F32),
        in_specs=[hbm] * 5,
        out_specs=hbm,
        scratch_shapes=[
            pltpu.SMEM((nv, rows), F32),
            pltpu.SMEM((nv, lev), F32),
            pltpu.VMEM(increment.shape, F32),
            pltpu.VMEM((nv, rows, lev), F32),
            pltpu.VMEM((nv, lev, lev), F32),
            pltpu.VMEM(increment.shape, F32),
            pltpu.VMEM((5, poles, BLK), F32),
            pltpu.VMEM((nv, rows, lev, BLK), F32),
            pltpu.VMEM((nv, rows, blocks * lev, BLK), F32),
            pltpu.VMEM((nv, rows, 2, 8 * (blocks + n_lon - 1), width), BF16),
            pltpu.VMEM((nv, rows, 8 * blocks, lev), F32),
            pltpu.VMEM((nv, rows // group, 8, group * lev), F32),
            pltpu.VMEM((nv, n_lon - 1, rows // group, 8, group * lev), F32),
            pltpu.VMEM((nv, blocks, lev * rows, BLK), F32),
            pltpu.VMEM((3, blocks, block, BLK), F32),
            pltpu.VMEM((3, blocks, block, BLK), F32),
            pltpu.VMEM((blocks, 5 * block, BLK), F32),
            pltpu.VMEM((blocks, 5 * block, BLK), F32),
            pltpu.VMEM((3, blocks, block, BLK), F32),
            pltpu.VMEM((3, blocks, block, BLK), F32),
            pltpu.VMEM((blocks, nv * lev * rows, BLK), F32),
            pltpu.VMEM((3, block, 6 * block), BF16),
            pltpu.VMEM((3, 2 * block, 9 * block), BF16),
            pltpu.VMEM((4 * block, 4 * block), F32),
            pltpu.VMEM((4 * block, 4 * block), F32),
            pltpu.VMEM((5 * block, 15 * block), BF16),
            pltpu.SemaphoreType.DMA((4 + nv,)),
            pltpu.SemaphoreType.DMA((len(PARTS), nv)),
            pltpu.SemaphoreType.DMA((nv, n_lon - 1)),
            pltpu.SemaphoreType.DMA((nv, n_lon - 1)),
            pltpu.SemaphoreType.DMA((len(PARTS), 3)),
            pltpu.SemaphoreType.DMA((len(PARTS), 3)),
            pltpu.SemaphoreType.DMA((len(PARTS),)),
            pltpu.SemaphoreType.DMA((len(PARTS),)),
            pltpu.SemaphoreType.DMA((len(PARTS),)),
            pltpu.SemaphoreType.DMA((len(PARTS),)),
            pltpu.SemaphoreType.DMA((len(PARTS), 3)),
            pltpu.SemaphoreType.DMA((len(PARTS), 3)),
            pltpu.SemaphoreType.DMA((len(PARTS), 3)),
        ],
        compiler_params=pltpu.CompilerParams(
            collective_id=0, has_side_effects=True, vmem_limit_bytes=60 * 1024 * 1024
        ),
    )(lon_scale, lat_scale, increment, spread, vertical)


def solution(mesh):
    in_specs = (P(None, "lat", None, "lon"), P(None, "lat", None), P(None, "lat"), P(), P())
    out_specs = P(None, "lat", None, "lon")
    body = functools.partial(per_device, mesh.shape["lon"], mesh.shape["lat"])
    return jax.shard_map(body, mesh=mesh, in_specs=in_specs, out_specs=out_specs, check_vma=False)
```
